32 devices in a mesh: seq: 8 (over z, core), chan: 4 (over y, x).
Axes of the slice: x: 2, y: 2, z: 4, core: 2. Of those that a mesh axis runs over, the one named last changes fastest.
Arguments:
- query_proj: bfloat16 [1024, 8192], P('seq', 'chan'), may hold values from -6 to 6
- key_proj: bfloat16 [1024, 8192], P('seq', 'chan'), may hold values from -6 to 6
- value_proj: bfloat16 [1024, 8192], P('seq', 'chan'), may hold values from -6 to 6
- short_filter: float32 [3, 512, 3], P(None, 'chan'), may hold values from -2.4 to 2.4
- long_filter: bfloat16 [512, 1024], P('chan'), may hold values from -4 to 4
- out_weight: bfloat16 [8192, 8192], P(None, 'chan'), may hold values from -0.09375 to 0.09375
- grad_out: bfloat16 [1024, 8192], P('seq', 'chan'), may hold values from -6 to 6
Outputs:
- mixer_out: bfloat16 [1024, 8192], P('seq', 'chan')
- grad_query: bfloat16 [1024, 8192], P('seq', 'chan')
- grad_key: bfloat16 [1024, 8192], P('seq', 'chan')
- grad_value: bfloat16 [1024, 8192], P('seq', 'chan')
The draws below stay inside these ranges and needn't reach their ends.
All inputs are finite; a program needn't handle non-finite values.
Results may differ from the reference program's by a relative error of at most 0.0064.
Values may be sent and summed in bfloat16 or wider, within the bound.
A program may use at most 128 MiB of HBM per device.

```python
import math
import jax
import jax.numpy as jnp
from jax import lax

D = 8192
GROUP = 16
SHORT = 3
FILTER_GROUPS = 512
SEQUENCE_LENGTH = 1024


def draw_long_filter(key, part):
    key_rows = jax.random.split(key, 6)
    delay_offsets = jnp.arange(SEQUENCE_LENGTH, dtype=jnp.float32)[None, :]
    slow = jnp.exp(jax.random.uniform(key_rows[0], (FILTER_GROUPS, 1), minval=math.log(SEQUENCE_LENGTH), maxval=math.log(8.0 * SEQUENCE_LENGTH)))
    quick = jnp.exp(jax.random.uniform(key_rows[1], (FILTER_GROUPS, 1), minval=math.log(20.0), maxval=math.log(60.0)))
    picked = jax.random.uniform(key_rows[2], (FILTER_GROUPS, 1)) < 0.5
    noise = jnp.clip(jax.random.normal(key_rows[3], (FILTER_GROUPS, SEQUENCE_LENGTH)), -4.0, 4.0)
    scale = jnp.where(picked, quick, slow)
    decay_profile = jnp.exp(-delay_offsets / scale)
    spike_position = jax.random.randint(key_rows[4], (FILTER_GROUPS, 2), 1, SEQUENCE_LENGTH).astype(jnp.float32)
    spike_retained = jax.random.uniform(key_rows[5], (FILTER_GROUPS, 2), minval=0.5, maxval=0.8)
    decay_profile = decay_profile * jnp.where(delay_offsets >= spike_position[:, 0:1], spike_retained[:, 0:1], 1.0)
    decay_profile = decay_profile * jnp.where(delay_offsets >= spike_position[:, 1:2], spike_retained[:, 1:2], 1.0)
    energy = (1.0 - jnp.exp(-2.0 * SEQUENCE_LENGTH / scale)) / (1.0 - jnp.exp(-2.0 / scale))
    return (noise * decay_profile / jnp.sqrt(energy)).astype(jnp.bfloat16)


def raised(entries, stream_key, source, target, parts, factor):
    def block_of(position):
        return (jnp.arange(entries.shape[position]) // (entries.shape[position] // parts)).reshape((-1,) + (1,) * (entries.ndim - 1 - position))

    near = jax.random.permutation(stream_key, parts)[block_of(target)]
    other_side = (block_of(target) + parts // 2) % parts
    return jnp.where((block_of(source) == near) | (block_of(source) == other_side), factor * entries, entries)


def shard_levels(rng, shape, shards, least, high):
    def one(axis_at, shards_of):
        draws = jax.random.uniform(jax.random.fold_in(jax.random.fold_in(rng, 6), axis_at), (shards_of,), jnp.float32, least / len(shards), high / len(shards))
        return jnp.repeat(jnp.exp(draws), shape[axis_at] // shards_of).reshape((-1,) + (1,) * (len(shape) - axis_at - 1))

    level = one(*shards[0])
    for cut in shards[1:]:
        level = level * one(*cut)
    return level


def normal_values(key, shape, width, most, shards=(), kind=jnp.bfloat16):
    values = jax.random.normal(key, shape, jnp.float32) * width
    if len(shards) > 0:
        values = shard_levels(key, shape, shards, -0.22, 0.18) * values
    return jnp.clip(values, min=-most, max=most).astype(kind)


def bell_draw_with(rng, dims, spread, reach, pieces, heavy, held_as=jnp.bfloat16):
    drawn = spread * jax.random.normal(rng, dims, jnp.float32)
    if pieces:
        drawn = drawn * shard_levels(rng, dims, pieces, -0.22, 0.18)
    return jnp.clip(raised(drawn, jax.random.fold_in(rng, 3), *heavy), -reach, reach).astype(held_as)


def setup_inputs(seed: int = 0) -> dict:
    seeds = jax.random.split(jax.random.key(seed), 8)
    query_proj = normal_values(seeds[0], (SEQUENCE_LENGTH, D), 1.0, 6.0, ((0, 8), (1, 4)))
    key_proj = normal_values(seeds[1], (SEQUENCE_LENGTH, D), 1.0, 6.0, ((0, 8), (1, 4)))
    value_proj = normal_values(seeds[2], (SEQUENCE_LENGTH, D), 1.0, 6.0, ((0, 8), (1, 4)))
    short_filter = normal_values(seeds[3], (3, FILTER_GROUPS, SHORT), 0.4, 2.4, ((1, 4),), jnp.float32)
    long_filter = draw_long_filter(jax.random.fold_in(seeds[7], 71), 0)
    out_weight = bell_draw_with(seeds[5], (D, D), D ** -0.5, 0.09375, ((1, 4),), (1, 0, 4, 2.0))
    grad_out = normal_values(seeds[6], (SEQUENCE_LENGTH, D), 1.0, 6.0, ((0, 8), (1, 4)))
    return dict(query_proj=query_proj, key_proj=key_proj, value_proj=value_proj, short_filter=short_filter, long_filter=long_filter, out_weight=out_weight, grad_out=grad_out)


def widen_taps(taps):
    return jnp.repeat(taps, GROUP, axis=0)


def causal_taps(stream, taps):
    values = stream.astype(jnp.float32)
    per_chan = widen_taps(taps)
    total = jnp.zeros_like(values)
    for lag_index in range(SHORT):
        moved = jnp.concatenate([jnp.zeros((lag_index, D), values.dtype), values[:SEQUENCE_LENGTH - lag_index]], axis=0)
        total = total + moved * per_chan[:, lag_index]
    return total


def anticausal_taps(grads, taps):
    values = grads.astype(jnp.float32)
    per_chan = widen_taps(taps)
    total = jnp.zeros_like(values)
    for lag_index in range(SHORT):
        moved = jnp.concatenate([values[lag_index:], jnp.zeros((lag_index, D), values.dtype)], axis=0)
        total = total + moved * per_chan[:, lag_index]
    return total


def long_mix(values, filt):
    span = math.gcd(FILTER_GROUPS, 32)
    count = FILTER_GROUPS // span
    grouped = values.reshape(SEQUENCE_LENGTH, count, span, GROUP).transpose(1, 0, 2, 3)
    filt_blocks = filt.reshape(count, span, SEQUENCE_LENGTH)

    def mix_block(bundle):
        block_vals, block_filt = bundle
        spectrum = jnp.fft.rfft(block_vals, n=2 * SEQUENCE_LENGTH, axis=0)
        kernel = jnp.fft.rfft(block_filt.T, n=2 * SEQUENCE_LENGTH, axis=0)
        joined = jnp.fft.irfft(spectrum * kernel[:, :, None], n=2 * SEQUENCE_LENGTH, axis=0)
        return joined[:SEQUENCE_LENGTH]

    result = lax.map(mix_block, (grouped, filt_blocks))
    return result.transpose(1, 0, 2, 3).reshape(SEQUENCE_LENGTH, D)


def reference(query_proj, key_proj, value_proj, short_filter, long_filter, out_weight, grad_out):
    query_f = causal_taps(query_proj, short_filter[0])
    key_f = causal_taps(key_proj, short_filter[1])
    value_f = causal_taps(value_proj, short_filter[2])
    products = (key_f * value_f).astype(jnp.bfloat16)
    filt = long_filter.astype(jnp.float32)
    mixed = long_mix(products.astype(jnp.float32), filt).astype(jnp.bfloat16)
    mixed_f = mixed.astype(jnp.float32)
    gated = (query_f * mixed_f).astype(jnp.bfloat16)
    mixer_out = jnp.dot(gated, out_weight, preferred_element_type=jnp.float32).astype(jnp.bfloat16)
    grad_gated = jnp.dot(grad_out, out_weight.T, preferred_element_type=jnp.float32)
    grad_qf = (grad_gated * mixed_f).astype(jnp.bfloat16)
    grad_mixed = (grad_gated * query_f).astype(jnp.bfloat16)
    grad_prod = long_mix(grad_mixed.astype(jnp.float32)[::-1], filt)[::-1].astype(jnp.bfloat16)
    grad_pf = grad_prod.astype(jnp.float32)
    grad_kf = (grad_pf * value_f).astype(jnp.bfloat16)
    grad_vf = (grad_pf * key_f).astype(jnp.bfloat16)
    grad_query = anticausal_taps(grad_qf, short_filter[0]).astype(jnp.bfloat16)
    grad_key = anticausal_taps(grad_kf, short_filter[1]).astype(jnp.bfloat16)
    grad_value = anticausal_taps(grad_vf, short_filter[2]).astype(jnp.bfloat16)
    return (mixer_out, grad_query, grad_key, grad_value)
```

```python
import jax
import jax.numpy as jnp
from jax import lax
from jax.experimental import pallas as pl
from jax.experimental.pallas import tpu as pltpu
from jax.sharding import PartitionSpec as P

GROUP = 16
F32 = jnp.float32
BF16 = jnp.bfloat16
MESH = pl.DeviceIdType.MESH


def causal(x, before, taps):
    row = lax.broadcasted_iota(jnp.int32, x.shape, 0)
    one = jnp.where(row == 0, before[1:2], pltpu.roll(x, 1, 0))
    two = jnp.where(row == 0, before[0:1], jnp.where(row == 1, before[1:2], pltpu.roll(x, 2, 0)))
    return x * taps[0:1] + one * taps[1:2] + two * taps[2:3]


def anticausal(g, after, taps):
    count = g.shape[0]
    row = lax.broadcasted_iota(jnp.int32, g.shape, 0)
    one = jnp.where(row == count - 1, after[0:1], pltpu.roll(g, count - 1, 0))
    two = jnp.where(
        row == count - 1,
        after[1:2],
        jnp.where(row == count - 2, after[0:1], pltpu.roll(g, count - 2, 0)),
    )
    return g * taps[0:1] + one * taps[1:2] + two * taps[2:3]


def rounded(x):
    return x.astype(BF16).astype(F32)


def step_kernel(
    q_ref, k_ref, v_ref, taps_ref, h_ref, w_hbm, go_ref,
    out_ref, gqf_ref, gp_ref, before_ref, after_ref,
    w_ref, got_ref, hr_ref, filt_ref, send_refs, recv_refs, part_send, part_recv, gall_ref,
    acc_ref, hsend_ref, hrecv_ref, tail_ref, head_ref,
    w_sem, seq_send, seq_recv, chan_send, chan_recv, halo_send, halo_recv,
):
    seq = lax.axis_size("seq")
    chan = lax.axis_size("chan")
    here = lax.axis_index("seq")
    mine = lax.axis_index("chan")
    count, width = q_ref.shape
    _, groups, gw, _ = recv_refs.shape[1:]
    per = groups * gw
    length = h_ref.shape[1]
    columns = go_ref.shape[1]
    tile = max(per, min(256, width))
    tiles = width // tile
    dests = tile // per
    rows = min(512, width)
    wide = min(512, columns)

    def seq_peer(off):
        return lax.rem(here + off, seq)

    def chan_peer(off):
        return lax.rem(mine + off, chan)

    def w_copy(off):
        at = pl.ds(pl.multiple_of(chan_peer(off) * width, width), width)
        return pltpu.make_async_copy(w_hbm.at[at], w_ref.at[at], w_sem.at[off])

    order = [off % chan for off in range(1, chan + 1)]
    for off in order:
        w_copy(off).start()

    barrier = pltpu.get_barrier_semaphore()

    def greet_seq(off, carry):
        pl.semaphore_signal(
            barrier, inc=1, device_id={"seq": seq_peer(off)}, device_id_type=MESH
        )
        return carry

    def greet_chan(off, carry):
        pl.semaphore_signal(
            barrier, inc=1, device_id={"chan": chan_peer(off)}, device_id_type=MESH
        )
        return carry

    lax.fori_loop(1, seq, greet_seq, 0)
    lax.fori_loop(1, chan, greet_chan, 0)

    for m, ref in enumerate((q_ref, k_ref, v_ref)):
        hsend_ref[0, 2 * m : 2 * m + 2, :] = ref[count - 16 :, :].astype(F32)[14:]
        hsend_ref[1, 2 * m : 2 * m + 2, :] = ref[:16, :].astype(F32)[:2]
    pl.semaphore_wait(barrier, seq + chan - 2)

    def halo(slot, by, src, dst):
        return pltpu.make_async_remote_copy(
            src_ref=src, dst_ref=dst, send_sem=halo_send.at[slot], recv_sem=halo_recv.at[slot],
            device_id={"seq": seq_peer(by)}, device_id_type=MESH,
        )

    halo_down = halo(0, 1, hsend_ref.at[0, 0:6], hrecv_ref.at[0, 0:6])
    halo_up = halo(1, seq - 1, hsend_ref.at[1, 0:6], hrecv_ref.at[1, 0:6])
    halo_down.start()
    halo_up.start()

    def turn(i, carry):
        at = pl.ds(pl.multiple_of(i * wide, wide), wide)
        got_ref[at, :] = go_ref[:, at].astype(F32).T.astype(BF16)
        return carry

    lax.fori_loop(0, columns // wide, turn, 0)

    def exchange(slot, off):
        return pltpu.make_async_remote_copy(
            src_ref=send_refs.at[slot, seq_peer(off)],
            dst_ref=recv_refs.at[slot, here],
            send_sem=seq_send.at[slot, off],
            recv_sem=seq_recv.at[slot, off],
            device_id={"seq": seq_peer(off)},
            device_id_type=MESH,
        )

    def exchange_start(slot):
        def go(off, carry):
            exchange(slot, off).start()
            return carry

        lax.fori_loop(1, seq, go, 0)
        recv_refs[slot, pl.ds(here, 1)] = send_refs[slot, pl.ds(here, 1)]

    def exchange_wait(slot):
        def go(off, carry):
            exchange(slot, off).wait()
            return carry

        lax.fori_loop(1, seq, go, 0)

    def to_send(slot, i, turned):
        send_refs[slot, pl.ds(i * dests, dests)] = turned.reshape(
            dests, groups, gw, count
        ).astype(BF16)

    def from_recv(slot, i):
        return recv_refs[slot, pl.ds(i * dests, dests)].astype(F32).reshape(tile, count)

    def cols(i):
        return pl.ds(pl.multiple_of(i * tile, tile), tile)

    def filtered(ref, m, at):
        ahead = jnp.where(here > 0, hrecv_ref[0, 2 * m : 2 * m + 2, at], 0.0)
        return causal(ref[:, at].astype(F32), ahead, taps_ref[3 * m : 3 * m + 3, at])

    halo_down.wait()
    halo_up.wait()

    def spread(slot, make):
        def one(i, carry):
            to_send(slot, i, make(cols(i)))
            return carry

        def off_to(off, carry):
            one(seq_peer(off), 0)
            exchange(slot, off).start()
            return carry

        if dests == 1:
            lax.fori_loop(1, seq, off_to, 0)
            one(here, 0)
            recv_refs[slot, pl.ds(here, 1)] = send_refs[slot, pl.ds(here, 1)]
        else:
            lax.fori_loop(0, tiles, one, 0)
            exchange_start(slot)

    spread(0, lambda at: (filtered(k_ref, 1, at) * filtered(v_ref, 2, at)).T)

    def part(off):
        return pltpu.make_async_remote_copy(
            src_ref=part_send.at[off - 1],
            dst_ref=part_recv.at[mine],
            send_sem=chan_send.at[0, off],
            recv_sem=chan_recv.at[0, off],
            device_id={"chan": chan_peer(off)},
            device_id_type=MESH,
        )

    def back_project(off):
        w_copy(off).wait()

        def some(i, carry):
            start = pl.multiple_of(chan_peer(off) * width + i * rows, rows)
            got = jnp.dot(w_ref[pl.ds(start, rows), :], got_ref[...], preferred_element_type=F32)
            at = pl.ds(pl.multiple_of(i * rows, rows), rows)
            if off:
                part_send[off - 1, at, :] = got.astype(BF16)
            else:
                part_recv[mine, at, :] = got.astype(BF16)
            return carry

        lax.fori_loop(0, width // rows, some, 0)
        if off:
            part(off).start()

    for off in range(1, chan):
        back_project(off)

    flip = (
        lax.broadcasted_iota(jnp.int32, (count, count), 0)
        + lax.broadcasted_iota(jnp.int32, (count, count), 1)
        == count - 1
    )
    flip = jnp.where(flip, 1.0, 0.0).astype(BF16)
    for k in range(length // count):
        hr_ref[:, length - (k + 1) * count : length - k * count] = jnp.dot(
            h_ref[:, k * count : (k + 1) * count].astype(BF16), flip, preferred_element_type=F32
        )

    def build(forward):
        def one(g, carry):
            pad = jnp.zeros((count, count), F32)
            row = (h_ref if forward else hr_ref)[pl.ds(g, 1), :]
            lines = jnp.broadcast_to(row, (count, length))
            pair = [pad, lines] if forward else [lines, pad]
            lined = pltpu.roll(
                jnp.concatenate(pair, axis=1), 0 if forward else 1, 1, stride=1, stride_axis=0
            ).astype(BF16)
            for k in range(length // count):
                at = (k + 1) * count if forward else length - k * count
                filt_ref[g, k * count : (k + 1) * count, :] = lined[:, at : at + count]
            return carry

        lax.fori_loop(0, groups, one, 0)

    def mix(forward, slot):
        total_rows = seq * gw

        def one(g, carry):
            x = recv_refs[slot, :, g]
            kind = F32 if gw % 16 else BF16
            x = x.astype(kind).reshape(total_rows, count)
            pieces = [x.astype(BF16)]
            for k in range(1, seq):
                pad = jnp.zeros((k * gw, count), kind)
                if forward:
                    moved = jnp.concatenate([pad, x[: total_rows - k * gw]], axis=0)
                else:
                    moved = jnp.concatenate([x[k * gw :], pad], axis=0)
                pieces.append(moved.astype(BF16))
            total = jnp.dot(
                jnp.concatenate(pieces, axis=1), filt_ref[g], preferred_element_type=F32
            )
            send_refs[slot + 1, :, g] = total.reshape(seq, gw, count).astype(BF16)
            return carry

        lax.fori_loop(0, groups, one, 0)

    build(True)
    exchange_wait(0)
    mix(True, 0)
    exchange_start(1)
    back_project(0)
    build(False)

    for off in range(1, chan):
        part(off).wait()

    def summed(at):
        return jnp.sum(part_recv[:, at, :].astype(F32), axis=0)

    spread(2, lambda at: summed(at) * filtered(q_ref, 0, at).T)

    def share(off):
        return pltpu.make_async_remote_copy(
            src_ref=gall_ref.at[mine],
            dst_ref=gall_ref.at[mine],
            send_sem=chan_send.at[1, off],
            recv_sem=chan_recv.at[1, off],
            device_id={"chan": chan_peer(off)},
            device_id_type=MESH,
        )

    exchange_wait(1)

    def gate(i, carry):
        at = cols(i)
        gall_ref[mine, :, at] = (filtered(q_ref, 0, at) * from_recv(1, i).T).astype(BF16)
        return carry

    lax.fori_loop(0, tiles, gate, 0)
    for off in range(1, chan):
        share(off).start()

    def grad_query(i, carry):
        at = cols(i)
        gqf_ref[:, at] = (summed(at) * from_recv(1, i)).T.astype(BF16)
        return carry

    lax.fori_loop(0, tiles, grad_query, 0)

    def project(off, first, last):
        owner = chan_peer(chan - off)

        def some(i, carry):
            at = pl.ds(pl.multiple_of(i * wide, wide), wide)
            start = pl.multiple_of(owner * width, width)
            got = jnp.dot(
                gall_ref[owner], w_ref[pl.ds(start, width), at], preferred_element_type=F32
            )
            if not first:
                got = got + acc_ref[:, at]
            if last:
                out_ref[:, at] = got.astype(BF16)
            else:
                acc_ref[:, at] = got
            return carry

        lax.fori_loop(0, columns // wide, some, 0)

    project(0, True, chan == 1)
    exchange_wait(2)
    mix(False, 2)
    exchange_start(3)
    for off in range(1, chan):
        share(off).wait()
        project(off, False, off == chan - 1)

    exchange_wait(3)

    def grad_products(i, carry):
        at = cols(i)
        gp_ref[:, at] = from_recv(3, i).T.astype(BF16)
        return carry

    lax.fori_loop(0, tiles, grad_products, 0)
    tail_ref[0:2, :] = gqf_ref[:16, :].astype(F32)[:2]
    tail_ref[2:4, :] = gp_ref[:16, :].astype(F32)[:2]
    tail = halo(2, seq - 1, tail_ref, head_ref)
    tail.start()
    before_ref[0:6, :] = jnp.where(here > 0, hrecv_ref[0, 0:6, :], 0.0)
    after_ref[4:8, :] = hrecv_ref[1, 2:6, :]
    tail.wait()
    after_ref[0:4, :] = jnp.where(here < seq - 1, head_ref[...], 0.0)


def last_kernel(
    k_ref, v_ref, taps_ref, mixer_ref, gqf_ref, gp_ref, before_ref, after_ref,
    out_ref, gq_ref, gk_ref, gv_ref,
):
    count = k_ref.shape[0]
    gp = gp_ref[...].astype(F32)
    gqf_next = after_ref[0:2]
    gp_next = after_ref[2:4]

    def both(ref, m):
        x = ref[...].astype(F32)
        taps = taps_ref[3 * m : 3 * m + 3]
        new = after_ref[2 + 2 * m : 4 + 2 * m]
        near, far = x[count - 1 : count], x[count - 2 : count - 1]
        first = new[0:1] * taps[0:1] + near * taps[1:2] + far * taps[2:3]
        second = new[1:2] * taps[0:1] + new[0:1] * taps[1:2] + near * taps[2:3]
        inside = causal(x, before_ref[2 * m : 2 * m + 2], taps)
        return inside, jnp.concatenate([first, second], axis=0)

    kf, kf_next = both(k_ref, 1)
    vf, vf_next = both(v_ref, 2)
    out_ref[...] = mixer_ref[...]
    gq_ref[...] = anticausal(gqf_ref[...].astype(F32), gqf_next, taps_ref[0:3]).astype(BF16)
    gk_ref[...] = anticausal(
        rounded(gp * vf), rounded(gp_next * vf_next), taps_ref[3:6]
    ).astype(BF16)
    gv_ref[...] = anticausal(
        rounded(gp * kf), rounded(gp_next * kf_next), taps_ref[6:9]
    ).astype(BF16)


def local(query_proj, key_proj, value_proj, short_filter, long_filter, out_weight, grad_out):
    count, width = query_proj.shape
    seq = lax.axis_size("seq")
    chan = lax.axis_size("chan")
    per = width // seq
    gw = min(per, GROUP)
    groups = per // gw
    length = long_filter.shape[1]
    depth, columns = out_weight.shape

    taps = jnp.repeat(short_filter.transpose(0, 2, 1).reshape(9, -1), GROUP, axis=1)
    first = lax.axis_index("seq") * per // GROUP
    chosen = lax.dynamic_slice_in_dim(long_filter, first, groups, 0).astype(F32)

    vmem = pl.BlockSpec(memory_space=pltpu.VMEM)
    flat = jax.ShapeDtypeStruct((count, width), BF16)
    rims = jax.ShapeDtypeStruct((8, width), F32)
    mixer_out, grad_qf, grad_prod, before, after = pl.pallas_call(
        step_kernel,
        in_specs=[vmem] * 5 + [pl.BlockSpec(memory_space=pl.ANY), vmem],
        out_specs=[vmem] * 5,
        out_shape=[jax.ShapeDtypeStruct((count, columns), BF16), flat, flat, rims, rims],
        scratch_shapes=[
            pltpu.VMEM((depth, columns), BF16),
            pltpu.VMEM((columns, count), BF16),
            pltpu.VMEM((groups, length), F32),
            pltpu.VMEM((groups, length, count), BF16),
            pltpu.VMEM((4, seq, groups, gw, count), BF16),
            pltpu.VMEM((4, seq, groups, gw, count), BF16),
            pltpu.VMEM((chan - 1, width, count), BF16),
            pltpu.VMEM((chan, width, count), BF16),
            pltpu.VMEM((chan, count, width), BF16),
            pltpu.VMEM((count, columns), F32),
            pltpu.VMEM((2, 8, width), F32),
            pltpu.VMEM((2, 8, width), F32),
            pltpu.VMEM((4, width), F32),
            pltpu.VMEM((4, width), F32),
            pltpu.SemaphoreType.DMA((chan,)),
            pltpu.SemaphoreType.DMA((4, seq)),
            pltpu.SemaphoreType.DMA((4, seq)),
            pltpu.SemaphoreType.DMA((2, chan)),
            pltpu.SemaphoreType.DMA((2, chan)),
            pltpu.SemaphoreType.DMA((3,)),
            pltpu.SemaphoreType.DMA((3,)),
        ],
        compiler_params=pltpu.CompilerParams(
            collective_id=0, has_side_effects=True, vmem_limit_bytes=62 * 1024 * 1024
        ),
        name="step",
    )(query_proj, key_proj, value_proj, taps, chosen, out_weight, grad_out)

    tile = min(512, width)

    def tall(rows):
        return pl.BlockSpec((rows, tile), lambda i: (0, i))

    return pl.pallas_call(
        last_kernel,
        grid=(width // tile,),
        in_specs=[tall(count), tall(count), tall(9)] + [tall(count)] * 3 + [tall(8)] * 2,
        out_specs=[tall(count)] * 4,
        out_shape=[flat] * 4,
        compiler_params=pltpu.CompilerParams(vmem_limit_bytes=62 * 1024 * 1024),
        name="last",
    )(key_proj, value_proj, taps, mixer_out, grad_qf, grad_prod, before, after)


def flipped(x, flip):
    return jnp.dot(flip, x, preferred_element_type=F32)


def pair_kernel(
    q_hbm, k_hbm, v_hbm, taps_in, h_hbm, w_hbm, go_hbm,
    out_hbm, gq_hbm, gk_hbm, gv_hbm,
    w_ref, go_ref, x_ref, taps_ref, h_ref, filt_ref, hf_ref,
    filtered_ref, prod_ref, gm_ref, rf_ref, rb_ref, xt_ref, ot_ref, ms_ref, mixed_ref, gp_ref,
    total_ref, sx_ref, sy_ref, rx_ref, ry_ref, ga_ref, acc_ref,
    gf_ref, head_ref, fin_ref, mo_send, mo_recv, mo_ref,
    w_sem, in_sem, send_sem, recv_sem, out_sem,
):
    here = lax.axis_index("seq")
    mine = lax.axis_index("chan")
    seq = lax.axis_size("seq")
    count = go_hbm.shape[0]
    width = q_hbm.shape[1]
    half = width // 2
    span = 2 * count
    nblk, _, bw = prod_ref.shape
    columns = go_hbm.shape[1]
    chips = seq // 2
    core = lax.rem(here, 2)
    other = 1 - core
    z = here // 2
    zo = z + 1 - 2 * lax.rem(z, 2)
    zq = lax.rem(z, 2)
    zh = z // 2
    bx = mine + 1 - 2 * lax.rem(mine, 2)
    by = lax.rem(mine + 2, 4)
    bd = lax.rem(bx + 2, 4)
    who_id = (mine, bx, by, bd)
    SIB = {"seq": 2 * z + other}
    X = {"chan": bx}
    Y = {"chan": by}
    groups = bw // GROUP
    length = h_ref.shape[1]

    def w_copy(who, blk):
        start = pl.multiple_of(who_id[who] * width + core * half + blk * bw, bw)
        return pltpu.make_async_copy(
            w_hbm.at[pl.ds(start, bw)], w_ref.at[who, blk], w_sem.at[who * 4 + blk]
        )

    mycols = pl.ds(pl.multiple_of(core * half, half), half)
    sibcols = pl.ds(pl.multiple_of(other * half, half), half)
    myrows = pl.ds(pl.multiple_of(core * count, count), count)
    sibrows = pl.ds(pl.multiple_of(other * count, count), count)
    slabrows = pl.ds(pl.multiple_of(16 + core * count, 16), count)

    ins = [pltpu.make_async_copy(go_hbm, go_ref.at[myrows], in_sem.at[0])]
    for m, src in enumerate((q_hbm, k_hbm, v_hbm)):
        ins.append(pltpu.make_async_copy(src.at[:, mycols], x_ref.at[m, slabrows], in_sem.at[1 + m]))
    first = pl.multiple_of(core * (half // GROUP) + zq * (half // GROUP // 2), 16)
    ins.append(pltpu.make_async_copy(h_hbm.at[pl.ds(first, 2 * groups)], h_ref, in_sem.at[4]))
    order = [
        [(3, c), (3, 2 + c), (1, c), (2, 2 + c), (0, c), (0, 2 + c), (1, 2 + c), (2, c)]
        for c in range(2)
    ]
    ins[0].start()
    w_copy(*order[0][0]).start()
    w_copy(*order[0][1]).start()
    for i in (2, 3, 1, 4):
        ins[i].start()
    for c in range(2):
        for who, blk in order[c]:
            if c or (who != 3):
                w_copy(who, blk).start()

    barrier = pltpu.get_barrier_semaphore()

    def greet(off, carry):
        pl.semaphore_signal(
            barrier, inc=1, device_id={"seq": lax.rem(here + off, seq)}, device_id_type=MESH
        )
        return carry

    lax.fori_loop(1, seq, greet, 0)
    for peer in (X, Y):
        pl.semaphore_signal(barrier, inc=1, device_id=peer, device_id_type=MESH)
    pl.semaphore_wait(barrier, seq + 1)

    def remote(src, dst, to, send, recv=None):
        return pltpu.make_async_remote_copy(
            src_ref=src, dst_ref=dst, send_sem=send_sem.at[send],
            recv_sem=recv_sem.at[send if recv is None else recv],
            device_id=to, device_id_type=MESH,
        )

    swaps = [remote(go_hbm, go_ref.at[myrows], SIB, 0)]
    for m, src in enumerate((q_hbm, k_hbm, v_hbm)):
        swaps.append(remote(src.at[:, sibcols], x_ref.at[m, slabrows], SIB, 1 + m))
    for i in (0, 2, 3, 1):
        swaps[i].start()

    def rim(m, to):
        src = (q_hbm, k_hbm, v_hbm)[m]
        at = pl.ds(pl.multiple_of(to * half, half), half)
        return remote(
            src.at[count - 16 : count, at], x_ref.at[m, 0:16],
            {"seq": 2 * lax.rem(z + 1, chips) + to}, 4 + 2 * m + to, 4 + 2 * m,
        )

    sends_rim = (core == 1) & (z < chips - 1)

    @pl.when(sends_rim)
    def _():
        for m in (1, 2, 0):
            for to in range(2):
                rim(m, to).start()

    @pl.when(z == 0)
    def _():
        x_ref[:, 0:16] = jnp.zeros((3, 16, half), BF16)

    def rim_wait(m):
        @pl.when(z > 0)
        def _():
            rim(m, 0).wait_recv()

    rows = [taps_in[m] for m in range(3)]
    taps9 = jnp.concatenate(rows + [jnp.zeros((7, taps_in.shape[2]), F32)], axis=0)
    shape = (taps_in.shape[2], bw)
    group_at = lax.broadcasted_iota(jnp.int32, shape, 0)
    chan_at = lax.broadcasted_iota(jnp.int32, shape, 1)
    for b in range(nblk):
        pick = group_at * GROUP - (core * half + b * bw)
        hot = jnp.where((chan_at >= pick) & (chan_at < pick + GROUP), 1.0, 0.0).astype(F32)
        taps_ref[b] = jnp.dot(taps9, hot, precision=lax.Precision.HIGHEST, preferred_element_type=F32)

    flip = (
        lax.broadcasted_iota(jnp.int32, (count, count), 0)
        + lax.broadcasted_iota(jnp.int32, (count, count), 1)
        == count - 1
    )
    flip = jnp.where(flip, 1.0, 0.0).astype(BF16)
    xt_ref[:, 0:3] = jnp.zeros((groups, 3, GROUP, count), BF16)

    def back(who, blk):
        w_copy(who, blk).wait()
        return lax.dot_general(
            go_ref[...], w_ref[who, blk], (((1,), (1,)), ((), ())), preferred_element_type=F32
        )

    def cx(c, i):
        return remote(sx_ref.at[c, i], rx_ref.at[c, i], X, 16 + c * 3 + i)

    def cy(c, i):
        return remote(sy_ref.at[c, i], ry_ref.at[c, i], Y, 22 + c * 3 + i)

    def sums_diag(c):
        sx_ref[c, 0] = back(3, c).astype(BF16)
        cx(c, 0).start()
        sy_ref[c, 0] = back(3, 2 + c).astype(BF16)
        cy(c, 0).start()

    def sums_near(c):
        sx_ref[c, 1] = back(1, c).astype(BF16)
        cx(c, 1).start()
        sy_ref[c, 1] = back(2, 2 + c).astype(BF16)
        cy(c, 1).start()

    def sums_own(c):
        total_ref[c] = back(0, c)
        total_ref[2 + c] = back(0, 2 + c)

    def sums_joined(c):
        cy(c, 0).wait_recv()
        sx_ref[c, 2] = (back(1, 2 + c) + ry_ref[c, 0].astype(F32)).astype(BF16)
        cx(c, 2).start()
        cx(c, 0).wait_recv()
        sy_ref[c, 2] = (back(2, c) + rx_ref[c, 0].astype(F32)).astype(BF16)
        cy(c, 2).start()

    def cols(b):
        return pl.ds(pl.multiple_of(b * bw, bw), bw)

    def filtering(m, b):
        x = x_ref[m, :, cols(b)].astype(F32)
        taps = taps_ref[b, 3 * m : 3 * m + 3]
        y = x * taps[0:1] + pltpu.roll(x, 1, 0) * taps[1:2] + pltpu.roll(x, 2, 0) * taps[2:3]
        filtered_ref[m, b] = y[16:]
        return y[16:]

    ZF, ZB, RF, RB = 32, 40, 48, 50

    def ok_fwd(src, dst):
        return dst // 2 >= src // 2

    def ok_bwd(src, dst):
        return dst // 2 <= src // 2

    def zcopy(base, src, dst, c, to, frm):
        return remote(
            src.at[2 * lax.rem(to, 2) + c], dst.at[frm, c], {"seq": 2 * to + core},
            base + 2 * to + c, base + 2 * frm + c,
        )

    def zeach(ok, act):
        for d in range(1, chips):
            peer = lax.rem(z + d, chips)
            pl.when(ok(peer))(lambda peer=peer: act(peer))

    def zsend(base, src, dst, c, ok):
        zeach(lambda p: ok(z, p), lambda p: zcopy(base, src, dst, c, p, z).start())
        dst[z, c] = src[2 * zq + c]

    def zwait(base, src, dst, c, ok):
        zeach(lambda p: ok(p, z), lambda p: zcopy(base, src, dst, c, z, p).wait_recv())

    def zdone(base, src, dst, c, ok):
        zeach(lambda p: ok(z, p), lambda p: zcopy(base, src, dst, c, p, z).wait_send())

    def ret(forward, c):
        dst = mixed_ref if forward else gp_ref
        base = RF if forward else RB
        i = 0 if forward else 1
        return remote(
            ms_ref.at[i, c, lax.rem(zo, 2)], dst.at[2 * zq + c], {"seq": 2 * zo + core}, base + c
        )

    def ret_wait(forward, c):
        dst = mixed_ref if forward else gp_ref
        base = RF if forward else RB
        i = 0 if forward else 1
        remote(
            ms_ref.at[i, c, 0], dst.at[2 * (1 - zq) + c], {"seq": 2 * zo + core}, base + c
        ).wait_recv()

    def build(lo, hi):
        def one(g, carry):
            row = hf_ref[pl.ds(g, 1), :]
            lines = jnp.broadcast_to(row, (count, length))
            both = jnp.concatenate([jnp.zeros((count, count), F32), lines], axis=1)
            lined = pltpu.roll(both, 0, 1, stride=1, stride_axis=0).astype(BF16)
            for k in range(length // count):
                at = (k + 1) * count
                filt_ref[g, k * count : (k + 1) * count, :] = lined[:, at : at + count]
            return carry

        lax.fori_loop(lo, hi, one, 0)

    def mix(forward, c):
        src = rf_ref if forward else rb_ref
        late = (zh == 1) if forward else (zh == 0)
        lags = length // count
        outs = lags // 2

        def fill(chip, slot):
            for blk in range(2):
                x = src[chip, c, blk * count : (blk + 1) * count, :]
                if forward:
                    at, x = blk, x.astype(F32)
                else:
                    at, x = 1 - blk, flipped(x, flip)
                xt_ref[:, 3 + slot + at] = x.T.reshape(groups, GROUP, count).astype(BF16)

        for i in range(2):
            r = i if forward else 1 - i
            fill(2 * zh + r, outs + 2 * i)

        def run(depth):
            def one(g, carry):
                pieces = [
                    xt_ref[g, 3 + outs - k : 3 + 2 * outs - k].reshape(outs * GROUP, count)
                    for k in range(depth)
                ]
                got = jnp.dot(
                    jnp.concatenate(pieces, axis=1),
                    filt_ref[groups * c + g, : depth * count],
                    preferred_element_type=F32,
                )
                ot_ref[:, g] = got.reshape(outs, GROUP, count)
                return carry

            lax.fori_loop(0, groups, one, 0)

        @pl.when(late)
        def _():
            for i in range(2):
                r = i if forward else 1 - i
                fill(2 * (1 - zh) + r, 2 * i)
            run(lags)

        @pl.when(jnp.logical_not(late))
        def _():
            xt_ref[:, 3 : 3 + outs] = jnp.zeros((groups, outs, GROUP, count), BF16)
            run(outs)

        i = 0 if forward else 1
        for b in range(outs):
            y = ot_ref[b].reshape(bw, count).T.astype(BF16)
            at = b
            if not forward:
                y = flipped(y, flip).astype(BF16)
                at = outs - 1 - b
            ms_ref[i, c, at // 2, (at % 2) * count : (at % 2 + 1) * count, :] = y
        ret(forward, c).start()
        dst = mixed_ref if forward else gp_ref
        dst[2 * zq + c] = ms_ref[i, c, zq]

    def sums_done(c):
        cx(c, 1).wait_recv()
        cy(c, 2).wait_recv()
        total_ref[c] += rx_ref[c, 1].astype(F32) + ry_ref[c, 2].astype(F32)
        gm_ref[c] = (total_ref[c] * filtered_ref[0, c]).astype(BF16)
        cy(c, 1).wait_recv()
        cx(c, 2).wait_recv()
        total_ref[2 + c] += ry_ref[c, 1].astype(F32) + rx_ref[c, 2].astype(F32)
        gm_ref[2 + c] = (total_ref[2 + c] * filtered_ref[0, 2 + c]).astype(BF16)
        zsend(ZB, gm_ref, rb_ref, c, ok_bwd)

    def ax(c, i):
        blk = (c, 2 + c, 2 + c)[i]
        return remote(ga_ref.at[2 if i == 2 else 0, blk], ga_ref.at[3 if i == 2 else 1, blk], X, 52 + 3 * c + i)

    def ay(c, i):
        blk = (2 + c, c, c)[i]
        return remote(ga_ref.at[1 if i == 2 else 0, blk], ga_ref.at[3 if i == 2 else 2, blk], Y, 58 + 3 * c + i)

    def gate(c):
        ret_wait(True, c)
        for b in (c, 2 + c):
            ga_ref[0, b] = (filtered_ref[0, b] * mixed_ref[b].astype(F32)).astype(BF16)
        for i in range(2):
            ax(c, i).start()
            ay(c, i).start()
        for b in (c, 2 + c):
            gf_ref[0, b] = (total_ref[b] * mixed_ref[b].astype(F32)).astype(BF16)

    def relay(c):
        ax(c, 0).wait_recv()
        ay(c, 2).start()
        ay(c, 0).wait_recv()
        ax(c, 2).start()

    wide = min(512, columns)

    def project(who, c, first_one=False):
        def some(i, carry):
            at = pl.ds(pl.multiple_of(i * wide, wide), wide)
            got = jnp.dot(ga_ref[who, c], w_ref[who, c, :, at], preferred_element_type=F32)
            got += jnp.dot(ga_ref[who, 2 + c], w_ref[who, 2 + c, :, at], preferred_element_type=F32)
            acc_ref[:, at] = got if first_one else acc_ref[:, at] + got
            return carry

        lax.fori_loop(0, columns // wide, some, 0)

    def heads(m):
        return remote(
            gf_ref.at[m, :, 0:16], head_ref.at[m],
            {"seq": 2 * lax.rem(z + chips - 1, chips) + core}, 64 + m,
        )

    def heads_start(m):
        @pl.when(z > 0)
        def _():
            heads(m).start()

    def finish(m, ref):
        @pl.when(z < chips - 1)
        def _():
            heads(m).wait_recv()

        for b in range(nblk):
            g = gf_ref[m, b].astype(F32)
            taps = taps_ref[b, 3 * m : 3 * m + 3]
            after = jnp.where(z < chips - 1, head_ref[m, b].astype(F32)[0:2], 0.0)
            fin_ref[m, :, b * bw : (b + 1) * bw] = anticausal(g, after, taps).astype(BF16)
        pltpu.make_async_copy(fin_ref.at[m, myrows], ref.at[:, mycols], out_sem.at[m]).start()
        remote(fin_ref.at[m, sibrows], ref.at[:, mycols], SIB, 67 + m).start()

    ins[0].wait()
    swaps[0].wait_recv()
    sums_diag(0)
    for m in (1, 2):
        ins[1 + m].wait()
        swaps[1 + m].wait_recv()
        rim_wait(m)
    for b in (0, 2, 1, 3):
        prod_ref[b] = (filtering(1, b) * filtering(2, b)).astype(BF16)
        if b >= 2:
            zsend(ZF, prod_ref, rf_ref, b - 2, ok_fwd)
    sums_near(0)
    sums_own(0)
    sums_joined(0)
    sums_diag(1)
    sums_near(1)
    sums_own(1)
    ins[1].wait()
    swaps[1].wait_recv()
    rim_wait(0)
    for b in range(nblk):
        filtering(0, b)
    ins[4].wait()
    hf_ref[...] = h_ref[...].astype(F32)
    build(0, groups)
    sums_done(0)
    sums_joined(1)
    build(groups, 2 * groups)
    zwait(ZF, prod_ref, rf_ref, 0, ok_fwd)
    mix(True, 0)
    sums_done(1)
    gate(0)
    project(0, 0, True)
    relay(0)
    zwait(ZF, prod_ref, rf_ref, 1, ok_fwd)
    mix(True, 1)
    ax(0, 1).wait_recv()
    project(1, 0)
    ay(0, 1).wait_recv()
    project(2, 0)
    zwait(ZB, gm_ref, rb_ref, 0, ok_bwd)
    mix(False, 0)
    gate(1)
    heads_start(0)
    project(0, 1)
    ax(0, 2).wait_recv()
    ay(0, 2).wait_recv()
    project(3, 0)
    finish(0, gq_hbm)
    relay(1)
    zwait(ZB, gm_ref, rb_ref, 1, ok_bwd)
    mix(False, 1)
    ax(1, 1).wait_recv()
    project(1, 1)
    ay(1, 1).wait_recv()
    project(2, 1)
    for c in range(2):
        ret_wait(False, c)
    for b in range(nblk):
        gp = gp_ref[b].astype(F32)
        gf_ref[1, b] = (gp * filtered_ref[2, b]).astype(BF16)
        gf_ref[2, b] = (gp * filtered_ref[1, b]).astype(BF16)
    heads_start(1)
    heads_start(2)
    ax(1, 2).wait_recv()
    ay(1, 2).wait_recv()
    project(3, 1)
    mo_send[...] = acc_ref[sibrows, :].astype(BF16)
    mo = remote(mo_send, mo_recv, SIB, 70)
    mo.start()
    finish(1, gk_hbm)
    finish(2, gv_hbm)
    mo.wait_recv()
    mo_ref[...] = (acc_ref[myrows, :] + mo_recv[...].astype(F32)).astype(BF16)
    pltpu.make_async_copy(mo_ref, out_hbm, out_sem.at[3]).start()

    for copy in swaps + [mo]:
        copy.wait_send()

    @pl.when(sends_rim)
    def _():
        for m in range(3):
            for to in range(2):
                rim(m, to).wait_send()

    for c in range(2):
        for i in range(3):
            for make in (cx, cy, ax, ay):
                make(c, i).wait_send()
        zdone(ZF, prod_ref, rf_ref, c, ok_fwd)
        zdone(ZB, gm_ref, rb_ref, c, ok_bwd)
        for forward in (True, False):
            ret(forward, c).wait_send()

    @pl.when(z > 0)
    def _():
        for m in range(3):
            heads(m).wait_send()

    for m, ref in enumerate((gq_hbm, gk_hbm, gv_hbm)):
        pltpu.make_async_copy(fin_ref.at[m, myrows], ref.at[:, mycols], out_sem.at[m]).wait()
        out = remote(fin_ref.at[m, sibrows], ref.at[:, mycols], SIB, 67 + m)
        out.wait_send()
        remote(fin_ref.at[m, sibrows], ref.at[:, sibcols], SIB, 67 + m).wait_recv()
    pltpu.make_async_copy(mo_ref, out_hbm, out_sem.at[3]).wait()


def copy_kernel(*refs):
    for src, dst in zip(refs[:4], refs[4:]):
        dst[...] = src[...]


def paired(query_proj, key_proj, value_proj, short_filter, long_filter, out_weight, grad_out):
    count, width = query_proj.shape
    length = long_filter.shape[1]
    columns = out_weight.shape[1]
    half = width // 2
    span = 2 * count
    bw = half // 4
    groups = bw // GROUP
    lags = length // count

    vmem = pl.BlockSpec(memory_space=pltpu.VMEM)
    hbm = pl.BlockSpec(memory_space=pl.ANY)
    flat = jax.ShapeDtypeStruct((count, width), BF16)
    block = (span, bw)
    results = pl.pallas_call(
        pair_kernel,
        in_specs=[hbm] * 3 + [vmem] + [hbm] * 3,
        out_specs=[hbm] * 4,
        out_shape=[flat] * 4,
        scratch_shapes=[
            pltpu.VMEM((4, 4, bw, columns), BF16),
            pltpu.VMEM((span, columns), BF16),
            pltpu.VMEM((3, 16 + span, half), BF16),
            pltpu.VMEM((4, 16, bw), F32),
            pltpu.VMEM((2 * groups, length), BF16),
            pltpu.VMEM((2 * groups, length, count), BF16),
            pltpu.VMEM((2 * groups, length), F32),
            pltpu.VMEM((3, 4) + block, F32),
            pltpu.VMEM((4,) + block, BF16),
            pltpu.VMEM((4,) + block, BF16),
            pltpu.VMEM((4, 2) + block, BF16),
            pltpu.VMEM((4, 2) + block, BF16),
            pltpu.VMEM((groups, 3 + lags, GROUP, count), BF16),
            pltpu.VMEM((lags // 2, groups, GROUP, count), F32),
            pltpu.VMEM((2, 2, 2) + block, BF16),
            pltpu.VMEM((4,) + block, BF16),
            pltpu.VMEM((4,) + block, BF16),
            pltpu.VMEM((4,) + block, F32),
            pltpu.VMEM((2, 3) + block, BF16),
            pltpu.VMEM((2, 3) + block, BF16),
            pltpu.VMEM((2, 3) + block, BF16),
            pltpu.VMEM((2, 3) + block, BF16),
            pltpu.VMEM((4, 4) + block, BF16),
            pltpu.VMEM((span, columns), F32),
            pltpu.VMEM((3, 4) + block, BF16),
            pltpu.VMEM((3, 4, 16, bw), BF16),
            pltpu.VMEM((3, span, half), BF16),
            pltpu.VMEM((count, columns), BF16),
            pltpu.VMEM((count, columns), BF16),
            pltpu.VMEM((count, columns), BF16),
            pltpu.SemaphoreType.DMA((16,)),
            pltpu.SemaphoreType.DMA((5,)),
            pltpu.SemaphoreType.DMA((72,)),
            pltpu.SemaphoreType.DMA((72,)),
            pltpu.SemaphoreType.DMA((4,)),
        ],
        compiler_params=pltpu.CompilerParams(
            collective_id=0, has_side_effects=True, vmem_limit_bytes=62 * 1024 * 1024
        ),
        name="step",
    )(
        query_proj, key_proj, value_proj, short_filter.transpose(0, 2, 1),
        long_filter, out_weight, grad_out,
    )
    return pl.pallas_call(
        copy_kernel,
        in_specs=[vmem] * 4,
        out_specs=[vmem] * 4,
        out_shape=[flat] * 4,
        compiler_params=pltpu.CompilerParams(vmem_limit_bytes=32 * 1024 * 1024),
        name="last",
    )(*results)


def either(query_proj, key_proj, value_proj, short_filter, long_filter, out_weight, grad_out):
    args = (query_proj, key_proj, value_proj, short_filter, long_filter, out_weight, grad_out)
    count, width = query_proj.shape
    fits = (
        lax.axis_size("seq") == 8
        and lax.axis_size("chan") == 4
        and count % 128 == 0
        and width % 2048 == 0
        and long_filter.shape[1] == 8 * count
    )
    return paired(*args) if fits else local(*args)


def solution(mesh):
    return jax.shard_map(
        either,
        mesh=mesh,
        in_specs=(
            P("seq", "chan"),
            P("seq", "chan"),
            P("seq", "chan"),
            P(None, "chan", None),
            P("chan", None),
            P(None, "chan"),
            P("seq", "chan"),
        ),
        out_specs=(P("seq", "chan"), P("seq", "chan"), P("seq", "chan"), P("seq", "chan")),
        check_vma=False,
    )
```

```python
import jax
import jax.numpy as jnp
from jax import lax
from jax.experimental import pallas as pl
from jax.experimental.pallas import tpu as pltpu
from jax.sharding import PartitionSpec as P

GROUP = 16
F32 = jnp.float32
BF16 = jnp.bfloat16
MESH = pl.DeviceIdType.MESH


def causal(x, before, taps):
    row = lax.broadcasted_iota(jnp.int32, x.shape, 0)
    one = jnp.where(row == 0, before[1:2], pltpu.roll(x, 1, 0))
    two = jnp.where(row == 0, before[0:1], jnp.where(row == 1, before[1:2], pltpu.roll(x, 2, 0)))
    return x * taps[0:1] + one * taps[1:2] + two * taps[2:3]


def anticausal(g, after, taps):
    count = g.shape[0]
    row = lax.broadcasted_iota(jnp.int32, g.shape, 0)
    one = jnp.where(row == count - 1, after[0:1], pltpu.roll(g, count - 1, 0))
    two = jnp.where(
        row == count - 1,
        after[1:2],
        jnp.where(row == count - 2, after[0:1], pltpu.roll(g, count - 2, 0)),
    )
    return g * taps[0:1] + one * taps[1:2] + two * taps[2:3]


def rounded(x):
    return x.astype(BF16).astype(F32)


def step_kernel(
    q_ref, k_ref, v_ref, taps_ref, h_ref, w_hbm, go_ref,
    out_ref, gqf_ref, gp_ref, before_ref, after_ref,
    w_ref, got_ref, hr_ref, filt_ref, send_refs, recv_refs, part_send, part_recv, gall_ref,
    acc_ref, hsend_ref, hrecv_ref, tail_ref, head_ref,
    w_sem, seq_send, seq_recv, chan_send, chan_recv, halo_send, halo_recv,
):
    seq = lax.axis_size("seq")
    chan = lax.axis_size("chan")
    here = lax.axis_index("seq")
    mine = lax.axis_index("chan")
    count, width = q_ref.shape
    _, groups, gw, _ = recv_refs.shape[1:]
    per = groups * gw
    length = h_ref.shape[1]
    columns = go_ref.shape[1]
    tile = max(per, min(256, width))
    tiles = width // tile
    dests = tile // per
    rows = min(512, width)
    wide = min(512, columns)

    def seq_peer(off):
        return lax.rem(here + off, seq)

    def chan_peer(off):
        return lax.rem(mine + off, chan)

    def w_copy(off):
        at = pl.ds(pl.multiple_of(chan_peer(off) * width, width), width)
        return pltpu.make_async_copy(w_hbm.at[at], w_ref.at[at], w_sem.at[off])

    order = [off % chan for off in range(1, chan + 1)]
    for off in order:
        w_copy(off).start()

    barrier = pltpu.get_barrier_semaphore()

    def greet_seq(off, carry):
        pl.semaphore_signal(
            barrier, inc=1, device_id={"seq": seq_peer(off)}, device_id_type=MESH
        )
        return carry

    def greet_chan(off, carry):
        pl.semaphore_signal(
            barrier, inc=1, device_id={"chan": chan_peer(off)}, device_id_type=MESH
        )
        return carry

    lax.fori_loop(1, seq, greet_seq, 0)
    lax.fori_loop(1, chan, greet_chan, 0)

    for m, ref in enumerate((q_ref, k_ref, v_ref)):
        hsend_ref[0, 2 * m : 2 * m + 2, :] = ref[count - 16 :, :].astype(F32)[14:]
        hsend_ref[1, 2 * m : 2 * m + 2, :] = ref[:16, :].astype(F32)[:2]
    pl.semaphore_wait(barrier, seq + chan - 2)

    def halo(slot, by, src, dst):
        return pltpu.make_async_remote_copy(
            src_ref=src, dst_ref=dst, send_sem=halo_send.at[slot], recv_sem=halo_recv.at[slot],
            device_id={"seq": seq_peer(by)}, device_id_type=MESH,
        )

    halo_down = halo(0, 1, hsend_ref.at[0, 0:6], hrecv_ref.at[0, 0:6])
    halo_up = halo(1, seq - 1, hsend_ref.at[1, 0:6], hrecv_ref.at[1, 0:6])
    halo_down.start()
    halo_up.start()

    def turn(i, carry):
        at = pl.ds(pl.multiple_of(i * wide, wide), wide)
        got_ref[at, :] = go_ref[:, at].astype(F32).T.astype(BF16)
        return carry

    lax.fori_loop(0, columns // wide, turn, 0)

    def exchange(slot, off):
        return pltpu.make_async_remote_copy(
            src_ref=send_refs.at[slot, seq_peer(off)],
            dst_ref=recv_refs.at[slot, here],
            send_sem=seq_send.at[slot, off],
            recv_sem=seq_recv.at[slot, off],
            device_id={"seq": seq_peer(off)},
            device_id_type=MESH,
        )

    def exchange_start(slot):
        def go(off, carry):
            exchange(slot, off).start()
            return carry

        lax.fori_loop(1, seq, go, 0)
        recv_refs[slot, pl.ds(here, 1)] = send_refs[slot, pl.ds(here, 1)]

    def exchange_wait(slot):
        def go(off, carry):
            exchange(slot, off).wait()
            return carry

        lax.fori_loop(1, seq, go, 0)

    def to_send(slot, i, turned):
        send_refs[slot, pl.ds(i * dests, dests)] = turned.reshape(
            dests, groups, gw, count
        ).astype(BF16)

    def from_recv(slot, i):
        return recv_refs[slot, pl.ds(i * dests, dests)].astype(F32).reshape(tile, count)

    def cols(i):
        return pl.ds(pl.multiple_of(i * tile, tile), tile)

    def filtered(ref, m, at):
        ahead = jnp.where(here > 0, hrecv_ref[0, 2 * m : 2 * m + 2, at], 0.0)
        return causal(ref[:, at].astype(F32), ahead, taps_ref[3 * m : 3 * m + 3, at])

    halo_down.wait()
    halo_up.wait()

    def spread(slot, make):
        def one(i, carry):
            to_send(slot, i, make(cols(i)))
            return carry

        def off_to(off, carry):
            one(seq_peer(off), 0)
            exchange(slot, off).start()
            return carry

        if dests == 1:
            lax.fori_loop(1, seq, off_to, 0)
            one(here, 0)
            recv_refs[slot, pl.ds(here, 1)] = send_refs[slot, pl.ds(here, 1)]
        else:
            lax.fori_loop(0, tiles, one, 0)
            exchange_start(slot)

    spread(0, lambda at: (filtered(k_ref, 1, at) * filtered(v_ref, 2, at)).T)

    def part(off):
        return pltpu.make_async_remote_copy(
            src_ref=part_send.at[off - 1],
            dst_ref=part_recv.at[mine],
            send_sem=chan_send.at[0, off],
            recv_sem=chan_recv.at[0, off],
            device_id={"chan": chan_peer(off)},
            device_id_type=MESH,
        )

    def back_project(off):
        w_copy(off).wait()

        def some(i, carry):
            start = pl.multiple_of(chan_peer(off) * width + i * rows, rows)
            got = jnp.dot(w_ref[pl.ds(start, rows), :], got_ref[...], preferred_element_type=F32)
            at = pl.ds(pl.multiple_of(i * rows, rows), rows)
            if off:
                part_send[off - 1, at, :] = got.astype(BF16)
            else:
                part_recv[mine, at, :] = got.astype(BF16)
            return carry

        lax.fori_loop(0, width // rows, some, 0)
        if off:
            part(off).start()

    for off in range(1, chan):
        back_project(off)

    flip = (
        lax.broadcasted_iota(jnp.int32, (count, count), 0)
        + lax.broadcasted_iota(jnp.int32, (count, count), 1)
        == count - 1
    )
    flip = jnp.where(flip, 1.0, 0.0).astype(BF16)
    for k in range(length // count):
        hr_ref[:, length - (k + 1) * count : length - k * count] = jnp.dot(
            h_ref[:, k * count : (k + 1) * count].astype(BF16), flip, preferred_element_type=F32
        )

    def build(forward):
        def one(g, carry):
            pad = jnp.zeros((count, count), F32)
            row = (h_ref if forward else hr_ref)[pl.ds(g, 1), :]
            lines = jnp.broadcast_to(row, (count, length))
            pair = [pad, lines] if forward else [lines, pad]
            lined = pltpu.roll(
                jnp.concatenate(pair, axis=1), 0 if forward else 1, 1, stride=1, stride_axis=0
            ).astype(BF16)
            for k in range(length // count):
                at = (k + 1) * count if forward else length - k * count
                filt_ref[g, k * count : (k + 1) * count, :] = lined[:, at : at + count]
            return carry

        lax.fori_loop(0, groups, one, 0)

    def mix(forward, slot):
        total_rows = seq * gw

        def one(g, carry):
            x = recv_refs[slot, :, g]
            kind = F32 if gw % 16 else BF16
            x = x.astype(kind).reshape(total_rows, count)
            pieces = [x.astype(BF16)]
            for k in range(1, seq):
                pad = jnp.zeros((k * gw, count), kind)
                if forward:
                    moved = jnp.concatenate([pad, x[: total_rows - k * gw]], axis=0)
                else:
                    moved = jnp.concatenate([x[k * gw :], pad], axis=0)
                pieces.append(moved.astype(BF16))
            total = jnp.dot(
                jnp.concatenate(pieces, axis=1), filt_ref[g], preferred_element_type=F32
            )
            send_refs[slot + 1, :, g] = total.reshape(seq, gw, count).astype(BF16)
            return carry

        lax.fori_loop(0, groups, one, 0)

    build(True)
    exchange_wait(0)
    mix(True, 0)
    exchange_start(1)
    back_project(0)
    build(False)

    for off in range(1, chan):
        part(off).wait()

    def summed(at):
        return jnp.sum(part_recv[:, at, :].astype(F32), axis=0)

    spread(2, lambda at: summed(at) * filtered(q_ref, 0, at).T)

    def share(off):
        return pltpu.make_async_remote_copy(
            src_ref=gall_ref.at[mine],
            dst_ref=gall_ref.at[mine],
            send_sem=chan_send.at[1, off],
            recv_sem=chan_recv.at[1, off],
            device_id={"chan": chan_peer(off)},
            device_id_type=MESH,
        )

    exchange_wait(1)

    def gate(i, carry):
        at = cols(i)
        gall_ref[mine, :, at] = (filtered(q_ref, 0, at) * from_recv(1, i).T).astype(BF16)
        return carry

    lax.fori_loop(0, tiles, gate, 0)
    for off in range(1, chan):
        share(off).start()

    def grad_query(i, carry):
        at = cols(i)
        gqf_ref[:, at] = (summed(at) * from_recv(1, i)).T.astype(BF16)
        return carry

    lax.fori_loop(0, tiles, grad_query, 0)

    def project(off, first, last):
        owner = chan_peer(chan - off)

        def some(i, carry):
            at = pl.ds(pl.multiple_of(i * wide, wide), wide)
            start = pl.multiple_of(owner * width, width)
            got = jnp.dot(
                gall_ref[owner], w_ref[pl.ds(start, width), at], preferred_element_type=F32
            )
            if not first:
                got = got + acc_ref[:, at]
            if last:
                out_ref[:, at] = got.astype(BF16)
            else:
                acc_ref[:, at] = got
            return carry

        lax.fori_loop(0, columns // wide, some, 0)

    project(0, True, chan == 1)
    exchange_wait(2)
    mix(False, 2)
    exchange_start(3)
    for off in range(1, chan):
        share(off).wait()
        project(off, False, off == chan - 1)

    exchange_wait(3)

    def grad_products(i, carry):
        at = cols(i)
        gp_ref[:, at] = from_recv(3, i).T.astype(BF16)
        return carry

    lax.fori_loop(0, tiles, grad_products, 0)
    tail_ref[0:2, :] = gqf_ref[:16, :].astype(F32)[:2]
    tail_ref[2:4, :] = gp_ref[:16, :].astype(F32)[:2]
    tail = halo(2, seq - 1, tail_ref, head_ref)
    tail.start()
    before_ref[0:6, :] = jnp.where(here > 0, hrecv_ref[0, 0:6, :], 0.0)
    after_ref[4:8, :] = hrecv_ref[1, 2:6, :]
    tail.wait()
    after_ref[0:4, :] = jnp.where(here < seq - 1, head_ref[...], 0.0)


def last_kernel(
    k_ref, v_ref, taps_ref, mixer_ref, gqf_ref, gp_ref, before_ref, after_ref,
    out_ref, gq_ref, gk_ref, gv_ref,
):
    count = k_ref.shape[0]
    gp = gp_ref[...].astype(F32)
    gqf_next = after_ref[0:2]
    gp_next = after_ref[2:4]

    def both(ref, m):
        x = ref[...].astype(F32)
        taps = taps_ref[3 * m : 3 * m + 3]
        new = after_ref[2 + 2 * m : 4 + 2 * m]
        near, far = x[count - 1 : count], x[count - 2 : count - 1]
        first = new[0:1] * taps[0:1] + near * taps[1:2] + far * taps[2:3]
        second = new[1:2] * taps[0:1] + new[0:1] * taps[1:2] + near * taps[2:3]
        inside = causal(x, before_ref[2 * m : 2 * m + 2], taps)
        return inside, jnp.concatenate([first, second], axis=0)

    kf, kf_next = both(k_ref, 1)
    vf, vf_next = both(v_ref, 2)
    out_ref[...] = mixer_ref[...]
    gq_ref[...] = anticausal(gqf_ref[...].astype(F32), gqf_next, taps_ref[0:3]).astype(BF16)
    gk_ref[...] = anticausal(
        rounded(gp * vf), rounded(gp_next * vf_next), taps_ref[3:6]
    ).astype(BF16)
    gv_ref[...] = anticausal(
        rounded(gp * kf), rounded(gp_next * kf_next), taps_ref[6:9]
    ).astype(BF16)


def local(query_proj, key_proj, value_proj, short_filter, long_filter, out_weight, grad_out):
    count, width = query_proj.shape
    seq = lax.axis_size("seq")
    chan = lax.axis_size("chan")
    per = width // seq
    gw = min(per, GROUP)
    groups = per // gw
    length = long_filter.shape[1]
    depth, columns = out_weight.shape

    taps = jnp.repeat(short_filter.transpose(0, 2, 1).reshape(9, -1), GROUP, axis=1)
    first = lax.axis_index("seq") * per // GROUP
    chosen = lax.dynamic_slice_in_dim(long_filter, first, groups, 0).astype(F32)

    vmem = pl.BlockSpec(memory_space=pltpu.VMEM)
    flat = jax.ShapeDtypeStruct((count, width), BF16)
    rims = jax.ShapeDtypeStruct((8, width), F32)
    mixer_out, grad_qf, grad_prod, before, after = pl.pallas_call(
        step_kernel,
        in_specs=[vmem] * 5 + [pl.BlockSpec(memory_space=pl.ANY), vmem],
        out_specs=[vmem] * 5,
        out_shape=[jax.ShapeDtypeStruct((count, columns), BF16), flat, flat, rims, rims],
        scratch_shapes=[
            pltpu.VMEM((depth, columns), BF16),
            pltpu.VMEM((columns, count), BF16),
            pltpu.VMEM((groups, length), F32),
            pltpu.VMEM((groups, length, count), BF16),
            pltpu.VMEM((4, seq, groups, gw, count), BF16),
            pltpu.VMEM((4, seq, groups, gw, count), BF16),
            pltpu.VMEM((chan - 1, width, count), BF16),
            pltpu.VMEM((chan, width, count), BF16),
            pltpu.VMEM((chan, count, width), BF16),
            pltpu.VMEM((count, columns), F32),
            pltpu.VMEM((2, 8, width), F32),
            pltpu.VMEM((2, 8, width), F32),
            pltpu.VMEM((4, width), F32),
            pltpu.VMEM((4, width), F32),
            pltpu.SemaphoreType.DMA((chan,)),
            pltpu.SemaphoreType.DMA((4, seq)),
            pltpu.SemaphoreType.DMA((4, seq)),
            pltpu.SemaphoreType.DMA((2, chan)),
            pltpu.SemaphoreType.DMA((2, chan)),
            pltpu.SemaphoreType.DMA((3,)),
            pltpu.SemaphoreType.DMA((3,)),
        ],
        compiler_params=pltpu.CompilerParams(
            collective_id=0, has_side_effects=True, vmem_limit_bytes=62 * 1024 * 1024
        ),
        name="step",
    )(query_proj, key_proj, value_proj, taps, chosen, out_weight, grad_out)

    tile = min(512, width)

    def tall(rows):
        return pl.BlockSpec((rows, tile), lambda i: (0, i))

    return pl.pallas_call(
        last_kernel,
        grid=(width // tile,),
        in_specs=[tall(count), tall(count), tall(9)] + [tall(count)] * 3 + [tall(8)] * 2,
        out_specs=[tall(count)] * 4,
        out_shape=[flat] * 4,
        compiler_params=pltpu.CompilerParams(vmem_limit_bytes=62 * 1024 * 1024),
        name="last",
    )(key_proj, value_proj, taps, mixer_out, grad_qf, grad_prod, before, after)


def flipped(x, flip):
    return jnp.dot(flip, x, preferred_element_type=F32)


def pair_kernel(
    q_hbm, k_hbm, v_hbm, taps_in, h_hbm, w_hbm, go_hbm,
    out_hbm, gq_hbm, gk_hbm, gv_hbm,
    w_ref, go_ref, x_ref, taps_ref, h_ref, filt_ref, hf_ref,
    filtered_ref, prod_ref, gm_ref, rf_ref, rb_ref, xt_ref, ot_ref, ms_ref, mixed_ref, gp_ref,
    total_ref, part_ref, sx_ref, sy_ref, rx_ref, ry_ref, ga_ref, acc_ref,
    gf_ref, head_ref, fin_ref, mo_send, mo_recv, mo_ref,
    w_sem, in_sem, send_sem, recv_sem, out_sem,
):
    here = lax.axis_index("seq")
    mine = lax.axis_index("chan")
    seq = lax.axis_size("seq")
    count = go_hbm.shape[0]
    width = q_hbm.shape[1]
    half = width // 2
    span = 2 * count
    nblk, _, bw = prod_ref.shape
    columns = go_hbm.shape[1]
    chips = seq // 2
    core = lax.rem(here, 2)
    other = 1 - core
    z = here // 2
    zo = z + 1 - 2 * lax.rem(z, 2)
    zq = lax.rem(z, 2)
    zh = z // 2
    bx = mine + 1 - 2 * lax.rem(mine, 2)
    by = lax.rem(mine + 2, 4)
    bd = lax.rem(bx + 2, 4)
    who_id = (mine, bx, by, bd)
    order = [
        [(3, c), (3, 2 + c), (1, c), (2, 2 + c), (0, c), (0, 2 + c), (1, 2 + c), (2, c)]
        for c in range(2)
    ]
    SIB = {"seq": 2 * z + other}
    X = {"chan": bx}
    Y = {"chan": by}
    groups = bw // GROUP
    length = h_ref.shape[1]

    def w_copy(c, j):
        who, blk = order[c][j]
        start = pl.multiple_of(who_id[who] * width + core * half + blk * bw, bw)
        return pltpu.make_async_copy(
            w_hbm.at[pl.ds(start, bw)], w_ref.at[c, j], w_sem.at[c, j]
        )

    def w_wait(c, j):
        pltpu.make_async_copy(w_hbm.at[pl.ds(0, bw)], w_ref.at[c, j], w_sem.at[c, j]).wait()

    mycols = pl.ds(pl.multiple_of(core * half, half), half)
    sibcols = pl.ds(pl.multiple_of(other * half, half), half)
    myrows = pl.ds(pl.multiple_of(core * count, count), count)
    sibrows = pl.ds(pl.multiple_of(other * count, count), count)
    slabrows = pl.ds(pl.multiple_of(16 + core * count, 16), count)

    ins = [pltpu.make_async_copy(go_hbm, go_ref.at[myrows], in_sem.at[0])]
    for m, src in enumerate((q_hbm, k_hbm, v_hbm)):
        ins.append(pltpu.make_async_copy(src.at[:, mycols], x_ref.at[m, slabrows], in_sem.at[1 + m]))
    first = pl.multiple_of(core * (half // GROUP) + zq * (half // GROUP // 2), 16)
    ins.append(pltpu.make_async_copy(h_hbm.at[pl.ds(first, 2 * groups)], h_ref, in_sem.at[4]))
    ins[0].start()
    w_copy(0, 0).start()
    w_copy(0, 1).start()
    for i in (2, 3, 1, 4):
        ins[i].start()
    for c in range(2):
        for j in range(8):
            if c or j > 1:
                w_copy(c, j).start()

    barrier = pltpu.get_barrier_semaphore()

    def greet(off, carry):
        pl.semaphore_signal(
            barrier, inc=1, device_id={"seq": lax.rem(here + off, seq)}, device_id_type=MESH
        )
        return carry

    lax.fori_loop(1, seq, greet, 0)
    for peer in (X, Y):
        pl.semaphore_signal(barrier, inc=1, device_id=peer, device_id_type=MESH)
    pl.semaphore_wait(barrier, seq + 1)

    def remote(src, dst, to, send, recv=None):
        return pltpu.make_async_remote_copy(
            src_ref=src, dst_ref=dst, send_sem=send_sem.at[send],
            recv_sem=recv_sem.at[send if recv is None else recv],
            device_id=to, device_id_type=MESH,
        )

    swaps = [remote(go_hbm, go_ref.at[myrows], SIB, 0)]
    for m, src in enumerate((q_hbm, k_hbm, v_hbm)):
        swaps.append(remote(src.at[:, sibcols], x_ref.at[m, slabrows], SIB, 1 + m))
    for i in (0, 2, 3, 1):
        swaps[i].start()

    def rim(m, to):
        src = (q_hbm, k_hbm, v_hbm)[m]
        at = pl.ds(pl.multiple_of(to * half, half), half)
        return remote(
            src.at[count - 16 : count, at], x_ref.at[m, 0:16],
            {"seq": 2 * lax.rem(z + 1, chips) + to}, 4 + 2 * m + to, 4 + 2 * m,
        )

    sends_rim = (core == 1) & (z < chips - 1)

    @pl.when(sends_rim)
    def _():
        for m in (1, 2, 0):
            for to in range(2):
                rim(m, to).start()

    @pl.when(z == 0)
    def _():
        x_ref[:, 0:16] = jnp.zeros((3, 16, half), BF16)

    def rim_wait(m):
        @pl.when(z > 0)
        def _():
            rim(m, 0).wait_recv()

    rows = [taps_in[m] for m in range(3)]
    taps9 = jnp.concatenate(rows + [jnp.zeros((7, taps_in.shape[2]), F32)], axis=0)
    shape = (taps_in.shape[2], bw)
    group_at = lax.broadcasted_iota(jnp.int32, shape, 0)
    chan_at = lax.broadcasted_iota(jnp.int32, shape, 1)
    for b in range(nblk):
        pick = group_at * GROUP - (core * half + b * bw)
        hot = jnp.where((chan_at >= pick) & (chan_at < pick + GROUP), 1.0, 0.0).astype(F32)
        taps_ref[b] = jnp.dot(taps9, hot, precision=lax.Precision.HIGHEST, preferred_element_type=F32)

    flip = (
        lax.broadcasted_iota(jnp.int32, (count, count), 0)
        + lax.broadcasted_iota(jnp.int32, (count, count), 1)
        == count - 1
    )
    flip = jnp.where(flip, 1.0, 0.0).astype(BF16)
    xt_ref[:, 0:3] = jnp.zeros((groups, 3, GROUP, count), BF16)

    def cx(c, i):
        return remote(sx_ref.at[c, i], rx_ref.at[c, i], X, 16 + c * 3 + i)

    def cy(c, i):
        return remote(sy_ref.at[c, i], ry_ref.at[c, i], Y, 22 + c * 3 + i)

    def sums(c, lo, hi):
        def one(p, carry):
            w_wait(c, 2 * p)
            w_wait(c, 2 * p + 1)
            part_ref[...] = lax.dot_general(
                go_ref[...], w_ref[c, pl.ds(2 * p, 2)].reshape(2 * bw, columns),
                (((1,), (1,)), ((), ())), preferred_element_type=F32,
            )

            def away():
                sx_ref[c, p] = part_ref[:, :bw].astype(BF16)
                cx(c, p).start()
                sy_ref[c, p] = part_ref[:, bw:].astype(BF16)
                cy(c, p).start()

            def own():
                total_ref[c] = part_ref[:, :bw]
                total_ref[2 + c] = part_ref[:, bw:]

            def joined():
                cy(c, 0).wait_recv()
                sx_ref[c, 2] = (part_ref[:, :bw] + ry_ref[c, 0].astype(F32)).astype(BF16)
                cx(c, 2).start()
                cx(c, 0).wait_recv()
                sy_ref[c, 2] = (part_ref[:, bw:] + rx_ref[c, 0].astype(F32)).astype(BF16)
                cy(c, 2).start()

            if lo < 2:
                pl.when(p < 2)(away)
            if lo <= 2 < hi:
                pl.when(p == 2)(own)
            if hi == 4:
                pl.when(p == 3)(joined)
            return carry

        lax.fori_loop(lo, hi, one, 0)

    def cols(b):
        return pl.ds(pl.multiple_of(b * bw, bw), bw)

    def filtering(m, b):
        x = x_ref[m, :, cols(b)].astype(F32)
        taps = taps_ref[b, 3 * m : 3 * m + 3]
        y = x * taps[0:1] + pltpu.roll(x, 1, 0) * taps[1:2] + pltpu.roll(x, 2, 0) * taps[2:3]
        filtered_ref[m, b] = y[16:]
        return y[16:]

    ZF, ZB, RF, RB = 32, 40, 48, 50

    def ok_fwd(src, dst):
        return dst // 2 >= src // 2

    def ok_bwd(src, dst):
        return dst // 2 <= src // 2

    def zcopy(base, src, dst, c, to, frm):
        return remote(
            src.at[2 * lax.rem(to, 2) + c], dst.at[frm, c], {"seq": 2 * to + core},
            base + 2 * to + c, base + 2 * frm + c,
        )

    def zeach(ok, act):
        for d in range(1, chips):
            peer = lax.rem(z + d, chips)
            pl.when(ok(peer))(lambda peer=peer: act(peer))

    def zsend(base, src, dst, c, ok):
        zeach(lambda p: ok(z, p), lambda p: zcopy(base, src, dst, c, p, z).start())
        dst[z, c] = src[2 * zq + c]

    def zwait(base, src, dst, c, ok):
        zeach(lambda p: ok(p, z), lambda p: zcopy(base, src, dst, c, z, p).wait_recv())

    def zdone(base, src, dst, c, ok):
        zeach(lambda p: ok(z, p), lambda p: zcopy(base, src, dst, c, p, z).wait_send())

    def ret(forward, c):
        dst = mixed_ref if forward else gp_ref
        base = RF if forward else RB
        i = 0 if forward else 1
        return remote(
            ms_ref.at[i, c, lax.rem(zo, 2)], dst.at[2 * zq + c], {"seq": 2 * zo + core}, base + c
        )

    def ret_wait(forward, c):
        dst = mixed_ref if forward else gp_ref
        base = RF if forward else RB
        i = 0 if forward else 1
        remote(
            ms_ref.at[i, c, 0], dst.at[2 * (1 - zq) + c], {"seq": 2 * zo + core}, base + c
        ).wait_recv()

    def several(lo, hi, together, one):
        def some(i, carry):
            for u in range(together):
                one(lo + i * together + u)
            return carry

        lax.fori_loop(0, (hi - lo) // together, some, 0)

    def build(lo, hi):
        def one(g):
            row = hf_ref[pl.ds(g, 1), :]
            lines = jnp.broadcast_to(row, (count, length))
            both = jnp.concatenate([jnp.zeros((count, count), F32), lines], axis=1)
            lined = pltpu.roll(both, 0, 1, stride=1, stride_axis=0).astype(BF16)
            for k in range(length // count):
                at = (k + 1) * count
                filt_ref[g, k * count : (k + 1) * count, :] = lined[:, at : at + count]

        several(lo, hi, 4, one)

    def mix(forward, c):
        src = rf_ref if forward else rb_ref
        late = (zh == 1) if forward else (zh == 0)
        lags = length // count
        outs = lags // 2

        def fill(chip, slot):
            for blk in range(2):
                x = src[chip, c, blk * count : (blk + 1) * count, :]
                if forward:
                    at, x = blk, x.astype(F32)
                else:
                    at, x = 1 - blk, flipped(x, flip)
                xt_ref[:, 3 + slot + at] = x.T.reshape(groups, GROUP, count).astype(BF16)

        for i in range(2):
            r = i if forward else 1 - i
            fill(2 * zh + r, outs + 2 * i)

        def run(depth):
            def one(g):
                pieces = [
                    xt_ref[g, 3 + outs - k : 3 + 2 * outs - k].reshape(outs * GROUP, count)
                    for k in range(depth)
                ]
                got = jnp.dot(
                    jnp.concatenate(pieces, axis=1),
                    filt_ref[groups * c + g, : depth * count],
                    preferred_element_type=F32,
                )
                ot_ref[:, g] = got.reshape(outs, GROUP, count)

            several(0, groups, 8, one)

        @pl.when(late)
        def _():
            for i in range(2):
                r = i if forward else 1 - i
                fill(2 * (1 - zh) + r, 2 * i)
            run(lags)

        @pl.when(jnp.logical_not(late))
        def _():
            xt_ref[:, 3 : 3 + outs] = jnp.zeros((groups, outs, GROUP, count), BF16)
            run(outs)

        i = 0 if forward else 1
        for b in range(outs):
            y = ot_ref[b].reshape(bw, count).T.astype(BF16)
            at = b
            if not forward:
                y = flipped(y, flip).astype(BF16)
                at = outs - 1 - b
            ms_ref[i, c, at // 2, (at % 2) * count : (at % 2 + 1) * count, :] = y
        ret(forward, c).start()
        dst = mixed_ref if forward else gp_ref
        dst[2 * zq + c] = ms_ref[i, c, zq]

    def sums_done(c):
        cx(c, 1).wait_recv()
        cy(c, 2).wait_recv()
        total_ref[c] += rx_ref[c, 1].astype(F32) + ry_ref[c, 2].astype(F32)
        gm_ref[c] = (total_ref[c] * filtered_ref[0, c]).astype(BF16)
        cy(c, 1).wait_recv()
        cx(c, 2).wait_recv()
        total_ref[2 + c] += ry_ref[c, 1].astype(F32) + rx_ref[c, 2].astype(F32)
        gm_ref[2 + c] = (total_ref[2 + c] * filtered_ref[0, 2 + c]).astype(BF16)
        zsend(ZB, gm_ref, rb_ref, c, ok_bwd)

    def ax(c, i):
        src, dst = ((4, 2), (5, 6), (3, 1))[i]
        return remote(ga_ref.at[c, src], ga_ref.at[c, dst], X, 52 + 3 * c + i)

    def ay(c, i):
        src, dst = ((5, 3), (4, 7), (2, 0))[i]
        return remote(ga_ref.at[c, src], ga_ref.at[c, dst], Y, 58 + 3 * c + i)

    def gate(c):
        ret_wait(True, c)
        for i, b in enumerate((c, 2 + c)):
            ga_ref[c, 4 + i] = (filtered_ref[0, b] * mixed_ref[b].astype(F32)).astype(BF16)
        for i in range(2):
            ax(c, i).start()
            ay(c, i).start()
        for b in (c, 2 + c):
            gf_ref[0, b] = (total_ref[b] * mixed_ref[b].astype(F32)).astype(BF16)

    def relay(c):
        ax(c, 0).wait_recv()
        ay(c, 2).start()
        ay(c, 0).wait_recv()
        ax(c, 2).start()

    def project(c, lo, hi, wide):
        def some(i, carry):
            at = pl.ds(pl.multiple_of(i * wide, wide), wide)
            got = jnp.dot(
                jnp.concatenate([ga_ref[c, j] for j in range(lo, hi)], axis=1),
                w_ref[c, lo:hi, :, at].reshape((hi - lo) * bw, wide),
                preferred_element_type=F32,
            )
            acc_ref[:, at] = acc_ref[:, at] + got if c else got
            return carry

        lax.fori_loop(0, columns // wide, some, 0)

    def heads(m):
        return remote(
            gf_ref.at[m, :, 0:16], head_ref.at[m],
            {"seq": 2 * lax.rem(z + chips - 1, chips) + core}, 64 + m,
        )

    def heads_start(m):
        @pl.when(z > 0)
        def _():
            heads(m).start()

    def finish(m, ref):
        @pl.when(z < chips - 1)
        def _():
            heads(m).wait_recv()

        for b in range(nblk):
            g = gf_ref[m, b].astype(F32)
            taps = taps_ref[b, 3 * m : 3 * m + 3]
            after = jnp.where(z < chips - 1, head_ref[m, b].astype(F32)[0:2], 0.0)
            fin_ref[m, :, b * bw : (b + 1) * bw] = anticausal(g, after, taps).astype(BF16)
        pltpu.make_async_copy(fin_ref.at[m, myrows], ref.at[:, mycols], out_sem.at[m]).start()
        remote(fin_ref.at[m, sibrows], ref.at[:, mycols], SIB, 67 + m).start()

    ins[0].wait()
    swaps[0].wait_recv()
    sums(0, 0, 1)
    for m in (1, 2):
        ins[1 + m].wait()
        swaps[1 + m].wait_recv()
        rim_wait(m)
    for b in (0, 2, 1, 3):
        prod_ref[b] = (filtering(1, b) * filtering(2, b)).astype(BF16)
        if b >= 2:
            zsend(ZF, prod_ref, rf_ref, b - 2, ok_fwd)
    sums(0, 1, 4)
    sums(1, 0, 3)
    ins[1].wait()
    swaps[1].wait_recv()
    rim_wait(0)
    for b in range(nblk):
        filtering(0, b)
    ins[4].wait()
    hf_ref[...] = h_ref[...].astype(F32)
    build(0, groups)
    sums_done(0)
    sums(1, 3, 4)
    build(groups, 2 * groups)
    zwait(ZF, prod_ref, rf_ref, 0, ok_fwd)
    mix(True, 0)
    sums_done(1)
    gate(0)
    relay(0)
    zwait(ZF, prod_ref, rf_ref, 1, ok_fwd)
    mix(True, 1)
    zwait(ZB, gm_ref, rb_ref, 0, ok_bwd)
    mix(False, 0)
    gate(1)
    heads_start(0)
    for make in (ax, ay):
        make(0, 1).wait_recv()
        make(0, 2).wait_recv()
    project(0, 0, 8, min(512, columns))
    finish(0, gq_hbm)
    relay(1)
    zwait(ZB, gm_ref, rb_ref, 1, ok_bwd)
    mix(False, 1)
    ax(1, 1).wait_recv()
    ay(1, 1).wait_recv()
    project(1, 2, 8, min(512, columns))
    for c in range(2):
        ret_wait(False, c)
    for b in range(nblk):
        gp = gp_ref[b].astype(F32)
        gf_ref[1, b] = (gp * filtered_ref[2, b]).astype(BF16)
        gf_ref[2, b] = (gp * filtered_ref[1, b]).astype(BF16)
    heads_start(1)
    heads_start(2)
    ax(1, 2).wait_recv()
    ay(1, 2).wait_recv()
    project(1, 0, 2, min(1024, columns))
    mo_send[...] = acc_ref[sibrows, :].astype(BF16)
    mo = remote(mo_send, mo_recv, SIB, 70)
    mo.start()
    finish(1, gk_hbm)
    finish(2, gv_hbm)
    mo.wait_recv()
    mo_ref[...] = (acc_ref[myrows, :] + mo_recv[...].astype(F32)).astype(BF16)
    pltpu.make_async_copy(mo_ref, out_hbm, out_sem.at[3]).start()

    for copy in swaps + [mo]:
        copy.wait_send()

    @pl.when(sends_rim)
    def _():
        for m in range(3):
            for to in range(2):
                rim(m, to).wait_send()

    for c in range(2):
        for i in range(3):
            for make in (cx, cy, ax, ay):
                make(c, i).wait_send()
        zdone(ZF, prod_ref, rf_ref, c, ok_fwd)
        zdone(ZB, gm_ref, rb_ref, c, ok_bwd)
        for forward in (True, False):
            ret(forward, c).wait_send()

    @pl.when(z > 0)
    def _():
        for m in range(3):
            heads(m).wait_send()

    for m, ref in enumerate((gq_hbm, gk_hbm, gv_hbm)):
        pltpu.make_async_copy(fin_ref.at[m, myrows], ref.at[:, mycols], out_sem.at[m]).wait()
        out = remote(fin_ref.at[m, sibrows], ref.at[:, mycols], SIB, 67 + m)
        out.wait_send()
        remote(fin_ref.at[m, sibrows], ref.at[:, sibcols], SIB, 67 + m).wait_recv()
    pltpu.make_async_copy(mo_ref, out_hbm, out_sem.at[3]).wait()


def copy_kernel(*refs):
    for src, dst in zip(refs[:4], refs[4:]):
        dst[...] = src[...]


def paired(query_proj, key_proj, value_proj, short_filter, long_filter, out_weight, grad_out):
    count, width = query_proj.shape
    length = long_filter.shape[1]
    columns = out_weight.shape[1]
    half = width // 2
    span = 2 * count
    bw = half // 4
    groups = bw // GROUP
    lags = length // count

    vmem = pl.BlockSpec(memory_space=pltpu.VMEM)
    hbm = pl.BlockSpec(memory_space=pl.ANY)
    flat = jax.ShapeDtypeStruct((count, width), BF16)
    block = (span, bw)
    results = pl.pallas_call(
        pair_kernel,
        in_specs=[hbm] * 3 + [vmem] + [hbm] * 3,
        out_specs=[hbm] * 4,
        out_shape=[flat] * 4,
        scratch_shapes=[
            pltpu.VMEM((2, 8, bw, columns), BF16),
            pltpu.VMEM((span, columns), BF16),
            pltpu.VMEM((3, 16 + span, half), BF16),
            pltpu.VMEM((4, 16, bw), F32),
            pltpu.VMEM((2 * groups, length), BF16),
            pltpu.VMEM((2 * groups, length, count), BF16),
            pltpu.VMEM((2 * groups, length), F32),
            pltpu.VMEM((3, 4) + block, F32),
            pltpu.VMEM((4,) + block, BF16),
            pltpu.VMEM((4,) + block, BF16),
            pltpu.VMEM((4, 2) + block, BF16),
            pltpu.VMEM((4, 2) + block, BF16),
            pltpu.VMEM((groups, 3 + lags, GROUP, count), BF16),
            pltpu.VMEM((lags // 2, groups, GROUP, count), F32),
            pltpu.VMEM((2, 2, 2) + block, BF16),
            pltpu.VMEM((4,) + block, BF16),
            pltpu.VMEM((4,) + block, BF16),
            pltpu.VMEM((4,) + block, F32),
            pltpu.VMEM((span, 2 * bw), F32),
            pltpu.VMEM((2, 3) + block, BF16),
            pltpu.VMEM((2, 3) + block, BF16),
            pltpu.VMEM((2, 3) + block, BF16),
            pltpu.VMEM((2, 3) + block, BF16),
            pltpu.VMEM((2, 8) + block, BF16),
            pltpu.VMEM((span, columns), F32),
            pltpu.VMEM((3, 4) + block, BF16),
            pltpu.VMEM((3, 4, 16, bw), BF16),
            pltpu.VMEM((3, span, half), BF16),
            pltpu.VMEM((count, columns), BF16),
            pltpu.VMEM((count, columns), BF16),
            pltpu.VMEM((count, columns), BF16),
            pltpu.SemaphoreType.DMA((2, 8)),
            pltpu.SemaphoreType.DMA((5,)),
            pltpu.SemaphoreType.DMA((72,)),
            pltpu.SemaphoreType.DMA((72,)),
            pltpu.SemaphoreType.DMA((4,)),
        ],
        compiler_params=pltpu.CompilerParams(
            collective_id=0, has_side_effects=True, vmem_limit_bytes=62 * 1024 * 1024
        ),
        name="step",
    )(
        query_proj, key_proj, value_proj, short_filter.transpose(0, 2, 1),
        long_filter, out_weight, grad_out,
    )
    return pl.pallas_call(
        copy_kernel,
        in_specs=[vmem] * 4,
        out_specs=[vmem] * 4,
        out_shape=[flat] * 4,
        compiler_params=pltpu.CompilerParams(vmem_limit_bytes=32 * 1024 * 1024),
        name="last",
    )(*results)


def either(query_proj, key_proj, value_proj, short_filter, long_filter, out_weight, grad_out):
    args = (query_proj, key_proj, value_proj, short_filter, long_filter, out_weight, grad_out)
    count, width = query_proj.shape
    fits = (
        lax.axis_size("seq") == 8
        and lax.axis_size("chan") == 4
        and count % 128 == 0
        and width % 2048 == 0
        and long_filter.shape[1] == 8 * count
    )
    return paired(*args) if fits else local(*args)


def solution(mesh):
    return jax.shard_map(
        either,
        mesh=mesh,
        in_specs=(
            P("seq", "chan"),
            P("seq", "chan"),
            P("seq", "chan"),
            P(None, "chan", None),
            P("chan", None),
            P(None, "chan"),
            P("seq", "chan"),
        ),
        out_specs=(P("seq", "chan"), P("seq", "chan"), P("seq", "chan"), P("seq", "chan")),
        check_vma=False,
    )
```

```python
import jax
import jax.numpy as jnp
from jax import lax
from jax.experimental import pallas as pl
from jax.experimental.pallas import tpu as pltpu
from jax.sharding import PartitionSpec as P

GROUP = 16
F32 = jnp.float32
BF16 = jnp.bfloat16
MESH = pl.DeviceIdType.MESH


def causal(x, before, taps):
    row = lax.broadcasted_iota(jnp.int32, x.shape, 0)
    one = jnp.where(row == 0, before[1:2], pltpu.roll(x, 1, 0))
    two = jnp.where(row == 0, before[0:1], jnp.where(row == 1, before[1:2], pltpu.roll(x, 2, 0)))
    return x * taps[0:1] + one * taps[1:2] + two * taps[2:3]


def anticausal(g, after, taps):
    count = g.shape[0]
    row = lax.broadcasted_iota(jnp.int32, g.shape, 0)
    one = jnp.where(row == count - 1, after[0:1], pltpu.roll(g, count - 1, 0))
    two = jnp.where(
        row == count - 1,
        after[1:2],
        jnp.where(row == count - 2, after[0:1], pltpu.roll(g, count - 2, 0)),
    )
    return g * taps[0:1] + one * taps[1:2] + two * taps[2:3]


def rounded(x):
    return x.astype(BF16).astype(F32)


def step_kernel(
    q_ref, k_ref, v_ref, taps_ref, h_ref, w_hbm, go_ref,
    out_ref, gqf_ref, gp_ref, before_ref, after_ref,
    w_ref, got_ref, hr_ref, filt_ref, send_refs, recv_refs, part_send, part_recv, gall_ref,
    acc_ref, hsend_ref, hrecv_ref, tail_ref, head_ref,
    w_sem, seq_send, seq_recv, chan_send, chan_recv, halo_send, halo_recv,
):
    seq = lax.axis_size("seq")
    chan = lax.axis_size("chan")
    here = lax.axis_index("seq")
    mine = lax.axis_index("chan")
    count, width = q_ref.shape
    _, groups, gw, _ = recv_refs.shape[1:]
    per = groups * gw
    length = h_ref.shape[1]
    columns = go_ref.shape[1]
    tile = max(per, min(256, width))
    tiles = width // tile
    dests = tile // per
    rows = min(512, width)
    wide = min(512, columns)

    def seq_peer(off):
        return lax.rem(here + off, seq)

    def chan_peer(off):
        return lax.rem(mine + off, chan)

    def w_copy(off):
        at = pl.ds(pl.multiple_of(chan_peer(off) * width, width), width)
        return pltpu.make_async_copy(w_hbm.at[at], w_ref.at[at], w_sem.at[off])

    order = [off % chan for off in range(1, chan + 1)]
    for off in order:
        w_copy(off).start()

    barrier = pltpu.get_barrier_semaphore()

    def greet_seq(off, carry):
        pl.semaphore_signal(
            barrier, inc=1, device_id={"seq": seq_peer(off)}, device_id_type=MESH
        )
        return carry

    def greet_chan(off, carry):
        pl.semaphore_signal(
            barrier, inc=1, device_id={"chan": chan_peer(off)}, device_id_type=MESH
        )
        return carry

    lax.fori_loop(1, seq, greet_seq, 0)
    lax.fori_loop(1, chan, greet_chan, 0)

    for m, ref in enumerate((q_ref, k_ref, v_ref)):
        hsend_ref[0, 2 * m : 2 * m + 2, :] = ref[count - 16 :, :].astype(F32)[14:]
        hsend_ref[1, 2 * m : 2 * m + 2, :] = ref[:16, :].astype(F32)[:2]
    pl.semaphore_wait(barrier, seq + chan - 2)

    def halo(slot, by, src, dst):
        return pltpu.make_async_remote_copy(
            src_ref=src, dst_ref=dst, send_sem=halo_send.at[slot], recv_sem=halo_recv.at[slot],
            device_id={"seq": seq_peer(by)}, device_id_type=MESH,
        )

    halo_down = halo(0, 1, hsend_ref.at[0, 0:6], hrecv_ref.at[0, 0:6])
    halo_up = halo(1, seq - 1, hsend_ref.at[1, 0:6], hrecv_ref.at[1, 0:6])
    halo_down.start()
    halo_up.start()

    def turn(i, carry):
        at = pl.ds(pl.multiple_of(i * wide, wide), wide)
        got_ref[at, :] = go_ref[:, at].astype(F32).T.astype(BF16)
        return carry

    lax.fori_loop(0, columns // wide, turn, 0)

    def exchange(slot, off):
        return pltpu.make_async_remote_copy(
            src_ref=send_refs.at[slot, seq_peer(off)],
            dst_ref=recv_refs.at[slot, here],
            send_sem=seq_send.at[slot, off],
            recv_sem=seq_recv.at[slot, off],
            device_id={"seq": seq_peer(off)},
            device_id_type=MESH,
        )

    def exchange_start(slot):
        def go(off, carry):
            exchange(slot, off).start()
            return carry

        lax.fori_loop(1, seq, go, 0)
        recv_refs[slot, pl.ds(here, 1)] = send_refs[slot, pl.ds(here, 1)]

    def exchange_wait(slot):
        def go(off, carry):
            exchange(slot, off).wait()
            return carry

        lax.fori_loop(1, seq, go, 0)

    def to_send(slot, i, turned):
        send_refs[slot, pl.ds(i * dests, dests)] = turned.reshape(
            dests, groups, gw, count
        ).astype(BF16)

    def from_recv(slot, i):
        return recv_refs[slot, pl.ds(i * dests, dests)].astype(F32).reshape(tile, count)

    def cols(i):
        return pl.ds(pl.multiple_of(i * tile, tile), tile)

    def filtered(ref, m, at):
        ahead = jnp.where(here > 0, hrecv_ref[0, 2 * m : 2 * m + 2, at], 0.0)
        return causal(ref[:, at].astype(F32), ahead, taps_ref[3 * m : 3 * m + 3, at])

    halo_down.wait()
    halo_up.wait()

    def spread(slot, make):
        def one(i, carry):
            to_send(slot, i, make(cols(i)))
            return carry

        def off_to(off, carry):
            one(seq_peer(off), 0)
            exchange(slot, off).start()
            return carry

        if dests == 1:
            lax.fori_loop(1, seq, off_to, 0)
            one(here, 0)
            recv_refs[slot, pl.ds(here, 1)] = send_refs[slot, pl.ds(here, 1)]
        else:
            lax.fori_loop(0, tiles, one, 0)
            exchange_start(slot)

    spread(0, lambda at: (filtered(k_ref, 1, at) * filtered(v_ref, 2, at)).T)

    def part(off):
        return pltpu.make_async_remote_copy(
            src_ref=part_send.at[off - 1],
            dst_ref=part_recv.at[mine],
            send_sem=chan_send.at[0, off],
            recv_sem=chan_recv.at[0, off],
            device_id={"chan": chan_peer(off)},
            device_id_type=MESH,
        )

    def back_project(off):
        w_copy(off).wait()

        def some(i, carry):
            start = pl.multiple_of(chan_peer(off) * width + i * rows, rows)
            got = jnp.dot(w_ref[pl.ds(start, rows), :], got_ref[...], preferred_element_type=F32)
            at = pl.ds(pl.multiple_of(i * rows, rows), rows)
            if off:
                part_send[off - 1, at, :] = got.astype(BF16)
            else:
                part_recv[mine, at, :] = got.astype(BF16)
            return carry

        lax.fori_loop(0, width // rows, some, 0)
        if off:
            part(off).start()

    for off in range(1, chan):
        back_project(off)

    flip = (
        lax.broadcasted_iota(jnp.int32, (count, count), 0)
        + lax.broadcasted_iota(jnp.int32, (count, count), 1)
        == count - 1
    )
    flip = jnp.where(flip, 1.0, 0.0).astype(BF16)
    for k in range(length // count):
        hr_ref[:, length - (k + 1) * count : length - k * count] = jnp.dot(
            h_ref[:, k * count : (k + 1) * count].astype(BF16), flip, preferred_element_type=F32
        )

    def build(forward):
        def one(g, carry):
            pad = jnp.zeros((count, count), F32)
            row = (h_ref if forward else hr_ref)[pl.ds(g, 1), :]
            lines = jnp.broadcast_to(row, (count, length))
            pair = [pad, lines] if forward else [lines, pad]
            lined = pltpu.roll(
                jnp.concatenate(pair, axis=1), 0 if forward else 1, 1, stride=1, stride_axis=0
            ).astype(BF16)
            for k in range(length // count):
                at = (k + 1) * count if forward else length - k * count
                filt_ref[g, k * count : (k + 1) * count, :] = lined[:, at : at + count]
            return carry

        lax.fori_loop(0, groups, one, 0)

    def mix(forward, slot):
        total_rows = seq * gw

        def one(g, carry):
            x = recv_refs[slot, :, g]
            kind = F32 if gw % 16 else BF16
            x = x.astype(kind).reshape(total_rows, count)
            pieces = [x.astype(BF16)]
            for k in range(1, seq):
                pad = jnp.zeros((k * gw, count), kind)
                if forward:
                    moved = jnp.concatenate([pad, x[: total_rows - k * gw]], axis=0)
                else:
                    moved = jnp.concatenate([x[k * gw :], pad], axis=0)
                pieces.append(moved.astype(BF16))
            total = jnp.dot(
                jnp.concatenate(pieces, axis=1), filt_ref[g], preferred_element_type=F32
            )
            send_refs[slot + 1, :, g] = total.reshape(seq, gw, count).astype(BF16)
            return carry

        lax.fori_loop(0, groups, one, 0)

    build(True)
    exchange_wait(0)
    mix(True, 0)
    exchange_start(1)
    back_project(0)
    build(False)

    for off in range(1, chan):
        part(off).wait()

    def summed(at):
        return jnp.sum(part_recv[:, at, :].astype(F32), axis=0)

    spread(2, lambda at: summed(at) * filtered(q_ref, 0, at).T)

    def share(off):
        return pltpu.make_async_remote_copy(
            src_ref=gall_ref.at[mine],
            dst_ref=gall_ref.at[mine],
            send_sem=chan_send.at[1, off],
            recv_sem=chan_recv.at[1, off],
            device_id={"chan": chan_peer(off)},
            device_id_type=MESH,
        )

    exchange_wait(1)

    def gate(i, carry):
        at = cols(i)
        gall_ref[mine, :, at] = (filtered(q_ref, 0, at) * from_recv(1, i).T).astype(BF16)
        return carry

    lax.fori_loop(0, tiles, gate, 0)
    for off in range(1, chan):
        share(off).start()

    def grad_query(i, carry):
        at = cols(i)
        gqf_ref[:, at] = (summed(at) * from_recv(1, i)).T.astype(BF16)
        return carry

    lax.fori_loop(0, tiles, grad_query, 0)

    def project(off, first, last):
        owner = chan_peer(chan - off)

        def some(i, carry):
            at = pl.ds(pl.multiple_of(i * wide, wide), wide)
            start = pl.multiple_of(owner * width, width)
            got = jnp.dot(
                gall_ref[owner], w_ref[pl.ds(start, width), at], preferred_element_type=F32
            )
            if not first:
                got = got + acc_ref[:, at]
            if last:
                out_ref[:, at] = got.astype(BF16)
            else:
                acc_ref[:, at] = got
            return carry

        lax.fori_loop(0, columns // wide, some, 0)

    project(0, True, chan == 1)
    exchange_wait(2)
    mix(False, 2)
    exchange_start(3)
    for off in range(1, chan):
        share(off).wait()
        project(off, False, off == chan - 1)

    exchange_wait(3)

    def grad_products(i, carry):
        at = cols(i)
        gp_ref[:, at] = from_recv(3, i).T.astype(BF16)
        return carry

    lax.fori_loop(0, tiles, grad_products, 0)
    tail_ref[0:2, :] = gqf_ref[:16, :].astype(F32)[:2]
    tail_ref[2:4, :] = gp_ref[:16, :].astype(F32)[:2]
    tail = halo(2, seq - 1, tail_ref, head_ref)
    tail.start()
    before_ref[0:6, :] = jnp.where(here > 0, hrecv_ref[0, 0:6, :], 0.0)
    after_ref[4:8, :] = hrecv_ref[1, 2:6, :]
    tail.wait()
    after_ref[0:4, :] = jnp.where(here < seq - 1, head_ref[...], 0.0)


def last_kernel(
    k_ref, v_ref, taps_ref, mixer_ref, gqf_ref, gp_ref, before_ref, after_ref,
    out_ref, gq_ref, gk_ref, gv_ref,
):
    count = k_ref.shape[0]
    gp = gp_ref[...].astype(F32)
    gqf_next = after_ref[0:2]
    gp_next = after_ref[2:4]

    def both(ref, m):
        x = ref[...].astype(F32)
        taps = taps_ref[3 * m : 3 * m + 3]
        new = after_ref[2 + 2 * m : 4 + 2 * m]
        near, far = x[count - 1 : count], x[count - 2 : count - 1]
        first = new[0:1] * taps[0:1] + near * taps[1:2] + far * taps[2:3]
        second = new[1:2] * taps[0:1] + new[0:1] * taps[1:2] + near * taps[2:3]
        inside = causal(x, before_ref[2 * m : 2 * m + 2], taps)
        return inside, jnp.concatenate([first, second], axis=0)

    kf, kf_next = both(k_ref, 1)
    vf, vf_next = both(v_ref, 2)
    out_ref[...] = mixer_ref[...]
    gq_ref[...] = anticausal(gqf_ref[...].astype(F32), gqf_next, taps_ref[0:3]).astype(BF16)
    gk_ref[...] = anticausal(
        rounded(gp * vf), rounded(gp_next * vf_next), taps_ref[3:6]
    ).astype(BF16)
    gv_ref[...] = anticausal(
        rounded(gp * kf), rounded(gp_next * kf_next), taps_ref[6:9]
    ).astype(BF16)


def local(query_proj, key_proj, value_proj, short_filter, long_filter, out_weight, grad_out):
    count, width = query_proj.shape
    seq = lax.axis_size("seq")
    chan = lax.axis_size("chan")
    per = width // seq
    gw = min(per, GROUP)
    groups = per // gw
    length = long_filter.shape[1]
    depth, columns = out_weight.shape

    taps = jnp.repeat(short_filter.transpose(0, 2, 1).reshape(9, -1), GROUP, axis=1)
    first = lax.axis_index("seq") * per // GROUP
    chosen = lax.dynamic_slice_in_dim(long_filter, first, groups, 0).astype(F32)

    vmem = pl.BlockSpec(memory_space=pltpu.VMEM)
    flat = jax.ShapeDtypeStruct((count, width), BF16)
    rims = jax.ShapeDtypeStruct((8, width), F32)
    mixer_out, grad_qf, grad_prod, before, after = pl.pallas_call(
        step_kernel,
        in_specs=[vmem] * 5 + [pl.BlockSpec(memory_space=pl.ANY), vmem],
        out_specs=[vmem] * 5,
        out_shape=[jax.ShapeDtypeStruct((count, columns), BF16), flat, flat, rims, rims],
        scratch_shapes=[
            pltpu.VMEM((depth, columns), BF16),
            pltpu.VMEM((columns, count), BF16),
            pltpu.VMEM((groups, length), F32),
            pltpu.VMEM((groups, length, count), BF16),
            pltpu.VMEM((4, seq, groups, gw, count), BF16),
            pltpu.VMEM((4, seq, groups, gw, count), BF16),
            pltpu.VMEM((chan - 1, width, count), BF16),
            pltpu.VMEM((chan, width, count), BF16),
            pltpu.VMEM((chan, count, width), BF16),
            pltpu.VMEM((count, columns), F32),
            pltpu.VMEM((2, 8, width), F32),
            pltpu.VMEM((2, 8, width), F32),
            pltpu.VMEM((4, width), F32),
            pltpu.VMEM((4, width), F32),
            pltpu.SemaphoreType.DMA((chan,)),
            pltpu.SemaphoreType.DMA((4, seq)),
            pltpu.SemaphoreType.DMA((4, seq)),
            pltpu.SemaphoreType.DMA((2, chan)),
            pltpu.SemaphoreType.DMA((2, chan)),
            pltpu.SemaphoreType.DMA((3,)),
            pltpu.SemaphoreType.DMA((3,)),
        ],
        compiler_params=pltpu.CompilerParams(
            collective_id=0, has_side_effects=True, vmem_limit_bytes=62 * 1024 * 1024
        ),
        name="step",
    )(query_proj, key_proj, value_proj, taps, chosen, out_weight, grad_out)

    tile = min(512, width)

    def tall(rows):
        return pl.BlockSpec((rows, tile), lambda i: (0, i))

    return pl.pallas_call(
        last_kernel,
        grid=(width // tile,),
        in_specs=[tall(count), tall(count), tall(9)] + [tall(count)] * 3 + [tall(8)] * 2,
        out_specs=[tall(count)] * 4,
        out_shape=[flat] * 4,
        compiler_params=pltpu.CompilerParams(vmem_limit_bytes=62 * 1024 * 1024),
        name="last",
    )(key_proj, value_proj, taps, mixer_out, grad_qf, grad_prod, before, after)


def flipped(x, flip):
    return jnp.dot(flip, x, preferred_element_type=F32)


def pair_kernel(
    q_hbm, k_hbm, v_hbm, taps_in, h_hbm, w_hbm, go_hbm,
    out_hbm, gq_hbm, gk_hbm, gv_hbm,
    w_ref, go_ref, x_ref, taps_ref, h_ref, filt_ref, near_ref, hf_ref,
    filtered_ref, prod_ref, gm_ref, rf_ref, rb_ref, ff_ref, fb_ref, xt_ref, ot_ref, ms_ref, mixed_ref, gp_ref,
    total_ref, join_ref, sx_ref, sy_ref, rx_ref, ry_ref, ga_ref, acc_ref,
    gf_ref, head_ref, fin_ref, mo_send, mo_recv, mo_ref,
    w_sem, in_sem, send_sem, recv_sem, out_sem,
):
    here = lax.axis_index("seq")
    mine = lax.axis_index("chan")
    seq = lax.axis_size("seq")
    count = go_hbm.shape[0]
    width = q_hbm.shape[1]
    half = width // 2
    span = 2 * count
    nblk, _, bw = prod_ref.shape
    parts = nblk // 2
    wb = w_ref.shape[2]
    columns = go_hbm.shape[1]
    chips = seq // 2
    core = lax.rem(here, 2)
    other = 1 - core
    z = here // 2
    zo = z + 1 - 2 * lax.rem(z, 2)
    zq = lax.rem(z, 2)
    zh = z // 2
    bx = mine + 1 - 2 * lax.rem(mine, 2)
    by = lax.rem(mine + 2, 4)
    bd = lax.rem(bx + 2, 4)
    who_id = (mine, bx, by, bd)
    order = [
        [(3, c), (3, 2 + c), (1, c), (2, 2 + c), (0, c), (0, 2 + c), (1, 2 + c), (2, c)]
        for c in range(2)
    ]
    SIB = {"seq": 2 * z + other}
    X = {"chan": bx}
    Y = {"chan": by}
    groups = bw // GROUP
    length = h_ref.shape[2]
    lags = length // count
    outs = lags // 2

    def w_copy(c, j):
        who, blk = order[c][j]
        start = pl.multiple_of(who_id[who] * width + core * half + blk * wb, wb)
        return pltpu.make_async_copy(w_hbm.at[pl.ds(start, wb)], w_ref.at[c, j], w_sem.at[c, j])

    def w_wait(c, j):
        pltpu.make_async_copy(w_hbm.at[pl.ds(0, wb)], w_ref.at[c, j], w_sem.at[c, j]).wait()

    mycols = pl.ds(pl.multiple_of(core * half, half), half)
    sibcols = pl.ds(pl.multiple_of(other * half, half), half)
    myrows = pl.ds(pl.multiple_of(core * count, count), count)
    sibrows = pl.ds(pl.multiple_of(other * count, count), count)
    slabrows = pl.ds(pl.multiple_of(16 + core * count, 16), count)

    ins = [pltpu.make_async_copy(go_hbm, go_ref.at[myrows], in_sem.at[0])]
    for m, src in enumerate((q_hbm, k_hbm, v_hbm)):
        ins.append(pltpu.make_async_copy(src.at[:, mycols], x_ref.at[m, slabrows], in_sem.at[1 + m]))
    for i, side in enumerate((zq, 1 - zq)):
        first = pl.multiple_of(core * (half // GROUP) + side * (half // GROUP // 2), 16)
        ins.append(pltpu.make_async_copy(
            h_hbm.at[pl.ds(first, parts * groups)], h_ref.at[i], in_sem.at[4 + i]
        ))
    ins[0].start()
    w_copy(0, 0).start()
    w_copy(0, 1).start()
    for i in (2, 3, 1, 4, 5):
        ins[i].start()
    for c in range(2):
        for j in range(8):
            if c or j > 1:
                w_copy(c, j).start()

    barrier = pltpu.get_barrier_semaphore()

    def greet(off, carry):
        pl.semaphore_signal(
            barrier, inc=1, device_id={"seq": lax.rem(here + off, seq)}, device_id_type=MESH
        )
        return carry

    lax.fori_loop(1, seq, greet, 0)
    for peer in (X, Y):
        pl.semaphore_signal(barrier, inc=1, device_id=peer, device_id_type=MESH)

    @pl.when(z == 0)
    def _():
        x_ref[:, 0:16] = jnp.zeros((3, 16, half), BF16)

    rows = [taps_in[m] for m in range(3)]
    taps9 = jnp.concatenate(rows + [jnp.zeros((7, taps_in.shape[2]), F32)], axis=0)
    shape = (taps_in.shape[2], half)
    pick = lax.broadcasted_iota(jnp.int32, shape, 0) * GROUP - core * half
    chan_at = lax.broadcasted_iota(jnp.int32, shape, 1)
    hot = jnp.where((chan_at >= pick) & (chan_at < pick + GROUP), 1.0, 0.0).astype(F32)
    wide_taps = jnp.dot(taps9, hot, precision=lax.Precision.HIGHEST, preferred_element_type=F32)
    for b in range(nblk):
        taps_ref[b] = wide_taps[:, b * bw : (b + 1) * bw]
    flip = (
        lax.broadcasted_iota(jnp.int32, (count, count), 0)
        + lax.broadcasted_iota(jnp.int32, (count, count), 1)
        == count - 1
    )
    flip = jnp.where(flip, 1.0, 0.0).astype(BF16)
    xt_ref[:, 0:3] = jnp.zeros((groups, 3, GROUP, count), BF16)
    pl.semaphore_wait(barrier, seq + 1)

    def remote(src, dst, to, send, recv=None):
        return pltpu.make_async_remote_copy(
            src_ref=src, dst_ref=dst, send_sem=send_sem.at[send],
            recv_sem=recv_sem.at[send if recv is None else recv],
            device_id=to, device_id_type=MESH,
        )

    swaps = [remote(go_hbm, go_ref.at[myrows], SIB, 0)]
    for m, src in enumerate((q_hbm, k_hbm, v_hbm)):
        swaps.append(remote(src.at[:, sibcols], x_ref.at[m, slabrows], SIB, 1 + m))

    def rim(m, to):
        src = (q_hbm, k_hbm, v_hbm)[m]
        at = pl.ds(pl.multiple_of(to * half, half), half)
        return remote(
            src.at[count - 16 : count, at], x_ref.at[m, 0:16],
            {"seq": 2 * lax.rem(z + 1, chips) + to}, 4 + 2 * m + to, 4 + 2 * m,
        )

    sends_rim = (core == 1) & (z < chips - 1)
    swaps[0].start()

    @pl.when(sends_rim)
    def _():
        for m in (1, 2, 0):
            for to in range(2):
                rim(m, to).start()

    for i in (2, 3, 1):
        swaps[i].start()

    def rim_wait(m):
        @pl.when(z > 0)
        def _():
            rim(m, 0).wait_recv()

    def cx(k, i):
        return remote(sx_ref.at[k, i], rx_ref.at[k, i], X, 96 + k * 3 + i)

    def cy(k, i):
        return remote(sy_ref.at[k, i], ry_ref.at[k, i], Y, 108 + k * 3 + i)

    def sums(c, lo, hi):
        def one(p, carry):
            w_wait(c, 2 * p)
            w_wait(c, 2 * p + 1)
            got = lax.dot_general(
                go_ref[...], w_ref[c, pl.ds(2 * p, 2)].reshape(2 * wb, columns),
                (((1,), (1,)), ((), ())), preferred_element_type=F32,
            )
            join_ref[c] = got

            def cut(side, s):
                return join_ref[c, :, side * wb + s * bw : side * wb + (s + 1) * bw]

            def away():
                for s in range(2):
                    sx_ref[2 * c + s, p] = cut(0, s).astype(BF16)
                    sy_ref[2 * c + s, p] = cut(1, s).astype(BF16)

            def own():
                for s in range(2):
                    total_ref[2 * c + s] = cut(0, s)
                    total_ref[parts + 2 * c + s] = cut(1, s)

            if lo < 2:
                pl.when(p < 2)(away)
            if lo <= 2 < hi:
                pl.when(p == 2)(own)
            return carry

        lax.fori_loop(lo, hi, one, 0)

    def sums_send(k, i):
        cx(k, i).start()
        cy(k, i).start()

    def sums_joined(k):
        c, s = k // 2, k % 2
        cy(k, 0).wait_recv()
        mine_x = join_ref[c, :, s * bw : (s + 1) * bw]
        sx_ref[k, 2] = (mine_x + ry_ref[k, 0].astype(F32)).astype(BF16)
        cx(k, 2).start()
        cx(k, 0).wait_recv()
        mine_y = join_ref[c, :, wb + s * bw : wb + (s + 1) * bw]
        sy_ref[k, 2] = (mine_y + rx_ref[k, 0].astype(F32)).astype(BF16)
        cy(k, 2).start()

    def cols(b):
        return pl.ds(pl.multiple_of(b * bw, bw), bw)

    def filtering(m, b):
        x = x_ref[m, :, cols(b)].astype(F32)
        taps = taps_ref[b, 3 * m : 3 * m + 3]
        y = x * taps[0:1] + pltpu.roll(x, 1, 0) * taps[1:2] + pltpu.roll(x, 2, 0) * taps[2:3]
        filtered_ref[m, b] = y[16:]
        return y[16:]

    def way(forward):
        if forward:
            return (0, 1, zh == 1, prod_ref, rf_ref, ff_ref, mixed_ref, 0)
        return (chips - 1, chips - 2, zh == 0, gm_ref, rb_ref, fb_ref, gp_ref, 1)

    ZS, ZR, ZP, ZQ = (32, 136), (48, 152), (64, 72), (128, 132)

    def to_late(forward, src, k, owner, to, relayed=False):
        _, _, _, _, dst, _, _, i = way(forward)
        return remote(
            src, dst.at[owner, k], {"seq": 2 * to + core},
            (ZR if relayed else ZS)[i] + 4 * to + k, ZS[i] + 4 * owner + k,
        )

    def late_chip(forward, side):
        return side + (2 if forward else 0)

    def to_second(forward, k, side):
        head, second, _, src, _, keep, _, i = way(forward)
        return remote(
            src.at[parts * side + k], keep.at[side, k], {"seq": 2 * second + core},
            ZP[i] + 4 * side + k,
        )

    def zeach(forward, k, act):
        head, second, late, src, dst, keep, _, _ = way(forward)

        @pl.when(z == head)
        def _():
            for side in range(2):
                act(to_second(forward, k, side))

        @pl.when(z == second)
        def _():
            for side in range(2):
                act(to_late(forward, src.at[parts * side + k], k, z, late_chip(forward, side)))

        @pl.when(late)
        def _():
            act(to_late(forward, src.at[parts * (1 - zq) + k], k, z, zo))

    def zsend(forward, k):
        zeach(forward, k, lambda copy: copy.start())

    def zpass(forward, k, side):
        head, _, _, _, _, keep, _, _ = way(forward)
        return to_late(forward, keep.at[side, k], k, head, late_chip(forward, side), True)

    def zrelay(forward, k):
        @pl.when(z == way(forward)[1])
        def _():
            for side in range(2):
                to_second(forward, k, side).wait_recv()
                zpass(forward, k, side).start()

    def zdone(forward, k):
        zeach(forward, k, lambda copy: copy.wait_send())

        @pl.when(z == way(forward)[1])
        def _():
            for side in range(2):
                zpass(forward, k, side).wait_send()

        @pl.when(way(forward)[2])
        def _():
            ret(forward, k).wait_send()

    def ret(forward, k):
        _, _, _, _, _, _, dst, i = way(forward)
        return remote(
            ms_ref.at[i, k, lax.rem(zo, 2)], dst.at[parts * zq + k], {"seq": 2 * zo + core}, ZQ[i] + k
        )

    def ret_wait(forward, k):
        _, _, late, _, _, _, dst, i = way(forward)

        @pl.when(late)
        def _():
            remote(
                ms_ref.at[i, k, 0], dst.at[parts * (1 - zq) + k], {"seq": 2 * zo + core}, ZQ[i] + k
            ).wait_recv()

    def several(lo, hi, together, one):
        def some(i, carry):
            for u in range(together):
                one(lo + i * together + u)
            return carry

        lax.fori_loop(0, (hi - lo) // together, some, 0)

    def build(lo, hi):
        def one(g, side, depth):
            row = hf_ref[side, pl.ds(g, 1), : depth * count]
            lines = jnp.broadcast_to(row, (count, depth * count))
            both = jnp.concatenate([jnp.zeros((count, count), F32), lines], axis=1)
            lined = pltpu.roll(both, 0, 1, stride=1, stride_axis=0).astype(BF16)
            for k in range(depth):
                at = (k + 1) * count
                to = (filt_ref, near_ref)[side]
                to[g, k * count : (k + 1) * count, :] = lined[:, at : at + count]

        several(lo, hi, 4, lambda g: one(g, 0, lags))
        several(lo, hi, 4, lambda g: one(g, 1, outs))

    def mix(forward, k):
        head, second, late, sent, src, keep, dst, way_at = way(forward)

        def fill(x2, slot):
            for blk in range(2):
                x = x2[blk * count : (blk + 1) * count]
                if forward:
                    at, x = blk, x.astype(F32)
                else:
                    at, x = 1 - blk, flipped(x, flip)
                xt_ref[:, 3 + slot + at] = x.T.reshape(groups, GROUP, count).astype(BF16)

        def run(filt, top, tall, depth):
            for g in range(groups):
                pieces = [
                    xt_ref[g, top - j : top - j + tall].reshape(tall * GROUP, count)
                    for j in range(depth)
                ]
                got = jnp.dot(
                    jnp.concatenate(pieces, axis=1),
                    filt[groups * k + g, : depth * count],
                    preferred_element_type=F32,
                )
                ot_ref[0:tall, g] = got.reshape(tall, GROUP, count)

        def turned(b, tall):
            y = ot_ref[b].reshape(bw, count).T.astype(BF16)
            if forward:
                return b, y
            return tall - 1 - b, flipped(y, flip).astype(BF16)

        @pl.when(late)
        def _():
            for d in range(1, chips):
                p = lax.rem(z + d, chips)
                to_late(forward, sent.at[0], k, p, z).wait_recv()
            for i in range(4):
                near = i >= 2
                r = i % 2 if forward else 1 - i % 2
                chip = 2 * zh + r if near else 2 * (1 - zh) + r
                if near:
                    own = zq == r
                    pl.when(own)(lambda i=i: fill(sent[parts * zq + k], 2 * i))
                    pl.when(jnp.logical_not(own))(lambda i=i, chip=chip: fill(src[chip, k], 2 * i))
                else:
                    fill(src[chip, k], 2 * i)
            run(filt_ref, 3 + outs, outs, lags)
            for b in range(outs):
                at, y = turned(b, outs)
                ms_ref[way_at, k, at // 2, (at % 2) * count : (at % 2 + 1) * count, :] = y
            ret(forward, k).start()
            dst[parts * zq + k] = ms_ref[way_at, k, zq]

        @pl.when(jnp.logical_not(late))
        def _():
            for i in range(2):
                side = zq if i == 0 else 1 - zq
                fill(sent[parts * side + k], 2)

                @pl.when(z == second)
                def _():
                    fill(keep[side, k], 0)

                @pl.when(z == head)
                def _():
                    xt_ref[:, 3:5] = jnp.zeros((groups, 2, GROUP, count), BF16)

                run((filt_ref, near_ref)[i], 5, 2, outs)
                for b in range(2):
                    at, y = turned(b, 2)
                    dst[parts * side + k, at * count : (at + 1) * count, :] = y

    def sums_done(k):
        cx(k, 1).wait_recv()
        cy(k, 2).wait_recv()
        a, b = k, parts + k
        total_ref[a] += rx_ref[k, 1].astype(F32) + ry_ref[k, 2].astype(F32)
        gm_ref[a] = (total_ref[a] * filtered_ref[0, a]).astype(BF16)
        cy(k, 1).wait_recv()
        cx(k, 2).wait_recv()
        total_ref[b] += ry_ref[k, 1].astype(F32) + rx_ref[k, 2].astype(F32)
        gm_ref[b] = (total_ref[b] * filtered_ref[0, b]).astype(BF16)
        zsend(False, k)

    def gat(k, j):
        s = k % 2
        return ga_ref.at[k // 2, j, :, s * bw : (s + 1) * bw]

    def ax(k, i):
        src, dst = ((4, 2), (5, 6), (3, 1))[i]
        return remote(gat(k, src), gat(k, dst), X, 168 + 3 * k + i)

    def ay(k, i):
        src, dst = ((5, 3), (4, 7), (2, 0))[i]
        return remote(gat(k, src), gat(k, dst), Y, 180 + 3 * k + i)

    def gate(k):
        ret_wait(True, k)
        for j, b in enumerate((k, parts + k)):
            s = k % 2
            ga_ref[k // 2, 4 + j, :, s * bw : (s + 1) * bw] = (
                filtered_ref[0, b] * mixed_ref[b].astype(F32)
            ).astype(BF16)
        for i in range(2):
            ax(k, i).start()
            ay(k, i).start()
        for b in (k, parts + k):
            gf_ref[0, b] = (total_ref[b] * mixed_ref[b].astype(F32)).astype(BF16)

    def relay(k):
        ax(k, 0).wait_recv()
        ay(k, 2).start()
        ay(k, 0).wait_recv()
        ax(k, 2).start()

    def gathered(k, i):
        ax(k, i).wait_recv()
        ay(k, i).wait_recv()

    def project(c, lo, hi, wide):
        def some(i, carry):
            at = pl.ds(pl.multiple_of(i * wide, wide), wide)
            got = jnp.dot(
                jnp.concatenate([ga_ref[c, j] for j in range(lo, hi)], axis=1),
                w_ref[c, lo:hi, :, at].reshape((hi - lo) * wb, wide),
                preferred_element_type=F32,
            )
            acc_ref[:, at] = acc_ref[:, at] + got if c else got
            return carry

        lax.fori_loop(0, columns // wide, some, 0)

    def heads(m):
        return remote(
            gf_ref.at[m, :, 0:16], head_ref.at[m],
            {"seq": 2 * lax.rem(z + chips - 1, chips) + core}, 120 + m,
        )

    def heads_start(m):
        @pl.when(z > 0)
        def _():
            heads(m).start()

    def finish(m, ref):
        @pl.when(z < chips - 1)
        def _():
            heads(m).wait_recv()

        def one(b, carry):
            g = gf_ref[m, b].astype(F32)
            taps = taps_ref[b, 3 * m : 3 * m + 3]
            after = jnp.where(z < chips - 1, head_ref[m, b].astype(F32)[0:2], 0.0)
            fin_ref[m, :, cols(b)] = anticausal(g, after, taps).astype(BF16)
            return carry

        lax.fori_loop(0, nblk, one, 0)
        pltpu.make_async_copy(fin_ref.at[m, myrows], ref.at[:, mycols], out_sem.at[m]).start()
        remote(fin_ref.at[m, sibrows], ref.at[:, mycols], SIB, 123 + m).start()

    def grads(k):
        ret_wait(False, k)
        for b in (k, parts + k):
            gp = gp_ref[b].astype(F32)
            gf_ref[1, b] = (gp * filtered_ref[2, b]).astype(BF16)
            gf_ref[2, b] = (gp * filtered_ref[1, b]).astype(BF16)

    ins[0].wait()
    swaps[0].wait_recv()
    sums(0, 0, 1)
    sums_send(0, 0)
    for m in (1, 2):
        ins[1 + m].wait()
        swaps[1 + m].wait_recv()
        rim_wait(m)

    def multiply(k, carry):
        for b in (k, parts + k):
            prod_ref[b] = (filtering(1, b) * filtering(2, b)).astype(BF16)
        zsend(True, k)
        return carry

    lax.fori_loop(0, parts, multiply, 0)
    sums(0, 1, 4)
    sums_send(0, 1)
    sums_joined(0)
    sums_send(1, 0)
    sums_send(1, 1)
    zrelay(True, 0)
    sums(1, 0, 4)
    zrelay(True, 1)
    ins[1].wait()
    swaps[1].wait_recv()
    rim_wait(0)

    def query(b, carry):
        filtering(0, b)
        return carry

    lax.fori_loop(0, nblk, query, 0)
    sums_done(0)
    sums_joined(1)
    sums_send(2, 0)
    sums_send(2, 1)
    zrelay(True, 2)
    ins[4].wait()
    ins[5].wait()
    hf_ref[...] = h_ref[...].astype(F32)
    build(0, 2 * groups)
    zrelay(False, 0)
    sums_done(1)
    mix(True, 0)
    sums_joined(2)
    sums_send(3, 0)
    sums_send(3, 1)
    zrelay(True, 3)
    zrelay(False, 1)
    sums_done(2)
    mix(False, 0)
    sums_joined(3)
    mix(True, 1)
    gate(0)
    build(2 * groups, 4 * groups)
    zrelay(False, 2)
    sums_done(3)
    mix(True, 2)
    gate(1)
    relay(0)
    mix(False, 1)
    zrelay(False, 3)
    gate(2)
    mix(False, 2)
    relay(1)
    mix(True, 3)
    mix(False, 3)
    relay(2)
    gate(3)
    heads_start(0)
    for k in range(2):
        gathered(k, 1)
        gathered(k, 2)
    project(0, 0, 8, min(512, columns))
    relay(3)
    for k in range(4):
        grads(k)
    heads_start(1)
    heads_start(2)
    finish(0, gq_hbm)
    gathered(2, 1)
    gathered(3, 1)
    project(1, 2, 8, min(512, columns))
    finish(1, gk_hbm)
    finish(2, gv_hbm)
    gathered(2, 2)
    gathered(3, 2)
    project(1, 0, 2, min(1024, columns))
    mo_send[...] = acc_ref[sibrows, :].astype(BF16)
    mo = remote(mo_send, mo_recv, SIB, 126)
    mo.start()
    mo.wait_recv()
    mo_ref[...] = (acc_ref[myrows, :] + mo_recv[...].astype(F32)).astype(BF16)
    pltpu.make_async_copy(mo_ref, out_hbm, out_sem.at[3]).start()

    for copy in swaps + [mo]:
        copy.wait_send()

    @pl.when(sends_rim)
    def _():
        for m in range(3):
            for to in range(2):
                rim(m, to).wait_send()

    for k in range(parts):
        for i in range(3):
            for make in (cx, cy, ax, ay):
                make(k, i).wait_send()
        for forward in (True, False):
            zdone(forward, k)

    @pl.when(z > 0)
    def _():
        for m in range(3):
            heads(m).wait_send()

    for m, ref in enumerate((gq_hbm, gk_hbm, gv_hbm)):
        pltpu.make_async_copy(fin_ref.at[m, myrows], ref.at[:, mycols], out_sem.at[m]).wait()
        remote(fin_ref.at[m, sibrows], ref.at[:, mycols], SIB, 123 + m).wait_send()
        remote(fin_ref.at[m, sibrows], ref.at[:, sibcols], SIB, 123 + m).wait_recv()
    pltpu.make_async_copy(mo_ref, out_hbm, out_sem.at[3]).wait()


def copy_kernel(*refs):
    srcs, dsts, held, sem_in, sem_out = refs[:4], refs[4:8], *refs[8:]
    into = [pltpu.make_async_copy(src, held.at[i], sem_in.at[i]) for i, src in enumerate(srcs)]
    out = [pltpu.make_async_copy(held.at[i], dst, sem_out.at[i]) for i, dst in enumerate(dsts)]
    for copy in into:
        copy.start()
    for i in range(4):
        into[i].wait()
        out[i].start()
    for copy in out:
        copy.wait()


def paired(query_proj, key_proj, value_proj, short_filter, long_filter, out_weight, grad_out):
    count, width = query_proj.shape
    length = long_filter.shape[1]
    columns = out_weight.shape[1]
    half = width // 2
    span = 2 * count
    bw = half // 8
    groups = bw // GROUP
    lags = length // count

    vmem = pl.BlockSpec(memory_space=pltpu.VMEM)
    hbm = pl.BlockSpec(memory_space=pl.ANY)
    flat = jax.ShapeDtypeStruct((count, width), BF16)
    block = (span, bw)
    results = pl.pallas_call(
        pair_kernel,
        in_specs=[hbm] * 3 + [vmem] + [hbm] * 3,
        out_specs=[hbm] * 4,
        out_shape=[flat] * 4,
        scratch_shapes=[
            pltpu.VMEM((2, 8, 2 * bw, columns), BF16),
            pltpu.VMEM((span, columns), BF16),
            pltpu.VMEM((3, 16 + span, half), BF16),
            pltpu.VMEM((8, 16, bw), F32),
            pltpu.VMEM((2, 4 * groups, length), BF16),
            pltpu.VMEM((4 * groups, length, count), BF16),
            pltpu.VMEM((4 * groups, length // 2, count), BF16),
            pltpu.VMEM((2, 4 * groups, length), F32),
            pltpu.VMEM((3, 8) + block, F32),
            pltpu.VMEM((8,) + block, BF16),
            pltpu.VMEM((8,) + block, BF16),
            pltpu.VMEM((4, 4) + block, BF16),
            pltpu.VMEM((4, 4) + block, BF16),
            pltpu.VMEM((2, 4) + block, BF16),
            pltpu.VMEM((2, 4) + block, BF16),
            pltpu.VMEM((groups, 3 + lags, GROUP, count), BF16),
            pltpu.VMEM((lags // 2, groups, GROUP, count), F32),
            pltpu.VMEM((2, 4, 2) + block, BF16),
            pltpu.VMEM((8,) + block, BF16),
            pltpu.VMEM((8,) + block, BF16),
            pltpu.VMEM((8,) + block, F32),
            pltpu.VMEM((2, span, 4 * bw), F32),
            pltpu.VMEM((4, 3) + block, BF16),
            pltpu.VMEM((4, 3) + block, BF16),
            pltpu.VMEM((4, 3) + block, BF16),
            pltpu.VMEM((4, 3) + block, BF16),
            pltpu.VMEM((2, 8, span, 2 * bw), BF16),
            pltpu.VMEM((span, columns), F32),
            pltpu.VMEM((3, 8) + block, BF16),
            pltpu.VMEM((3, 8, 16, bw), BF16),
            pltpu.VMEM((3, span, half), BF16),
            pltpu.VMEM((count, columns), BF16),
            pltpu.VMEM((count, columns), BF16),
            pltpu.VMEM((count, columns), BF16),
            pltpu.SemaphoreType.DMA((2, 8)),
            pltpu.SemaphoreType.DMA((6,)),
            pltpu.SemaphoreType.DMA((192,)),
            pltpu.SemaphoreType.DMA((192,)),
            pltpu.SemaphoreType.DMA((4,)),
        ],
        compiler_params=pltpu.CompilerParams(
            collective_id=0, has_side_effects=True, vmem_limit_bytes=62 * 1024 * 1024
        ),
        name="step",
    )(
        query_proj, key_proj, value_proj, short_filter.transpose(0, 2, 1),
        long_filter, out_weight, grad_out,
    )
    return pl.pallas_call(
        copy_kernel,
        in_specs=[hbm] * 4,
        out_specs=[hbm] * 4,
        out_shape=[flat] * 4,
        scratch_shapes=[
            pltpu.VMEM((4, count, width), BF16),
            pltpu.SemaphoreType.DMA((4,)),
            pltpu.SemaphoreType.DMA((4,)),
        ],
        compiler_params=pltpu.CompilerParams(vmem_limit_bytes=62 * 1024 * 1024),
        name="last",
    )(*results)


def either(query_proj, key_proj, value_proj, short_filter, long_filter, out_weight, grad_out):
    args = (query_proj, key_proj, value_proj, short_filter, long_filter, out_weight, grad_out)
    count, width = query_proj.shape
    fits = (
        lax.axis_size("seq") == 8
        and lax.axis_size("chan") == 4
        and count % 128 == 0
        and width % 2048 == 0
        and long_filter.shape[1] == 8 * count
    )
    return paired(*args) if fits else local(*args)


def solution(mesh):
    return jax.shard_map(
        either,
        mesh=mesh,
        in_specs=(
            P("seq", "chan"),
            P("seq", "chan"),
            P("seq", "chan"),
            P(None, "chan", None),
            P("chan", None),
            P(None, "chan"),
            P("seq", "chan"),
        ),
        out_specs=(P("seq", "chan"), P("seq", "chan"), P("seq", "chan"), P("seq", "chan")),
        check_vma=False,
    )
```

```python
import jax
import jax.numpy as jnp
from jax import lax
from jax.experimental import pallas as pl
from jax.experimental.pallas import tpu as pltpu
from jax.sharding import PartitionSpec as P

GROUP = 16
F32 = jnp.float32
BF16 = jnp.bfloat16
MESH = pl.DeviceIdType.MESH


def causal(x, before, taps):
    row = lax.broadcasted_iota(jnp.int32, x.shape, 0)
    one = jnp.where(row == 0, before[1:2], pltpu.roll(x, 1, 0))
    two = jnp.where(row == 0, before[0:1], jnp.where(row == 1, before[1:2], pltpu.roll(x, 2, 0)))
    return x * taps[0:1] + one * taps[1:2] + two * taps[2:3]


def anticausal(g, after, taps):
    count = g.shape[0]
    row = lax.broadcasted_iota(jnp.int32, g.shape, 0)
    one = jnp.where(row == count - 1, after[0:1], pltpu.roll(g, count - 1, 0))
    two = jnp.where(
        row == count - 1,
        after[1:2],
        jnp.where(row == count - 2, after[0:1], pltpu.roll(g, count - 2, 0)),
    )
    return g * taps[0:1] + one * taps[1:2] + two * taps[2:3]


def rounded(x):
    return x.astype(BF16).astype(F32)


def step_kernel(
    q_ref, k_ref, v_ref, taps_ref, h_ref, w_hbm, go_ref,
    out_ref, gqf_ref, gp_ref, before_ref, after_ref,
    w_ref, got_ref, hr_ref, filt_ref, send_refs, recv_refs, part_send, part_recv, gall_ref,
    acc_ref, hsend_ref, hrecv_ref, tail_ref, head_ref,
    w_sem, seq_send, seq_recv, chan_send, chan_recv, halo_send, halo_recv,
):
    seq = lax.axis_size("seq")
    chan = lax.axis_size("chan")
    here = lax.axis_index("seq")
    mine = lax.axis_index("chan")
    count, width = q_ref.shape
    _, groups, gw, _ = recv_refs.shape[1:]
    per = groups * gw
    length = h_ref.shape[1]
    columns = go_ref.shape[1]
    tile = max(per, min(256, width))
    tiles = width // tile
    dests = tile // per
    rows = min(512, width)
    wide = min(512, columns)

    def seq_peer(off):
        return lax.rem(here + off, seq)

    def chan_peer(off):
        return lax.rem(mine + off, chan)

    def w_copy(off):
        at = pl.ds(pl.multiple_of(chan_peer(off) * width, width), width)
        return pltpu.make_async_copy(w_hbm.at[at], w_ref.at[at], w_sem.at[off])

    order = [off % chan for off in range(1, chan + 1)]
    for off in order:
        w_copy(off).start()

    barrier = pltpu.get_barrier_semaphore()

    def greet_seq(off, carry):
        pl.semaphore_signal(
            barrier, inc=1, device_id={"seq": seq_peer(off)}, device_id_type=MESH
        )
        return carry

    def greet_chan(off, carry):
        pl.semaphore_signal(
            barrier, inc=1, device_id={"chan": chan_peer(off)}, device_id_type=MESH
        )
        return carry

    lax.fori_loop(1, seq, greet_seq, 0)
    lax.fori_loop(1, chan, greet_chan, 0)

    for m, ref in enumerate((q_ref, k_ref, v_ref)):
        hsend_ref[0, 2 * m : 2 * m + 2, :] = ref[count - 16 :, :].astype(F32)[14:]
        hsend_ref[1, 2 * m : 2 * m + 2, :] = ref[:16, :].astype(F32)[:2]
    pl.semaphore_wait(barrier, seq + chan - 2)

    def halo(slot, by, src, dst):
        return pltpu.make_async_remote_copy(
            src_ref=src, dst_ref=dst, send_sem=halo_send.at[slot], recv_sem=halo_recv.at[slot],
            device_id={"seq": seq_peer(by)}, device_id_type=MESH,
        )

    halo_down = halo(0, 1, hsend_ref.at[0, 0:6], hrecv_ref.at[0, 0:6])
    halo_up = halo(1, seq - 1, hsend_ref.at[1, 0:6], hrecv_ref.at[1, 0:6])
    halo_down.start()
    halo_up.start()

    def turn(i, carry):
        at = pl.ds(pl.multiple_of(i * wide, wide), wide)
        got_ref[at, :] = go_ref[:, at].astype(F32).T.astype(BF16)
        return carry

    lax.fori_loop(0, columns // wide, turn, 0)

    def exchange(slot, off):
        return pltpu.make_async_remote_copy(
            src_ref=send_refs.at[slot, seq_peer(off)],
            dst_ref=recv_refs.at[slot, here],
            send_sem=seq_send.at[slot, off],
            recv_sem=seq_recv.at[slot, off],
            device_id={"seq": seq_peer(off)},
            device_id_type=MESH,
        )

    def exchange_start(slot):
        def go(off, carry):
            exchange(slot, off).start()
            return carry

        lax.fori_loop(1, seq, go, 0)
        recv_refs[slot, pl.ds(here, 1)] = send_refs[slot, pl.ds(here, 1)]

    def exchange_wait(slot):
        def go(off, carry):
            exchange(slot, off).wait()
            return carry

        lax.fori_loop(1, seq, go, 0)

    def to_send(slot, i, turned):
        send_refs[slot, pl.ds(i * dests, dests)] = turned.reshape(
            dests, groups, gw, count
        ).astype(BF16)

    def from_recv(slot, i):
        return recv_refs[slot, pl.ds(i * dests, dests)].astype(F32).reshape(tile, count)

    def cols(i):
        return pl.ds(pl.multiple_of(i * tile, tile), tile)

    def filtered(ref, m, at):
        ahead = jnp.where(here > 0, hrecv_ref[0, 2 * m : 2 * m + 2, at], 0.0)
        return causal(ref[:, at].astype(F32), ahead, taps_ref[3 * m : 3 * m + 3, at])

    halo_down.wait()
    halo_up.wait()

    def spread(slot, make):
        def one(i, carry):
            to_send(slot, i, make(cols(i)))
            return carry

        def off_to(off, carry):
            one(seq_peer(off), 0)
            exchange(slot, off).start()
            return carry

        if dests == 1:
            lax.fori_loop(1, seq, off_to, 0)
            one(here, 0)
            recv_refs[slot, pl.ds(here, 1)] = send_refs[slot, pl.ds(here, 1)]
        else:
            lax.fori_loop(0, tiles, one, 0)
            exchange_start(slot)

    spread(0, lambda at: (filtered(k_ref, 1, at) * filtered(v_ref, 2, at)).T)

    def part(off):
        return pltpu.make_async_remote_copy(
            src_ref=part_send.at[off - 1],
            dst_ref=part_recv.at[mine],
            send_sem=chan_send.at[0, off],
            recv_sem=chan_recv.at[0, off],
            device_id={"chan": chan_peer(off)},
            device_id_type=MESH,
        )

    def back_project(off):
        w_copy(off).wait()

        def some(i, carry):
            start = pl.multiple_of(chan_peer(off) * width + i * rows, rows)
            got = jnp.dot(w_ref[pl.ds(start, rows), :], got_ref[...], preferred_element_type=F32)
            at = pl.ds(pl.multiple_of(i * rows, rows), rows)
            if off:
                part_send[off - 1, at, :] = got.astype(BF16)
            else:
                part_recv[mine, at, :] = got.astype(BF16)
            return carry

        lax.fori_loop(0, width // rows, some, 0)
        if off:
            part(off).start()

    for off in range(1, chan):
        back_project(off)

    flip = (
        lax.broadcasted_iota(jnp.int32, (count, count), 0)
        + lax.broadcasted_iota(jnp.int32, (count, count), 1)
        == count - 1
    )
    flip = jnp.where(flip, 1.0, 0.0).astype(BF16)
    for k in range(length // count):
        hr_ref[:, length - (k + 1) * count : length - k * count] = jnp.dot(
            h_ref[:, k * count : (k + 1) * count].astype(BF16), flip, preferred_element_type=F32
        )

    def build(forward):
        def one(g, carry):
            pad = jnp.zeros((count, count), F32)
            row = (h_ref if forward else hr_ref)[pl.ds(g, 1), :]
            lines = jnp.broadcast_to(row, (count, length))
            pair = [pad, lines] if forward else [lines, pad]
            lined = pltpu.roll(
                jnp.concatenate(pair, axis=1), 0 if forward else 1, 1, stride=1, stride_axis=0
            ).astype(BF16)
            for k in range(length // count):
                at = (k + 1) * count if forward else length - k * count
                filt_ref[g, k * count : (k + 1) * count, :] = lined[:, at : at + count]
            return carry

        lax.fori_loop(0, groups, one, 0)

    def mix(forward, slot):
        total_rows = seq * gw

        def one(g, carry):
            x = recv_refs[slot, :, g]
            kind = F32 if gw % 16 else BF16
            x = x.astype(kind).reshape(total_rows, count)
            pieces = [x.astype(BF16)]
            for k in range(1, seq):
                pad = jnp.zeros((k * gw, count), kind)
                if forward:
                    moved = jnp.concatenate([pad, x[: total_rows - k * gw]], axis=0)
                else:
                    moved = jnp.concatenate([x[k * gw :], pad], axis=0)
                pieces.append(moved.astype(BF16))
            total = jnp.dot(
                jnp.concatenate(pieces, axis=1), filt_ref[g], preferred_element_type=F32
            )
            send_refs[slot + 1, :, g] = total.reshape(seq, gw, count).astype(BF16)
            return carry

        lax.fori_loop(0, groups, one, 0)

    build(True)
    exchange_wait(0)
    mix(True, 0)
    exchange_start(1)
    back_project(0)
    build(False)

    for off in range(1, chan):
        part(off).wait()

    def summed(at):
        return jnp.sum(part_recv[:, at, :].astype(F32), axis=0)

    spread(2, lambda at: summed(at) * filtered(q_ref, 0, at).T)

    def share(off):
        return pltpu.make_async_remote_copy(
            src_ref=gall_ref.at[mine],
            dst_ref=gall_ref.at[mine],
            send_sem=chan_send.at[1, off],
            recv_sem=chan_recv.at[1, off],
            device_id={"chan": chan_peer(off)},
            device_id_type=MESH,
        )

    exchange_wait(1)

    def gate(i, carry):
        at = cols(i)
        gall_ref[mine, :, at] = (filtered(q_ref, 0, at) * from_recv(1, i).T).astype(BF16)
        return carry

    lax.fori_loop(0, tiles, gate, 0)
    for off in range(1, chan):
        share(off).start()

    def grad_query(i, carry):
        at = cols(i)
        gqf_ref[:, at] = (summed(at) * from_recv(1, i)).T.astype(BF16)
        return carry

    lax.fori_loop(0, tiles, grad_query, 0)

    def project(off, first, last):
        owner = chan_peer(chan - off)

        def some(i, carry):
            at = pl.ds(pl.multiple_of(i * wide, wide), wide)
            start = pl.multiple_of(owner * width, width)
            got = jnp.dot(
                gall_ref[owner], w_ref[pl.ds(start, width), at], preferred_element_type=F32
            )
            if not first:
                got = got + acc_ref[:, at]
            if last:
                out_ref[:, at] = got.astype(BF16)
            else:
                acc_ref[:, at] = got
            return carry

        lax.fori_loop(0, columns // wide, some, 0)

    project(0, True, chan == 1)
    exchange_wait(2)
    mix(False, 2)
    exchange_start(3)
    for off in range(1, chan):
        share(off).wait()
        project(off, False, off == chan - 1)

    exchange_wait(3)

    def grad_products(i, carry):
        at = cols(i)
        gp_ref[:, at] = from_recv(3, i).T.astype(BF16)
        return carry

    lax.fori_loop(0, tiles, grad_products, 0)
    tail_ref[0:2, :] = gqf_ref[:16, :].astype(F32)[:2]
    tail_ref[2:4, :] = gp_ref[:16, :].astype(F32)[:2]
    tail = halo(2, seq - 1, tail_ref, head_ref)
    tail.start()
    before_ref[0:6, :] = jnp.where(here > 0, hrecv_ref[0, 0:6, :], 0.0)
    after_ref[4:8, :] = hrecv_ref[1, 2:6, :]
    tail.wait()
    after_ref[0:4, :] = jnp.where(here < seq - 1, head_ref[...], 0.0)


def last_kernel(
    k_ref, v_ref, taps_ref, mixer_ref, gqf_ref, gp_ref, before_ref, after_ref,
    out_ref, gq_ref, gk_ref, gv_ref,
):
    count = k_ref.shape[0]
    gp = gp_ref[...].astype(F32)
    gqf_next = after_ref[0:2]
    gp_next = after_ref[2:4]

    def both(ref, m):
        x = ref[...].astype(F32)
        taps = taps_ref[3 * m : 3 * m + 3]
        new = after_ref[2 + 2 * m : 4 + 2 * m]
        near, far = x[count - 1 : count], x[count - 2 : count - 1]
        first = new[0:1] * taps[0:1] + near * taps[1:2] + far * taps[2:3]
        second = new[1:2] * taps[0:1] + new[0:1] * taps[1:2] + near * taps[2:3]
        inside = causal(x, before_ref[2 * m : 2 * m + 2], taps)
        return inside, jnp.concatenate([first, second], axis=0)

    kf, kf_next = both(k_ref, 1)
    vf, vf_next = both(v_ref, 2)
    out_ref[...] = mixer_ref[...]
    gq_ref[...] = anticausal(gqf_ref[...].astype(F32), gqf_next, taps_ref[0:3]).astype(BF16)
    gk_ref[...] = anticausal(
        rounded(gp * vf), rounded(gp_next * vf_next), taps_ref[3:6]
    ).astype(BF16)
    gv_ref[...] = anticausal(
        rounded(gp * kf), rounded(gp_next * kf_next), taps_ref[6:9]
    ).astype(BF16)


def local(query_proj, key_proj, value_proj, short_filter, long_filter, out_weight, grad_out):
    count, width = query_proj.shape
    seq = lax.axis_size("seq")
    chan = lax.axis_size("chan")
    per = width // seq
    gw = min(per, GROUP)
    groups = per // gw
    length = long_filter.shape[1]
    depth, columns = out_weight.shape

    taps = jnp.repeat(short_filter.transpose(0, 2, 1).reshape(9, -1), GROUP, axis=1)
    first = lax.axis_index("seq") * per // GROUP
    chosen = lax.dynamic_slice_in_dim(long_filter, first, groups, 0).astype(F32)

    vmem = pl.BlockSpec(memory_space=pltpu.VMEM)
    flat = jax.ShapeDtypeStruct((count, width), BF16)
    rims = jax.ShapeDtypeStruct((8, width), F32)
    mixer_out, grad_qf, grad_prod, before, after = pl.pallas_call(
        step_kernel,
        in_specs=[vmem] * 5 + [pl.BlockSpec(memory_space=pl.ANY), vmem],
        out_specs=[vmem] * 5,
        out_shape=[jax.ShapeDtypeStruct((count, columns), BF16), flat, flat, rims, rims],
        scratch_shapes=[
            pltpu.VMEM((depth, columns), BF16),
            pltpu.VMEM((columns, count), BF16),
            pltpu.VMEM((groups, length), F32),
            pltpu.VMEM((groups, length, count), BF16),
            pltpu.VMEM((4, seq, groups, gw, count), BF16),
            pltpu.VMEM((4, seq, groups, gw, count), BF16),
            pltpu.VMEM((chan - 1, width, count), BF16),
            pltpu.VMEM((chan, width, count), BF16),
            pltpu.VMEM((chan, count, width), BF16),
            pltpu.VMEM((count, columns), F32),
            pltpu.VMEM((2, 8, width), F32),
            pltpu.VMEM((2, 8, width), F32),
            pltpu.VMEM((4, width), F32),
            pltpu.VMEM((4, width), F32),
            pltpu.SemaphoreType.DMA((chan,)),
            pltpu.SemaphoreType.DMA((4, seq)),
            pltpu.SemaphoreType.DMA((4, seq)),
            pltpu.SemaphoreType.DMA((2, chan)),
            pltpu.SemaphoreType.DMA((2, chan)),
            pltpu.SemaphoreType.DMA((3,)),
            pltpu.SemaphoreType.DMA((3,)),
        ],
        compiler_params=pltpu.CompilerParams(
            collective_id=0, has_side_effects=True, vmem_limit_bytes=62 * 1024 * 1024
        ),
        name="step",
    )(query_proj, key_proj, value_proj, taps, chosen, out_weight, grad_out)

    tile = min(512, width)

    def tall(rows):
        return pl.BlockSpec((rows, tile), lambda i: (0, i))

    return pl.pallas_call(
        last_kernel,
        grid=(width // tile,),
        in_specs=[tall(count), tall(count), tall(9)] + [tall(count)] * 3 + [tall(8)] * 2,
        out_specs=[tall(count)] * 4,
        out_shape=[flat] * 4,
        compiler_params=pltpu.CompilerParams(vmem_limit_bytes=62 * 1024 * 1024),
        name="last",
    )(key_proj, value_proj, taps, mixer_out, grad_qf, grad_prod, before, after)


def flipped(x, flip):
    return jnp.dot(flip, x, preferred_element_type=F32)


def pair_kernel(
    q_hbm, k_hbm, v_hbm, taps_in, h_hbm, w_hbm, go_hbm,
    out_hbm, gq_hbm, gk_hbm, gv_hbm,
    w_ref, go_ref, x_ref, taps_ref, h_ref, filt_ref, near_ref, hf_ref,
    filtered_ref, prod_ref, gm_ref, rf_ref, rb_ref, ff_ref, fb_ref, xt_ref, ot_ref, ms_ref, mixed_ref, gp_ref,
    total_ref, join_ref, sx_ref, sy_ref, rx_ref, ry_ref, ga_ref, acc_ref,
    gf_ref, head_ref, fin_ref, mo_send, mo_recv, mo_ref,
    w_sem, in_sem, send_sem, recv_sem, out_sem,
):
    here = lax.axis_index("seq")
    mine = lax.axis_index("chan")
    seq = lax.axis_size("seq")
    count = go_hbm.shape[0]
    width = q_hbm.shape[1]
    half = width // 2
    span = 2 * count
    nblk, _, bw = prod_ref.shape
    parts = nblk // 2
    wb = w_ref.shape[2]
    columns = go_hbm.shape[1]
    chips = seq // 2
    core = lax.rem(here, 2)
    other = 1 - core
    z = here // 2
    zo = z + 1 - 2 * lax.rem(z, 2)
    zq = lax.rem(z, 2)
    zh = z // 2
    bx = mine + 1 - 2 * lax.rem(mine, 2)
    by = lax.rem(mine + 2, 4)
    bd = lax.rem(bx + 2, 4)
    who_id = (mine, bx, by, bd)
    order = [
        [(3, c), (3, 2 + c), (1, c), (2, 2 + c), (0, c), (0, 2 + c), (1, 2 + c), (2, c)]
        for c in range(2)
    ]
    SIB = {"seq": 2 * z + other}
    X = {"chan": bx}
    Y = {"chan": by}
    groups = bw // GROUP
    length = h_ref.shape[2]
    lags = length // count
    outs = lags // 2

    def w_copy(c, j):
        who, blk = order[c][j]
        start = pl.multiple_of(who_id[who] * width + core * half + blk * wb, wb)
        return pltpu.make_async_copy(w_hbm.at[pl.ds(start, wb)], w_ref.at[c, j], w_sem.at[c, j])

    def w_wait(c, j):
        pltpu.make_async_copy(w_hbm.at[pl.ds(0, wb)], w_ref.at[c, j], w_sem.at[c, j]).wait()

    mycols = pl.ds(pl.multiple_of(core * half, half), half)
    sibcols = pl.ds(pl.multiple_of(other * half, half), half)
    myrows = pl.ds(pl.multiple_of(core * count, count), count)
    sibrows = pl.ds(pl.multiple_of(other * count, count), count)
    slabrows = pl.ds(pl.multiple_of(16 + core * count, 16), count)

    ins = [pltpu.make_async_copy(go_hbm, go_ref.at[myrows], in_sem.at[0])]
    for m, src in enumerate((q_hbm, k_hbm, v_hbm)):
        ins.append(pltpu.make_async_copy(src.at[:, mycols], x_ref.at[m, slabrows], in_sem.at[1 + m]))
    for i, side in enumerate((zq, 1 - zq)):
        first = pl.multiple_of(core * (half // GROUP) + side * (half // GROUP // 2), 16)
        ins.append(pltpu.make_async_copy(
            h_hbm.at[pl.ds(first, parts * groups)], h_ref.at[i], in_sem.at[4 + i]
        ))
    ins[0].start()
    w_copy(0, 0).start()
    w_copy(0, 1).start()
    for i in (2, 3, 1, 4, 5):
        ins[i].start()
    for c in range(2):
        for j in range(8):
            if c or j > 1:
                w_copy(c, j).start()

    barrier = pltpu.get_barrier_semaphore()

    def greet(off, carry):
        pl.semaphore_signal(
            barrier, inc=1, device_id={"seq": lax.rem(here + off, seq)}, device_id_type=MESH
        )
        return carry

    lax.fori_loop(1, seq, greet, 0)
    for peer in (X, Y):
        pl.semaphore_signal(barrier, inc=1, device_id=peer, device_id_type=MESH)

    @pl.when(z == 0)
    def _():
        x_ref[:, 0:16] = jnp.zeros((3, 16, half), BF16)

    rows = [taps_in[m] for m in range(3)]
    taps9 = jnp.concatenate(rows + [jnp.zeros((7, taps_in.shape[2]), F32)], axis=0)
    shape = (taps_in.shape[2], half)
    pick = lax.broadcasted_iota(jnp.int32, shape, 0) * GROUP - core * half
    chan_at = lax.broadcasted_iota(jnp.int32, shape, 1)
    hot = jnp.where((chan_at >= pick) & (chan_at < pick + GROUP), 1.0, 0.0).astype(F32)
    wide_taps = jnp.dot(taps9, hot, precision=lax.Precision.HIGHEST, preferred_element_type=F32)
    for b in range(nblk):
        taps_ref[b] = wide_taps[:, b * bw : (b + 1) * bw]
    flip = (
        lax.broadcasted_iota(jnp.int32, (count, count), 0)
        + lax.broadcasted_iota(jnp.int32, (count, count), 1)
        == count - 1
    )
    flip = jnp.where(flip, 1.0, 0.0).astype(BF16)
    xt_ref[:, 0:3] = jnp.zeros((groups, 3, GROUP, count), BF16)
    pl.semaphore_wait(barrier, seq + 1)

    def remote(src, dst, to, send, recv=None):
        return pltpu.make_async_remote_copy(
            src_ref=src, dst_ref=dst, send_sem=send_sem.at[send],
            recv_sem=recv_sem.at[send if recv is None else recv],
            device_id=to, device_id_type=MESH,
        )

    swaps = [remote(go_hbm, go_ref.at[myrows], SIB, 0)]
    for m, src in enumerate((q_hbm, k_hbm, v_hbm)):
        swaps.append(remote(src.at[:, sibcols], x_ref.at[m, slabrows], SIB, 1 + m))

    def rim(m, to):
        src = (q_hbm, k_hbm, v_hbm)[m]
        at = pl.ds(pl.multiple_of(to * half, half), half)
        return remote(
            src.at[count - 16 : count, at], x_ref.at[m, 0:16],
            {"seq": 2 * lax.rem(z + 1, chips) + to}, 4 + 2 * m + to, 4 + 2 * m,
        )

    sends_rim = (core == 1) & (z < chips - 1)
    swaps[0].start()

    @pl.when(sends_rim)
    def _():
        for m in (1, 2, 0):
            for to in range(2):
                rim(m, to).start()

    for i in (2, 3, 1):
        swaps[i].start()

    def rim_wait(m):
        @pl.when(z > 0)
        def _():
            rim(m, 0).wait_recv()

    def cx(k, i):
        return remote(sx_ref.at[k, i], rx_ref.at[k, i], X, 96 + k * 3 + i)

    def cy(k, i):
        return remote(sy_ref.at[k, i], ry_ref.at[k, i], Y, 108 + k * 3 + i)

    def sums(c, lo, hi):
        def one(p, carry):
            w_wait(c, 2 * p)
            w_wait(c, 2 * p + 1)
            got = lax.dot_general(
                go_ref[...], w_ref[c, pl.ds(2 * p, 2)].reshape(2 * wb, columns),
                (((1,), (1,)), ((), ())), preferred_element_type=F32,
            )
            join_ref[c] = got

            def cut(side, s):
                return join_ref[c, :, side * wb + s * bw : side * wb + (s + 1) * bw]

            def away():
                for s in range(2):
                    sx_ref[2 * c + s, p] = cut(0, s).astype(BF16)
                    sy_ref[2 * c + s, p] = cut(1, s).astype(BF16)

            def own():
                for s in range(2):
                    total_ref[2 * c + s] = cut(0, s)
                    total_ref[parts + 2 * c + s] = cut(1, s)

            if lo < 2:
                pl.when(p < 2)(away)
            if lo <= 2 < hi:
                pl.when(p == 2)(own)
            return carry

        lax.fori_loop(lo, hi, one, 0)

    def sums_send(k, i):
        cx(k, i).start()
        cy(k, i).start()

    def sums_joined(k):
        c, s = k // 2, k % 2
        cy(k, 0).wait_recv()
        mine_x = join_ref[c, :, s * bw : (s + 1) * bw]
        sx_ref[k, 2] = (mine_x + ry_ref[k, 0].astype(F32)).astype(BF16)
        cx(k, 2).start()
        cx(k, 0).wait_recv()
        mine_y = join_ref[c, :, wb + s * bw : wb + (s + 1) * bw]
        sy_ref[k, 2] = (mine_y + rx_ref[k, 0].astype(F32)).astype(BF16)
        cy(k, 2).start()

    def cols(b):
        return pl.ds(pl.multiple_of(b * bw, bw), bw)

    def filtering(m, b):
        x = x_ref[m, :, cols(b)].astype(F32)
        taps = taps_ref[b, 3 * m : 3 * m + 3]
        y = x * taps[0:1] + pltpu.roll(x, 1, 0) * taps[1:2] + pltpu.roll(x, 2, 0) * taps[2:3]
        filtered_ref[m, b] = y[16:]
        return y[16:]

    def way(forward):
        if forward:
            return (0, 1, zh == 1, prod_ref, rf_ref, ff_ref, mixed_ref, 0)
        return (chips - 1, chips - 2, zh == 0, gm_ref, rb_ref, fb_ref, gp_ref, 1)

    ZS, ZR, ZP, ZQ = (32, 136), (48, 152), (64, 72), (128, 132)

    def to_late(forward, src, k, owner, to, relayed=False):
        _, _, _, _, dst, _, _, i = way(forward)
        return remote(
            src, dst.at[owner, k], {"seq": 2 * to + core},
            (ZR if relayed else ZS)[i] + 4 * to + k, ZS[i] + 4 * owner + k,
        )

    def late_chip(forward, side):
        return side + (2 if forward else 0)

    def to_second(forward, k, side):
        head, second, _, src, _, keep, _, i = way(forward)
        return remote(
            src.at[parts * side + k], keep.at[side, k], {"seq": 2 * second + core},
            ZP[i] + 4 * side + k,
        )

    def zeach(forward, k, act):
        head, second, late, src, dst, keep, _, _ = way(forward)

        @pl.when(z == head)
        def _():
            for side in range(2):
                act(to_second(forward, k, side))

        @pl.when(z == second)
        def _():
            for side in range(2):
                act(to_late(forward, src.at[parts * side + k], k, z, late_chip(forward, side)))

        @pl.when(late)
        def _():
            act(to_late(forward, src.at[parts * (1 - zq) + k], k, z, zo))

    def zsend(forward, k):
        zeach(forward, k, lambda copy: copy.start())

    def zpass(forward, k, side):
        head, _, _, _, _, keep, _, _ = way(forward)
        return to_late(forward, keep.at[side, k], k, head, late_chip(forward, side), True)

    def zrelay(forward, k):
        @pl.when(z == way(forward)[1])
        def _():
            for side in range(2):
                to_second(forward, k, side).wait_recv()
                zpass(forward, k, side).start()

    def zdone(forward, k):
        zeach(forward, k, lambda copy: copy.wait_send())

        @pl.when(z == way(forward)[1])
        def _():
            for side in range(2):
                zpass(forward, k, side).wait_send()

        @pl.when(way(forward)[2])
        def _():
            ret(forward, k).wait_send()

    def ret(forward, k):
        _, _, _, _, _, _, dst, i = way(forward)
        return remote(
            ms_ref.at[i, k, lax.rem(zo, 2)], dst.at[parts * zq + k], {"seq": 2 * zo + core}, ZQ[i] + k
        )

    def ret_wait(forward, k):
        _, _, late, _, _, _, dst, i = way(forward)

        @pl.when(late)
        def _():
            remote(
                ms_ref.at[i, k, 0], dst.at[parts * (1 - zq) + k], {"seq": 2 * zo + core}, ZQ[i] + k
            ).wait_recv()

    def several(lo, hi, together, one):
        def some(i, carry):
            for u in range(together):
                one(lo + i * together + u)
            return carry

        lax.fori_loop(0, (hi - lo) // together, some, 0)

    def build(lo, hi):
        def one(g, side, depth):
            row = hf_ref[side, pl.ds(g, 1), : depth * count]
            lines = jnp.broadcast_to(row, (count, depth * count))
            both = jnp.concatenate([jnp.zeros((count, count), F32), lines], axis=1)
            lined = pltpu.roll(both, 0, 1, stride=1, stride_axis=0).astype(BF16)
            for k in range(depth):
                at = (k + 1) * count
                to = (filt_ref, near_ref)[side]
                to[g, k * count : (k + 1) * count, :] = lined[:, at : at + count]

        several(lo, hi, 4, lambda g: one(g, 0, lags))
        several(lo, hi, 4, lambda g: one(g, 1, outs))

    def mix(forward, k, last_half):
        head, second, late, sent, src, keep, dst, way_at = way(forward)

        def fill(x2, slot):
            for blk in range(2):
                x = x2[blk * count : (blk + 1) * count]
                if forward:
                    at, x = blk, x.astype(F32)
                else:
                    at, x = 1 - blk, flipped(x, flip)
                xt_ref[:, 3 + slot + at] = x.T.reshape(groups, GROUP, count).astype(BF16)

        def run(filt, top, tall, depth):
            for g in range(groups):
                pieces = [
                    xt_ref[g, top - j : top - j + tall].reshape(tall * GROUP, count)
                    for j in range(depth)
                ]
                got = jnp.dot(
                    jnp.concatenate(pieces, axis=1),
                    filt[groups * k + g, : depth * count],
                    preferred_element_type=F32,
                )
                ot_ref[0:tall, g] = got.reshape(tall, GROUP, count)

        def turned(b, tall):
            y = ot_ref[b].reshape(bw, count).T.astype(BF16)
            if forward:
                return b, y
            return tall - 1 - b, flipped(y, flip).astype(BF16)

        if last_half:
            for d in range(1, chips):
                p = lax.rem(z + d, chips)
                to_late(forward, sent.at[0], k, p, z).wait_recv()
            for i in range(4):
                near = i >= 2
                r = i % 2 if forward else 1 - i % 2
                chip = 2 * zh + r if near else 2 * (1 - zh) + r
                if near:
                    own = zq == r
                    pl.when(own)(lambda i=i: fill(sent[parts * zq + k], 2 * i))
                    pl.when(jnp.logical_not(own))(lambda i=i, chip=chip: fill(src[chip, k], 2 * i))
                else:
                    fill(src[chip, k], 2 * i)
            run(filt_ref, 3 + outs, outs, lags)
            for b in range(outs):
                at, y = turned(b, outs)
                ms_ref[way_at, k, at // 2, (at % 2) * count : (at % 2 + 1) * count, :] = y
            ret(forward, k).start()
            dst[parts * zq + k] = ms_ref[way_at, k, zq]

        else:
            for i in range(2):
                side = zq if i == 0 else 1 - zq
                fill(sent[parts * side + k], 2)

                @pl.when(z == second)
                def _():
                    fill(keep[side, k], 0)

                @pl.when(z == head)
                def _():
                    xt_ref[:, 3:5] = jnp.zeros((groups, 2, GROUP, count), BF16)

                run((filt_ref, near_ref)[i], 5, 2, outs)
                for b in range(2):
                    at, y = turned(b, 2)
                    dst[parts * side + k, at * count : (at + 1) * count, :] = y

    def sums_done(k):
        cx(k, 1).wait_recv()
        cy(k, 2).wait_recv()
        a, b = k, parts + k
        total_ref[a] += rx_ref[k, 1].astype(F32) + ry_ref[k, 2].astype(F32)
        gm_ref[a] = (total_ref[a] * filtered_ref[0, a]).astype(BF16)
        cy(k, 1).wait_recv()
        cx(k, 2).wait_recv()
        total_ref[b] += ry_ref[k, 1].astype(F32) + rx_ref[k, 2].astype(F32)
        gm_ref[b] = (total_ref[b] * filtered_ref[0, b]).astype(BF16)
        zsend(False, k)

    def gat(k, j):
        s = k % 2
        return ga_ref.at[k // 2, j, :, s * bw : (s + 1) * bw]

    def ax(k, i):
        src, dst = ((4, 2), (5, 6), (3, 1))[i]
        return remote(gat(k, src), gat(k, dst), X, 168 + 3 * k + i)

    def ay(k, i):
        src, dst = ((5, 3), (4, 7), (2, 0))[i]
        return remote(gat(k, src), gat(k, dst), Y, 180 + 3 * k + i)

    def gate(k):
        ret_wait(True, k)
        for j, b in enumerate((k, parts + k)):
            s = k % 2
            ga_ref[k // 2, 4 + j, :, s * bw : (s + 1) * bw] = (
                filtered_ref[0, b] * mixed_ref[b].astype(F32)
            ).astype(BF16)
        for i in range(2):
            ax(k, i).start()
            ay(k, i).start()
        for b in (k, parts + k):
            gf_ref[0, b] = (total_ref[b] * mixed_ref[b].astype(F32)).astype(BF16)

    def relay(k):
        ax(k, 0).wait_recv()
        ay(k, 2).start()
        ay(k, 0).wait_recv()
        ax(k, 2).start()

    def gathered(k, i):
        ax(k, i).wait_recv()
        ay(k, i).wait_recv()

    wide = columns // 4

    def project(c, lo, hi, first=False, then=None):
        def some(i, carry):
            at = pl.ds(pl.multiple_of(i * wide, wide), wide)
            got = jnp.dot(
                jnp.concatenate([ga_ref[c, j] for j in range(lo, hi)], axis=1),
                w_ref[c, lo:hi, :, at].reshape((hi - lo) * wb, wide),
                preferred_element_type=F32,
            )
            acc_ref[:, at] = got if first else acc_ref[:, at] + got
            if then is not None:
                then(i, at)
            return carry

        lax.fori_loop(0, columns // wide, some, 0)

    def mo(i, at):
        return remote(mo_send.at[:, at], mo_recv.at[:, at], SIB, 192 + i)

    def mo_out(i, at):
        return pltpu.make_async_copy(mo_ref.at[:, at], out_hbm.at[:, at], out_sem.at[3 + i])

    def give(i, at):
        mo_send[:, at] = acc_ref[sibrows, at].astype(BF16)
        mo(i, at).start()

    def heads(m):
        return remote(
            gf_ref.at[m, :, 0:16], head_ref.at[m],
            {"seq": 2 * lax.rem(z + chips - 1, chips) + core}, 120 + m,
        )

    def heads_start(m):
        @pl.when(z > 0)
        def _():
            heads(m).start()

    def finish(m, ref):
        @pl.when(z < chips - 1)
        def _():
            heads(m).wait_recv()

        def one(b, carry):
            g = gf_ref[m, b].astype(F32)
            taps = taps_ref[b, 3 * m : 3 * m + 3]
            after = jnp.where(z < chips - 1, head_ref[m, b].astype(F32)[0:2], 0.0)
            fin_ref[m, :, cols(b)] = anticausal(g, after, taps).astype(BF16)
            return carry

        lax.fori_loop(0, nblk, one, 0)
        pltpu.make_async_copy(fin_ref.at[m, myrows], ref.at[:, mycols], out_sem.at[m]).start()
        remote(fin_ref.at[m, sibrows], ref.at[:, mycols], SIB, 123 + m).start()

    def grads(k):
        ret_wait(False, k)
        for b in (k, parts + k):
            gp = gp_ref[b].astype(F32)
            gf_ref[1, b] = (gp * filtered_ref[2, b]).astype(BF16)
            gf_ref[2, b] = (gp * filtered_ref[1, b]).astype(BF16)

    def multiply(k, carry):
        for b in (k, parts + k):
            prod_ref[b] = (filtering(1, b) * filtering(2, b)).astype(BF16)
        zsend(True, k)
        return carry

    def query(b, carry):
        filtering(0, b)
        return carry

    def arrived(m):
        ins[1 + m].wait()
        swaps[1 + m].wait_recv()
        rim_wait(m)

    def filters(lo, hi):
        if lo == 0:
            ins[4].wait()
            ins[5].wait()
            hf_ref[...] = h_ref[...].astype(F32)
        build(lo * groups, hi * groups)

    def next_sums(k):
        sums_joined(k)
        if k + 1 < parts:
            sums_send(k + 1, 0)
            sums_send(k + 1, 1)

    def early(act):
        pl.when(zh == 0)(act)

    def later(act):
        pl.when(zh == 1)(act)

    def mixed(forward, k):
        for last_half in (True, False):
            half_at = 1 if forward == last_half else 0
            pl.when(zh == half_at)(lambda last_half=last_half: mix(forward, k, last_half))

    def near_in(ks):
        for k in ks:
            gathered(k, 1)

    def far_in(ks):
        for k in ks:
            gathered(k, 2)

    ins[0].wait()
    swaps[0].wait_recv()
    sums(0, 0, 1)
    sums_send(0, 0)
    sums_send(1, 0)
    arrived(1)
    arrived(2)
    lax.fori_loop(0, parts, multiply, 0)
    sums(0, 1, 4)
    sums_send(0, 1)
    sums_joined(0)
    sums_send(1, 1)
    sums(1, 0, 4)
    zrelay(True, 0)
    arrived(0)
    lax.fori_loop(0, nblk, query, 0)
    sums_done(0)
    next_sums(1)
    zrelay(True, 1)
    zrelay(True, 2)
    filters(0, 2)
    zrelay(False, 0)
    sums_done(1)
    next_sums(2)
    mixed(True, 0)
    zrelay(True, 3)
    zrelay(False, 1)
    sums_done(2)
    mixed(False, 0)
    next_sums(3)
    gate(0)
    mixed(True, 1)
    filters(2, 4)
    zrelay(False, 2)
    sums_done(3)
    mixed(True, 2)
    gate(1)
    relay(0)
    mixed(False, 1)
    zrelay(False, 3)
    gate(2)
    relay(1)
    mixed(False, 2)
    mixed(True, 3)
    later(lambda: mix(False, 3, False))
    relay(2)
    gate(3)
    early(lambda: mix(False, 3, True))
    heads_start(0)
    near_in((0, 1))
    far_in((0, 1))
    project(0, 0, 8, True)
    relay(3)
    for k in range(parts):
        grads(k)
    heads_start(1)
    heads_start(2)
    finish(0, gq_hbm)
    near_in((2, 3))
    project(1, 2, 8)
    finish(1, gk_hbm)
    finish(2, gv_hbm)

    for k in range(2, 4):
        gathered(k, 2)
    project(1, 0, 2, then=give)
    for i in range(4):
        at = pl.ds(i * wide, wide)
        mo(i, at).wait_recv()
        mo_ref[:, at] = (acc_ref[myrows, at] + mo_recv[:, at].astype(F32)).astype(BF16)
        mo_out(i, at).start()

    for copy in swaps:
        copy.wait_send()

    @pl.when(sends_rim)
    def _():
        for m in range(3):
            for to in range(2):
                rim(m, to).wait_send()

    for k in range(parts):
        for i in range(3):
            for make in (cx, cy, ax, ay):
                make(k, i).wait_send()
        for forward in (True, False):
            zdone(forward, k)

    @pl.when(z > 0)
    def _():
        for m in range(3):
            heads(m).wait_send()

    for m, ref in enumerate((gq_hbm, gk_hbm, gv_hbm)):
        pltpu.make_async_copy(fin_ref.at[m, myrows], ref.at[:, mycols], out_sem.at[m]).wait()
        remote(fin_ref.at[m, sibrows], ref.at[:, mycols], SIB, 123 + m).wait_send()
        remote(fin_ref.at[m, sibrows], ref.at[:, sibcols], SIB, 123 + m).wait_recv()
    for i in range(4):
        at = pl.ds(i * wide, wide)
        mo(i, at).wait_send()
        mo_out(i, at).wait()


def copy_kernel(*refs):
    srcs, dsts, held, sem_in, sem_out = refs[:4], refs[4:8], *refs[8:]
    into = [pltpu.make_async_copy(src, held.at[i], sem_in.at[i]) for i, src in enumerate(srcs)]
    out = [pltpu.make_async_copy(held.at[i], dst, sem_out.at[i]) for i, dst in enumerate(dsts)]
    for copy in into:
        copy.start()
    for i in range(4):
        into[i].wait()
        out[i].start()
    for copy in out:
        copy.wait()


def paired(query_proj, key_proj, value_proj, short_filter, long_filter, out_weight, grad_out):
    count, width = query_proj.shape
    length = long_filter.shape[1]
    columns = out_weight.shape[1]
    half = width // 2
    span = 2 * count
    bw = half // 8
    groups = bw // GROUP
    lags = length // count

    vmem = pl.BlockSpec(memory_space=pltpu.VMEM)
    hbm = pl.BlockSpec(memory_space=pl.ANY)
    flat = jax.ShapeDtypeStruct((count, width), BF16)
    block = (span, bw)
    results = pl.pallas_call(
        pair_kernel,
        in_specs=[hbm] * 3 + [vmem] + [hbm] * 3,
        out_specs=[hbm] * 4,
        out_shape=[flat] * 4,
        scratch_shapes=[
            pltpu.VMEM((2, 8, 2 * bw, columns), BF16),
            pltpu.VMEM((span, columns), BF16),
            pltpu.VMEM((3, 16 + span, half), BF16),
            pltpu.VMEM((8, 16, bw), F32),
            pltpu.VMEM((2, 4 * groups, length), BF16),
            pltpu.VMEM((4 * groups, length, count), BF16),
            pltpu.VMEM((4 * groups, length // 2, count), BF16),
            pltpu.VMEM((2, 4 * groups, length), F32),
            pltpu.VMEM((3, 8) + block, F32),
            pltpu.VMEM((8,) + block, BF16),
            pltpu.VMEM((8,) + block, BF16),
            pltpu.VMEM((4, 4) + block, BF16),
            pltpu.VMEM((4, 4) + block, BF16),
            pltpu.VMEM((2, 4) + block, BF16),
            pltpu.VMEM((2, 4) + block, BF16),
            pltpu.VMEM((groups, 3 + lags, GROUP, count), BF16),
            pltpu.VMEM((lags // 2, groups, GROUP, count), F32),
            pltpu.VMEM((2, 4, 2) + block, BF16),
            pltpu.VMEM((8,) + block, BF16),
            pltpu.VMEM((8,) + block, BF16),
            pltpu.VMEM((8,) + block, F32),
            pltpu.VMEM((2, span, 4 * bw), F32),
            pltpu.VMEM((4, 3) + block, BF16),
            pltpu.VMEM((4, 3) + block, BF16),
            pltpu.VMEM((4, 3) + block, BF16),
            pltpu.VMEM((4, 3) + block, BF16),
            pltpu.VMEM((2, 8, span, 2 * bw), BF16),
            pltpu.VMEM((span, columns), F32),
            pltpu.VMEM((3, 8) + block, BF16),
            pltpu.VMEM((3, 8, 16, bw), BF16),
            pltpu.VMEM((3, span, half), BF16),
            pltpu.VMEM((count, columns), BF16),
            pltpu.VMEM((count, columns), BF16),
            pltpu.VMEM((count, columns), BF16),
            pltpu.SemaphoreType.DMA((2, 8)),
            pltpu.SemaphoreType.DMA((6,)),
            pltpu.SemaphoreType.DMA((196,)),
            pltpu.SemaphoreType.DMA((196,)),
            pltpu.SemaphoreType.DMA((7,)),
        ],
        compiler_params=pltpu.CompilerParams(
            collective_id=0, has_side_effects=True, vmem_limit_bytes=62 * 1024 * 1024
        ),
        name="step",
    )(
        query_proj, key_proj, value_proj, short_filter.transpose(0, 2, 1),
        long_filter, out_weight, grad_out,
    )
    return pl.pallas_call(
        copy_kernel,
        in_specs=[hbm] * 4,
        out_specs=[hbm] * 4,
        out_shape=[flat] * 4,
        scratch_shapes=[
            pltpu.VMEM((4, count, width), BF16),
            pltpu.SemaphoreType.DMA((4,)),
            pltpu.SemaphoreType.DMA((4,)),
        ],
        compiler_params=pltpu.CompilerParams(vmem_limit_bytes=62 * 1024 * 1024),
        name="last",
    )(*results)


def either(query_proj, key_proj, value_proj, short_filter, long_filter, out_weight, grad_out):
    args = (query_proj, key_proj, value_proj, short_filter, long_filter, out_weight, grad_out)
    count, width = query_proj.shape
    fits = (
        lax.axis_size("seq") == 8
        and lax.axis_size("chan") == 4
        and count % 128 == 0
        and width % 2048 == 0
        and long_filter.shape[1] == 8 * count
    )
    return paired(*args) if fits else local(*args)


def solution(mesh):
    return jax.shard_map(
        either,
        mesh=mesh,
        in_specs=(
            P("seq", "chan"),
            P("seq", "chan"),
            P("seq", "chan"),
            P(None, "chan", None),
            P("chan", None),
            P(None, "chan"),
            P("seq", "chan"),
        ),
        out_specs=(P("seq", "chan"), P("seq", "chan"), P("seq", "chan"), P("seq", "chan")),
        check_vma=False,
    )
```

```python
import jax
import jax.numpy as jnp
from jax import lax
from jax.experimental import pallas as pl
from jax.experimental.pallas import tpu as pltpu
from jax.sharding import PartitionSpec as P

GROUP = 16
F32 = jnp.float32
BF16 = jnp.bfloat16
MESH = pl.DeviceIdType.MESH


def causal(x, before, taps):
    row = lax.broadcasted_iota(jnp.int32, x.shape, 0)
    one = jnp.where(row == 0, before[1:2], pltpu.roll(x, 1, 0))
    two = jnp.where(row == 0, before[0:1], jnp.where(row == 1, before[1:2], pltpu.roll(x, 2, 0)))
    return x * taps[0:1] + one * taps[1:2] + two * taps[2:3]


def anticausal(g, after, taps):
    count = g.shape[0]
    row = lax.broadcasted_iota(jnp.int32, g.shape, 0)
    one = jnp.where(row == count - 1, after[0:1], pltpu.roll(g, count - 1, 0))
    two = jnp.where(
        row == count - 1,
        after[1:2],
        jnp.where(row == count - 2, after[0:1], pltpu.roll(g, count - 2, 0)),
    )
    return g * taps[0:1] + one * taps[1:2] + two * taps[2:3]


def rounded(x):
    return x.astype(BF16).astype(F32)


def step_kernel(
    q_ref, k_ref, v_ref, taps_ref, h_ref, w_hbm, go_ref,
    out_ref, gqf_ref, gp_ref, before_ref, after_ref,
    w_ref, got_ref, hr_ref, filt_ref, send_refs, recv_refs, part_send, part_recv, gall_ref,
    acc_ref, hsend_ref, hrecv_ref, tail_ref, head_ref,
    w_sem, seq_send, seq_recv, chan_send, chan_recv, halo_send, halo_recv,
):
    seq = lax.axis_size("seq")
    chan = lax.axis_size("chan")
    here = lax.axis_index("seq")
    mine = lax.axis_index("chan")
    count, width = q_ref.shape
    _, groups, gw, _ = recv_refs.shape[1:]
    per = groups * gw
    length = h_ref.shape[1]
    columns = go_ref.shape[1]
    tile = max(per, min(256, width))
    tiles = width // tile
    dests = tile // per
    rows = min(512, width)
    wide = min(512, columns)

    def seq_peer(off):
        return lax.rem(here + off, seq)

    def chan_peer(off):
        return lax.rem(mine + off, chan)

    def w_copy(off):
        at = pl.ds(pl.multiple_of(chan_peer(off) * width, width), width)
        return pltpu.make_async_copy(w_hbm.at[at], w_ref.at[at], w_sem.at[off])

    order = [off % chan for off in range(1, chan + 1)]
    for off in order:
        w_copy(off).start()

    barrier = pltpu.get_barrier_semaphore()

    def greet_seq(off, carry):
        pl.semaphore_signal(
            barrier, inc=1, device_id={"seq": seq_peer(off)}, device_id_type=MESH
        )
        return carry

    def greet_chan(off, carry):
        pl.semaphore_signal(
            barrier, inc=1, device_id={"chan": chan_peer(off)}, device_id_type=MESH
        )
        return carry

    lax.fori_loop(1, seq, greet_seq, 0)
    lax.fori_loop(1, chan, greet_chan, 0)

    for m, ref in enumerate((q_ref, k_ref, v_ref)):
        hsend_ref[0, 2 * m : 2 * m + 2, :] = ref[count - 16 :, :].astype(F32)[14:]
        hsend_ref[1, 2 * m : 2 * m + 2, :] = ref[:16, :].astype(F32)[:2]
    pl.semaphore_wait(barrier, seq + chan - 2)

    def halo(slot, by, src, dst):
        return pltpu.make_async_remote_copy(
            src_ref=src, dst_ref=dst, send_sem=halo_send.at[slot], recv_sem=halo_recv.at[slot],
            device_id={"seq": seq_peer(by)}, device_id_type=MESH,
        )

    halo_down = halo(0, 1, hsend_ref.at[0, 0:6], hrecv_ref.at[0, 0:6])
    halo_up = halo(1, seq - 1, hsend_ref.at[1, 0:6], hrecv_ref.at[1, 0:6])
    halo_down.start()
    halo_up.start()

    def turn(i, carry):
        at = pl.ds(pl.multiple_of(i * wide, wide), wide)
        got_ref[at, :] = go_ref[:, at].astype(F32).T.astype(BF16)
        return carry

    lax.fori_loop(0, columns // wide, turn, 0)

    def exchange(slot, off):
        return pltpu.make_async_remote_copy(
            src_ref=send_refs.at[slot, seq_peer(off)],
            dst_ref=recv_refs.at[slot, here],
            send_sem=seq_send.at[slot, off],
            recv_sem=seq_recv.at[slot, off],
            device_id={"seq": seq_peer(off)},
            device_id_type=MESH,
        )

    def exchange_start(slot):
        def go(off, carry):
            exchange(slot, off).start()
            return carry

        lax.fori_loop(1, seq, go, 0)
        recv_refs[slot, pl.ds(here, 1)] = send_refs[slot, pl.ds(here, 1)]

    def exchange_wait(slot):
        def go(off, carry):
            exchange(slot, off).wait()
            return carry

        lax.fori_loop(1, seq, go, 0)

    def to_send(slot, i, turned):
        send_refs[slot, pl.ds(i * dests, dests)] = turned.reshape(
            dests, groups, gw, count
        ).astype(BF16)

    def from_recv(slot, i):
        return recv_refs[slot, pl.ds(i * dests, dests)].astype(F32).reshape(tile, count)

    def cols(i):
        return pl.ds(pl.multiple_of(i * tile, tile), tile)

    def filtered(ref, m, at):
        ahead = jnp.where(here > 0, hrecv_ref[0, 2 * m : 2 * m + 2, at], 0.0)
        return causal(ref[:, at].astype(F32), ahead, taps_ref[3 * m : 3 * m + 3, at])

    halo_down.wait()
    halo_up.wait()

    def spread(slot, make):
        def one(i, carry):
            to_send(slot, i, make(cols(i)))
            return carry

        def off_to(off, carry):
            one(seq_peer(off), 0)
            exchange(slot, off).start()
            return carry

        if dests == 1:
            lax.fori_loop(1, seq, off_to, 0)
            one(here, 0)
            recv_refs[slot, pl.ds(here, 1)] = send_refs[slot, pl.ds(here, 1)]
        else:
            lax.fori_loop(0, tiles, one, 0)
            exchange_start(slot)

    spread(0, lambda at: (filtered(k_ref, 1, at) * filtered(v_ref, 2, at)).T)

    def part(off):
        return pltpu.make_async_remote_copy(
            src_ref=part_send.at[off - 1],
            dst_ref=part_recv.at[mine],
            send_sem=chan_send.at[0, off],
            recv_sem=chan_recv.at[0, off],
            device_id={"chan": chan_peer(off)},
            device_id_type=MESH,
        )

    def back_project(off):
        w_copy(off).wait()

        def some(i, carry):
            start = pl.multiple_of(chan_peer(off) * width + i * rows, rows)
            got = jnp.dot(w_ref[pl.ds(start, rows), :], got_ref[...], preferred_element_type=F32)
            at = pl.ds(pl.multiple_of(i * rows, rows), rows)
            if off:
                part_send[off - 1, at, :] = got.astype(BF16)
            else:
                part_recv[mine, at, :] = got.astype(BF16)
            return carry

        lax.fori_loop(0, width // rows, some, 0)
        if off:
            part(off).start()

    for off in range(1, chan):
        back_project(off)

    flip = (
        lax.broadcasted_iota(jnp.int32, (count, count), 0)
        + lax.broadcasted_iota(jnp.int32, (count, count), 1)
        == count - 1
    )
    flip = jnp.where(flip, 1.0, 0.0).astype(BF16)
    for k in range(length // count):
        hr_ref[:, length - (k + 1) * count : length - k * count] = jnp.dot(
            h_ref[:, k * count : (k + 1) * count].astype(BF16), flip, preferred_element_type=F32
        )

    def build(forward):
        def one(g, carry):
            pad = jnp.zeros((count, count), F32)
            row = (h_ref if forward else hr_ref)[pl.ds(g, 1), :]
            lines = jnp.broadcast_to(row, (count, length))
            pair = [pad, lines] if forward else [lines, pad]
            lined = pltpu.roll(
                jnp.concatenate(pair, axis=1), 0 if forward else 1, 1, stride=1, stride_axis=0
            ).astype(BF16)
            for k in range(length // count):
                at = (k + 1) * count if forward else length - k * count
                filt_ref[g, k * count : (k + 1) * count, :] = lined[:, at : at + count]
            return carry

        lax.fori_loop(0, groups, one, 0)

    def mix(forward, slot):
        total_rows = seq * gw

        def one(g, carry):
            x = recv_refs[slot, :, g]
            kind = F32 if gw % 16 else BF16
            x = x.astype(kind).reshape(total_rows, count)
            pieces = [x.astype(BF16)]
            for k in range(1, seq):
                pad = jnp.zeros((k * gw, count), kind)
                if forward:
                    moved = jnp.concatenate([pad, x[: total_rows - k * gw]], axis=0)
                else:
                    moved = jnp.concatenate([x[k * gw :], pad], axis=0)
                pieces.append(moved.astype(BF16))
            total = jnp.dot(
                jnp.concatenate(pieces, axis=1), filt_ref[g], preferred_element_type=F32
            )
            send_refs[slot + 1, :, g] = total.reshape(seq, gw, count).astype(BF16)
            return carry

        lax.fori_loop(0, groups, one, 0)

    build(True)
    exchange_wait(0)
    mix(True, 0)
    exchange_start(1)
    back_project(0)
    build(False)

    for off in range(1, chan):
        part(off).wait()

    def summed(at):
        return jnp.sum(part_recv[:, at, :].astype(F32), axis=0)

    spread(2, lambda at: summed(at) * filtered(q_ref, 0, at).T)

    def share(off):
        return pltpu.make_async_remote_copy(
            src_ref=gall_ref.at[mine],
            dst_ref=gall_ref.at[mine],
            send_sem=chan_send.at[1, off],
            recv_sem=chan_recv.at[1, off],
            device_id={"chan": chan_peer(off)},
            device_id_type=MESH,
        )

    exchange_wait(1)

    def gate(i, carry):
        at = cols(i)
        gall_ref[mine, :, at] = (filtered(q_ref, 0, at) * from_recv(1, i).T).astype(BF16)
        return carry

    lax.fori_loop(0, tiles, gate, 0)
    for off in range(1, chan):
        share(off).start()

    def grad_query(i, carry):
        at = cols(i)
        gqf_ref[:, at] = (summed(at) * from_recv(1, i)).T.astype(BF16)
        return carry

    lax.fori_loop(0, tiles, grad_query, 0)

    def project(off, first, last):
        owner = chan_peer(chan - off)

        def some(i, carry):
            at = pl.ds(pl.multiple_of(i * wide, wide), wide)
            start = pl.multiple_of(owner * width, width)
            got = jnp.dot(
                gall_ref[owner], w_ref[pl.ds(start, width), at], preferred_element_type=F32
            )
            if not first:
                got = got + acc_ref[:, at]
            if last:
                out_ref[:, at] = got.astype(BF16)
            else:
                acc_ref[:, at] = got
            return carry

        lax.fori_loop(0, columns // wide, some, 0)

    project(0, True, chan == 1)
    exchange_wait(2)
    mix(False, 2)
    exchange_start(3)
    for off in range(1, chan):
        share(off).wait()
        project(off, False, off == chan - 1)

    exchange_wait(3)

    def grad_products(i, carry):
        at = cols(i)
        gp_ref[:, at] = from_recv(3, i).T.astype(BF16)
        return carry

    lax.fori_loop(0, tiles, grad_products, 0)
    tail_ref[0:2, :] = gqf_ref[:16, :].astype(F32)[:2]
    tail_ref[2:4, :] = gp_ref[:16, :].astype(F32)[:2]
    tail = halo(2, seq - 1, tail_ref, head_ref)
    tail.start()
    before_ref[0:6, :] = jnp.where(here > 0, hrecv_ref[0, 0:6, :], 0.0)
    after_ref[4:8, :] = hrecv_ref[1, 2:6, :]
    tail.wait()
    after_ref[0:4, :] = jnp.where(here < seq - 1, head_ref[...], 0.0)


def last_kernel(
    k_ref, v_ref, taps_ref, mixer_ref, gqf_ref, gp_ref, before_ref, after_ref,
    out_ref, gq_ref, gk_ref, gv_ref,
):
    count = k_ref.shape[0]
    gp = gp_ref[...].astype(F32)
    gqf_next = after_ref[0:2]
    gp_next = after_ref[2:4]

    def both(ref, m):
        x = ref[...].astype(F32)
        taps = taps_ref[3 * m : 3 * m + 3]
        new = after_ref[2 + 2 * m : 4 + 2 * m]
        near, far = x[count - 1 : count], x[count - 2 : count - 1]
        first = new[0:1] * taps[0:1] + near * taps[1:2] + far * taps[2:3]
        second = new[1:2] * taps[0:1] + new[0:1] * taps[1:2] + near * taps[2:3]
        inside = causal(x, before_ref[2 * m : 2 * m + 2], taps)
        return inside, jnp.concatenate([first, second], axis=0)

    kf, kf_next = both(k_ref, 1)
    vf, vf_next = both(v_ref, 2)
    out_ref[...] = mixer_ref[...]
    gq_ref[...] = anticausal(gqf_ref[...].astype(F32), gqf_next, taps_ref[0:3]).astype(BF16)
    gk_ref[...] = anticausal(
        rounded(gp * vf), rounded(gp_next * vf_next), taps_ref[3:6]
    ).astype(BF16)
    gv_ref[...] = anticausal(
        rounded(gp * kf), rounded(gp_next * kf_next), taps_ref[6:9]
    ).astype(BF16)


def local(query_proj, key_proj, value_proj, short_filter, long_filter, out_weight, grad_out):
    count, width = query_proj.shape
    seq = lax.axis_size("seq")
    chan = lax.axis_size("chan")
    per = width // seq
    gw = min(per, GROUP)
    groups = per // gw
    length = long_filter.shape[1]
    depth, columns = out_weight.shape

    taps = jnp.repeat(short_filter.transpose(0, 2, 1).reshape(9, -1), GROUP, axis=1)
    first = lax.axis_index("seq") * per // GROUP
    chosen = lax.dynamic_slice_in_dim(long_filter, first, groups, 0).astype(F32)

    vmem = pl.BlockSpec(memory_space=pltpu.VMEM)
    flat = jax.ShapeDtypeStruct((count, width), BF16)
    rims = jax.ShapeDtypeStruct((8, width), F32)
    mixer_out, grad_qf, grad_prod, before, after = pl.pallas_call(
        step_kernel,
        in_specs=[vmem] * 5 + [pl.BlockSpec(memory_space=pl.ANY), vmem],
        out_specs=[vmem] * 5,
        out_shape=[jax.ShapeDtypeStruct((count, columns), BF16), flat, flat, rims, rims],
        scratch_shapes=[
            pltpu.VMEM((depth, columns), BF16),
            pltpu.VMEM((columns, count), BF16),
            pltpu.VMEM((groups, length), F32),
            pltpu.VMEM((groups, length, count), BF16),
            pltpu.VMEM((4, seq, groups, gw, count), BF16),
            pltpu.VMEM((4, seq, groups, gw, count), BF16),
            pltpu.VMEM((chan - 1, width, count), BF16),
            pltpu.VMEM((chan, width, count), BF16),
            pltpu.VMEM((chan, count, width), BF16),
            pltpu.VMEM((count, columns), F32),
            pltpu.VMEM((2, 8, width), F32),
            pltpu.VMEM((2, 8, width), F32),
            pltpu.VMEM((4, width), F32),
            pltpu.VMEM((4, width), F32),
            pltpu.SemaphoreType.DMA((chan,)),
            pltpu.SemaphoreType.DMA((4, seq)),
            pltpu.SemaphoreType.DMA((4, seq)),
            pltpu.SemaphoreType.DMA((2, chan)),
            pltpu.SemaphoreType.DMA((2, chan)),
            pltpu.SemaphoreType.DMA((3,)),
            pltpu.SemaphoreType.DMA((3,)),
        ],
        compiler_params=pltpu.CompilerParams(
            collective_id=0, has_side_effects=True, vmem_limit_bytes=62 * 1024 * 1024
        ),
        name="step",
    )(query_proj, key_proj, value_proj, taps, chosen, out_weight, grad_out)

    tile = min(512, width)

    def tall(rows):
        return pl.BlockSpec((rows, tile), lambda i: (0, i))

    return pl.pallas_call(
        last_kernel,
        grid=(width // tile,),
        in_specs=[tall(count), tall(count), tall(9)] + [tall(count)] * 3 + [tall(8)] * 2,
        out_specs=[tall(count)] * 4,
        out_shape=[flat] * 4,
        compiler_params=pltpu.CompilerParams(vmem_limit_bytes=62 * 1024 * 1024),
        name="last",
    )(key_proj, value_proj, taps, mixer_out, grad_qf, grad_prod, before, after)


def flipped(x, flip):
    return jnp.dot(flip, x, preferred_element_type=F32)


def pair_kernel(
    q_hbm, k_hbm, v_hbm, taps_in, h_hbm, w_hbm, go_hbm,
    out_hbm, gq_hbm, gk_hbm, gv_hbm,
    w_ref, go_ref, x_ref, taps_ref, h_ref, filt_ref, near_ref, hf_ref,
    filtered_ref, prod_ref, gm_ref, rf_ref, rb_ref, ff_ref, fb_ref, xt_ref, ot_ref, ms_ref, mixed_ref, gp_ref,
    total_ref, join_ref, sx_ref, sy_ref, rx_ref, ry_ref, ga_ref, acc_ref,
    gf_ref, head_ref, fin_ref, mo_send, mo_recv, mo_ref,
    w_sem, in_sem, send_sem, recv_sem, out_sem,
):
    here = lax.axis_index("seq")
    mine = lax.axis_index("chan")
    seq = lax.axis_size("seq")
    count = go_hbm.shape[0]
    width = q_hbm.shape[1]
    half = width // 2
    span = 2 * count
    nblk, _, bw = prod_ref.shape
    parts = nblk // 2
    wb = w_ref.shape[2]
    columns = go_hbm.shape[1]
    chips = seq // 2
    core = lax.rem(here, 2)
    other = 1 - core
    z = here // 2
    zo = z + 1 - 2 * lax.rem(z, 2)
    zq = lax.rem(z, 2)
    zh = z // 2
    bx = mine + 1 - 2 * lax.rem(mine, 2)
    by = lax.rem(mine + 2, 4)
    bd = lax.rem(bx + 2, 4)
    who_id = (mine, bx, by, bd)
    order = [
        [(3, c), (3, 2 + c), (1, c), (2, 2 + c), (0, c), (0, 2 + c), (1, 2 + c), (2, c)]
        for c in range(2)
    ]
    SIB = {"seq": 2 * z + other}
    X = {"chan": bx}
    Y = {"chan": by}
    groups = bw // GROUP
    length = h_ref.shape[2]
    lags = length // count
    outs = lags // 2

    def w_copy(c, j):
        who, blk = order[c][j]
        start = pl.multiple_of(who_id[who] * width + core * half + blk * wb, wb)
        return pltpu.make_async_copy(w_hbm.at[pl.ds(start, wb)], w_ref.at[c, j], w_sem.at[c, j])

    def w_wait(c, j):
        pltpu.make_async_copy(w_hbm.at[pl.ds(0, wb)], w_ref.at[c, j], w_sem.at[c, j]).wait()

    mycols = pl.ds(pl.multiple_of(core * half, half), half)
    sibcols = pl.ds(pl.multiple_of(other * half, half), half)
    myrows = pl.ds(pl.multiple_of(core * count, count), count)
    sibrows = pl.ds(pl.multiple_of(other * count, count), count)
    slabrows = pl.ds(pl.multiple_of(16 + core * count, 16), count)

    ins = [pltpu.make_async_copy(go_hbm, go_ref.at[myrows], in_sem.at[0])]
    for m, src in enumerate((q_hbm, k_hbm, v_hbm)):
        ins.append(pltpu.make_async_copy(src.at[:, mycols], x_ref.at[m, slabrows], in_sem.at[1 + m]))
    for i, side in enumerate((zq, 1 - zq)):
        first = pl.multiple_of(core * (half // GROUP) + side * (half // GROUP // 2), 16)
        ins.append(pltpu.make_async_copy(
            h_hbm.at[pl.ds(first, parts * groups)], h_ref.at[i], in_sem.at[4 + i]
        ))
    ins[0].start()
    w_copy(0, 0).start()
    w_copy(0, 1).start()
    for i in (2, 3, 1, 4, 5):
        ins[i].start()
    for c in range(2):
        for j in range(8):
            if c or j > 1:
                w_copy(c, j).start()

    barrier = pltpu.get_barrier_semaphore()

    def greet(off, carry):
        pl.semaphore_signal(
            barrier, inc=1, device_id={"seq": lax.rem(here + off, seq)}, device_id_type=MESH
        )
        return carry

    lax.fori_loop(1, seq, greet, 0)
    for peer in (X, Y):
        pl.semaphore_signal(barrier, inc=1, device_id=peer, device_id_type=MESH)

    @pl.when(z == 0)
    def _():
        x_ref[:, 0:16] = jnp.zeros((3, 16, half), BF16)

    rows = [taps_in[m] for m in range(3)]
    taps9 = jnp.concatenate(rows + [jnp.zeros((7, taps_in.shape[2]), F32)], axis=0)
    shape = (taps_in.shape[2], half)
    pick = lax.broadcasted_iota(jnp.int32, shape, 0) * GROUP - core * half
    chan_at = lax.broadcasted_iota(jnp.int32, shape, 1)
    hot = jnp.where((chan_at >= pick) & (chan_at < pick + GROUP), 1.0, 0.0).astype(F32)
    wide_taps = jnp.dot(taps9, hot, precision=lax.Precision.HIGHEST, preferred_element_type=F32)
    for b in range(nblk):
        taps_ref[b] = wide_taps[:, b * bw : (b + 1) * bw]
    flip = (
        lax.broadcasted_iota(jnp.int32, (count, count), 0)
        + lax.broadcasted_iota(jnp.int32, (count, count), 1)
        == count - 1
    )
    flip = jnp.where(flip, 1.0, 0.0).astype(BF16)
    xt_ref[:, 0:3] = jnp.zeros((groups, 3, GROUP, count), BF16)
    pl.semaphore_wait(barrier, seq + 1)

    def remote(src, dst, to, send, recv=None):
        return pltpu.make_async_remote_copy(
            src_ref=src, dst_ref=dst, send_sem=send_sem.at[send],
            recv_sem=recv_sem.at[send if recv is None else recv],
            device_id=to, device_id_type=MESH,
        )

    swaps = [remote(go_hbm, go_ref.at[myrows], SIB, 0)]
    for m, src in enumerate((q_hbm, k_hbm, v_hbm)):
        swaps.append(remote(src.at[:, sibcols], x_ref.at[m, slabrows], SIB, 1 + m))

    def rim(m, to):
        src = (q_hbm, k_hbm, v_hbm)[m]
        at = pl.ds(pl.multiple_of(to * half, half), half)
        return remote(
            src.at[count - 16 : count, at], x_ref.at[m, 0:16],
            {"seq": 2 * lax.rem(z + 1, chips) + to}, 4 + 2 * m + to, 4 + 2 * m,
        )

    sends_rim = (core == 1) & (z < chips - 1)
    swaps[0].start()

    @pl.when(sends_rim)
    def _():
        for m in (1, 2, 0):
            for to in range(2):
                rim(m, to).start()

    for i in (2, 3, 1):
        swaps[i].start()

    def rim_wait(m):
        @pl.when(z > 0)
        def _():
            rim(m, 0).wait_recv()

    def cx(k, i):
        return remote(sx_ref.at[k, i], rx_ref.at[k, i], X, 96 + k * 3 + i)

    def cy(k, i):
        return remote(sy_ref.at[k, i], ry_ref.at[k, i], Y, 108 + k * 3 + i)

    def sums(c, lo, hi):
        def one(p, carry):
            w_wait(c, 2 * p)
            w_wait(c, 2 * p + 1)
            got = lax.dot_general(
                go_ref[...], w_ref[c, pl.ds(2 * p, 2)].reshape(2 * wb, columns),
                (((1,), (1,)), ((), ())), preferred_element_type=F32,
            )
            join_ref[c] = got

            def cut(side, s):
                return join_ref[c, :, side * wb + s * bw : side * wb + (s + 1) * bw]

            def away():
                for s in range(2):
                    sx_ref[2 * c + s, p] = cut(0, s).astype(BF16)
                    sy_ref[2 * c + s, p] = cut(1, s).astype(BF16)

            def own():
                for s in range(2):
                    total_ref[2 * c + s] = cut(0, s)
                    total_ref[parts + 2 * c + s] = cut(1, s)

            if lo < 2:
                pl.when(p < 2)(away)
            if lo <= 2 < hi:
                pl.when(p == 2)(own)
            return carry

        lax.fori_loop(lo, hi, one, 0)

    def sums_send(k, i):
        cx(k, i).start()
        cy(k, i).start()

    def sums_joined(k):
        c, s = k // 2, k % 2
        cy(k, 0).wait_recv()
        mine_x = join_ref[c, :, s * bw : (s + 1) * bw]
        sx_ref[k, 2] = (mine_x + ry_ref[k, 0].astype(F32)).astype(BF16)
        cx(k, 2).start()
        cx(k, 0).wait_recv()
        mine_y = join_ref[c, :, wb + s * bw : wb + (s + 1) * bw]
        sy_ref[k, 2] = (mine_y + rx_ref[k, 0].astype(F32)).astype(BF16)
        cy(k, 2).start()

    def cols(b):
        return pl.ds(pl.multiple_of(b * bw, bw), bw)

    def filtering(m, b):
        x = x_ref[m, :, cols(b)].astype(F32)
        taps = taps_ref[b, 3 * m : 3 * m + 3]
        y = x * taps[0:1] + pltpu.roll(x, 1, 0) * taps[1:2] + pltpu.roll(x, 2, 0) * taps[2:3]
        filtered_ref[m, b] = y[16:]
        return y[16:]

    def way(forward):
        if forward:
            return (0, 1, zh == 1, prod_ref, rf_ref, ff_ref, mixed_ref, 0)
        return (chips - 1, chips - 2, zh == 0, gm_ref, rb_ref, fb_ref, gp_ref, 1)

    ZS, ZR, ZP, ZQ = (32, 136), (48, 152), (64, 72), (128, 132)

    def to_late(forward, src, k, owner, to, relayed=False):
        _, _, _, _, dst, _, _, i = way(forward)
        return remote(
            src, dst.at[owner, k], {"seq": 2 * to + core},
            (ZR if relayed else ZS)[i] + 4 * to + k, ZS[i] + 4 * owner + k,
        )

    def late_chip(forward, side):
        return side + (2 if forward else 0)

    def to_second(forward, k, side):
        head, second, _, src, _, keep, _, i = way(forward)
        return remote(
            src.at[parts * side + k], keep.at[side, k], {"seq": 2 * second + core},
            ZP[i] + 4 * side + k,
        )

    def zeach(forward, k, act):
        head, second, late, src, dst, keep, _, _ = way(forward)

        @pl.when(z == head)
        def _():
            for side in range(2):
                act(to_second(forward, k, side))

        @pl.when(z == second)
        def _():
            for side in range(2):
                act(to_late(forward, src.at[parts * side + k], k, z, late_chip(forward, side)))

        @pl.when(late)
        def _():
            act(to_late(forward, src.at[parts * (1 - zq) + k], k, z, zo))

    def zsend(forward, k):
        zeach(forward, k, lambda copy: copy.start())

    def zpass(forward, k, side):
        head, _, _, _, _, keep, _, _ = way(forward)
        return to_late(forward, keep.at[side, k], k, head, late_chip(forward, side), True)

    def zrelay(forward, k):
        @pl.when(z == way(forward)[1])
        def _():
            for side in range(2):
                to_second(forward, k, side).wait_recv()
                zpass(forward, k, side).start()

    def zdone(forward, k):
        zeach(forward, k, lambda copy: copy.wait_send())

        @pl.when(z == way(forward)[1])
        def _():
            for side in range(2):
                zpass(forward, k, side).wait_send()

        @pl.when(way(forward)[2])
        def _():
            ret(forward, k).wait_send()

    def ret(forward, k):
        _, _, _, _, _, _, dst, i = way(forward)
        return remote(
            ms_ref.at[i, k, lax.rem(zo, 2)], dst.at[parts * zq + k], {"seq": 2 * zo + core}, ZQ[i] + k
        )

    def ret_wait(forward, k):
        _, _, late, _, _, _, dst, i = way(forward)

        @pl.when(late)
        def _():
            remote(
                ms_ref.at[i, k, 0], dst.at[parts * (1 - zq) + k], {"seq": 2 * zo + core}, ZQ[i] + k
            ).wait_recv()

    def several(lo, hi, together, one):
        def some(i, carry):
            for u in range(together):
                one(lo + i * together + u)
            return carry

        lax.fori_loop(0, (hi - lo) // together, some, 0)

    def build(lo, hi):
        def one(g, side, depth):
            row = hf_ref[side, pl.ds(g, 1), : depth * count]
            lines = jnp.broadcast_to(row, (count, depth * count))
            both = jnp.concatenate([jnp.zeros((count, count), F32), lines], axis=1)
            lined = pltpu.roll(both, 0, 1, stride=1, stride_axis=0).astype(BF16)
            for k in range(depth):
                at = (k + 1) * count
                to = (filt_ref, near_ref)[side]
                to[g, k * count : (k + 1) * count, :] = lined[:, at : at + count]

        several(lo, hi, 4, lambda g: one(g, 0, lags))
        several(lo, hi, 4, lambda g: one(g, 1, outs))

    def mix(forward, k, last_half):
        head, second, late, sent, src, keep, dst, way_at = way(forward)

        def fill(x2, slot):
            for blk in range(2):
                x = x2[blk * count : (blk + 1) * count]
                if forward:
                    at, x = blk, x.astype(F32)
                else:
                    at, x = 1 - blk, flipped(x, flip)
                xt_ref[:, 3 + slot + at] = x.T.reshape(groups, GROUP, count).astype(BF16)

        def run(filt, top, tall, depth):
            for g in range(groups):
                pieces = [
                    xt_ref[g, top - j : top - j + tall].reshape(tall * GROUP, count)
                    for j in range(depth)
                ]
                got = jnp.dot(
                    jnp.concatenate(pieces, axis=1),
                    filt[groups * k + g, : depth * count],
                    preferred_element_type=F32,
                )
                ot_ref[0:tall, g] = got.reshape(tall, GROUP, count)

        def turned(b, tall):
            y = ot_ref[b].reshape(bw, count).T.astype(BF16)
            if forward:
                return b, y
            return tall - 1 - b, flipped(y, flip).astype(BF16)

        if last_half:
            for d in range(1, chips):
                p = lax.rem(z + d, chips)
                to_late(forward, sent.at[0], k, p, z).wait_recv()
            for i in range(4):
                near = i >= 2
                r = i % 2 if forward else 1 - i % 2
                chip = 2 * zh + r if near else 2 * (1 - zh) + r
                if near:
                    own = zq == r
                    pl.when(own)(lambda i=i: fill(sent[parts * zq + k], 2 * i))
                    pl.when(jnp.logical_not(own))(lambda i=i, chip=chip: fill(src[chip, k], 2 * i))
                else:
                    fill(src[chip, k], 2 * i)
            run(filt_ref, 3 + outs, outs, lags)
            for b in range(outs):
                at, y = turned(b, outs)
                ms_ref[way_at, k, at // 2, (at % 2) * count : (at % 2 + 1) * count, :] = y
            ret(forward, k).start()
            dst[parts * zq + k] = ms_ref[way_at, k, zq]

        else:
            for i in range(2):
                side = zq if i == 0 else 1 - zq
                fill(sent[parts * side + k], 2)

                @pl.when(z == second)
                def _():
                    fill(keep[side, k], 0)

                @pl.when(z == head)
                def _():
                    xt_ref[:, 3:5] = jnp.zeros((groups, 2, GROUP, count), BF16)

                run((filt_ref, near_ref)[i], 5, 2, outs)
                for b in range(2):
                    at, y = turned(b, 2)
                    dst[parts * side + k, at * count : (at + 1) * count, :] = y

    def sums_done(k):
        cx(k, 1).wait_recv()
        cy(k, 2).wait_recv()
        a, b = k, parts + k
        total_ref[a] += rx_ref[k, 1].astype(F32) + ry_ref[k, 2].astype(F32)
        gm_ref[a] = (total_ref[a] * filtered_ref[0, a]).astype(BF16)
        cy(k, 1).wait_recv()
        cx(k, 2).wait_recv()
        total_ref[b] += ry_ref[k, 1].astype(F32) + rx_ref[k, 2].astype(F32)
        gm_ref[b] = (total_ref[b] * filtered_ref[0, b]).astype(BF16)
        zsend(False, k)

    def gat(k, j):
        s = k % 2
        return ga_ref.at[k // 2, j, :, s * bw : (s + 1) * bw]

    def ax(k, i):
        src, dst = ((4, 2), (5, 6), (3, 1))[i]
        return remote(gat(k, src), gat(k, dst), X, 168 + 3 * k + i)

    def ay(k, i):
        src, dst = ((5, 3), (4, 7), (2, 0))[i]
        return remote(gat(k, src), gat(k, dst), Y, 180 + 3 * k + i)

    def gate(k):
        ret_wait(True, k)
        for j, b in enumerate((k, parts + k)):
            s = k % 2
            ga_ref[k // 2, 4 + j, :, s * bw : (s + 1) * bw] = (
                filtered_ref[0, b] * mixed_ref[b].astype(F32)
            ).astype(BF16)
        for i in range(2):
            ax(k, i).start()
            ay(k, i).start()
        for b in (k, parts + k):
            gf_ref[0, b] = (total_ref[b] * mixed_ref[b].astype(F32)).astype(BF16)

    def relay(k):
        ax(k, 0).wait_recv()
        ay(k, 2).start()
        ay(k, 0).wait_recv()
        ax(k, 2).start()

    def gathered(k, i):
        ax(k, i).wait_recv()
        ay(k, i).wait_recv()

    wide = columns // 4

    def project(c, lo, hi, first=False, then=None):
        def some(i, carry):
            at = pl.ds(pl.multiple_of(i * wide, wide), wide)
            got = jnp.dot(
                jnp.concatenate([ga_ref[c, j] for j in range(lo, hi)], axis=1),
                w_ref[c, lo:hi, :, at].reshape((hi - lo) * wb, wide),
                preferred_element_type=F32,
            )
            acc_ref[:, at] = got if first else acc_ref[:, at] + got
            if then is not None:
                then(i, at)
            return carry

        lax.fori_loop(0, columns // wide, some, 0)

    def mo(i, at):
        return remote(mo_send.at[:, at], mo_recv.at[:, at], SIB, 192 + i)

    def mo_out(i, at):
        return pltpu.make_async_copy(mo_ref.at[:, at], out_hbm.at[:, at], out_sem.at[3 + i])

    def give(i, at):
        mo_send[:, at] = acc_ref[sibrows, at].astype(BF16)
        mo(i, at).start()

    def heads(m):
        return remote(
            gf_ref.at[m, :, 0:16], head_ref.at[m],
            {"seq": 2 * lax.rem(z + chips - 1, chips) + core}, 120 + m,
        )

    def heads_start(m):
        @pl.when(z > 0)
        def _():
            heads(m).start()

    def finish(m, ref):
        @pl.when(z < chips - 1)
        def _():
            heads(m).wait_recv()

        def one(b, carry):
            g = gf_ref[m, b].astype(F32)
            taps = taps_ref[b, 3 * m : 3 * m + 3]
            after = jnp.where(z < chips - 1, head_ref[m, b].astype(F32)[0:2], 0.0)
            fin_ref[m, :, cols(b)] = anticausal(g, after, taps).astype(BF16)
            return carry

        lax.fori_loop(0, nblk, one, 0)
        pltpu.make_async_copy(fin_ref.at[m, myrows], ref.at[:, mycols], out_sem.at[m]).start()
        remote(fin_ref.at[m, sibrows], ref.at[:, mycols], SIB, 123 + m).start()

    def grads(k):
        ret_wait(False, k)
        for b in (k, parts + k):
            gp = gp_ref[b].astype(F32)
            gf_ref[1, b] = (gp * filtered_ref[2, b]).astype(BF16)
            gf_ref[2, b] = (gp * filtered_ref[1, b]).astype(BF16)

    def multiply(k, carry):
        for b in (k, parts + k):
            prod_ref[b] = (filtering(1, b) * filtering(2, b)).astype(BF16)
        zsend(True, k)
        return carry

    def query(b, carry):
        filtering(0, b)
        return carry

    def arrived(m):
        ins[1 + m].wait()
        swaps[1 + m].wait_recv()
        rim_wait(m)

    def filters(lo, hi):
        if lo == 0:
            ins[4].wait()
            ins[5].wait()
            hf_ref[...] = h_ref[...].astype(F32)
        build(lo * groups, hi * groups)

    def next_sums(k):
        sums_joined(k)
        if k + 1 < parts:
            sums_send(k + 1, 0)
            sums_send(k + 1, 1)

    def early(act):
        pl.when(zh == 0)(act)

    def later(act):
        pl.when(zh == 1)(act)

    def mixed(forward, k):
        for last_half in (True, False):
            half_at = 1 if forward == last_half else 0
            pl.when(zh == half_at)(lambda last_half=last_half: mix(forward, k, last_half))

    def near_in(ks):
        for k in ks:
            gathered(k, 1)

    def far_in(ks):
        for k in ks:
            gathered(k, 2)

    ins[0].wait()
    swaps[0].wait_recv()
    sums(0, 0, 1)
    sums_send(0, 0)
    sums_send(1, 0)
    arrived(1)
    arrived(2)
    lax.fori_loop(0, parts, multiply, 0)
    sums(0, 1, 4)
    sums_send(0, 1)
    sums_joined(0)
    sums_send(1, 1)
    sums(1, 0, 4)
    zrelay(True, 0)
    arrived(0)
    lax.fori_loop(0, nblk, query, 0)
    sums_done(0)
    next_sums(1)
    zrelay(True, 1)
    zrelay(True, 2)
    filters(0, 2)
    zrelay(False, 0)
    sums_done(1)
    next_sums(2)
    mixed(True, 0)
    zrelay(True, 3)
    zrelay(False, 1)
    sums_done(2)
    mixed(False, 0)
    next_sums(3)
    gate(0)
    mixed(True, 1)
    filters(2, 4)
    zrelay(False, 2)
    sums_done(3)
    mixed(True, 2)
    gate(1)
    relay(0)
    mixed(False, 1)
    zrelay(False, 3)
    gate(2)
    relay(1)
    mixed(False, 2)
    mixed(True, 3)
    later(lambda: mix(False, 3, False))
    relay(2)
    gate(3)
    early(lambda: mix(False, 3, True))
    heads_start(0)
    near_in((0, 1))
    far_in((0, 1))
    project(0, 0, 8, True)
    relay(3)
    for k in range(parts):
        grads(k)
    heads_start(1)
    heads_start(2)
    finish(0, gq_hbm)
    near_in((2, 3))
    project(1, 2, 8)
    finish(1, gk_hbm)
    finish(2, gv_hbm)

    for copy in swaps:
        copy.wait_send()

    @pl.when(sends_rim)
    def _():
        for m in range(3):
            for to in range(2):
                rim(m, to).wait_send()

    for k in range(parts):
        for i in range(3):
            for make in (cx, cy):
                make(k, i).wait_send()
        for forward in (True, False):
            zdone(forward, k)

    for k in range(2, 4):
        gathered(k, 2)
    project(1, 0, 2, then=give)
    for i in range(4):
        at = pl.ds(i * wide, wide)
        mo(i, at).wait_recv()
        mo_ref[:, at] = (acc_ref[myrows, at] + mo_recv[:, at].astype(F32)).astype(BF16)
        mo_out(i, at).start()

    for k in range(parts):
        for i in range(3):
            for make in (ax, ay):
                make(k, i).wait_send()

    @pl.when(z > 0)
    def _():
        for m in range(3):
            heads(m).wait_send()

    for m, ref in enumerate((gq_hbm, gk_hbm, gv_hbm)):
        pltpu.make_async_copy(fin_ref.at[m, myrows], ref.at[:, mycols], out_sem.at[m]).wait()
        remote(fin_ref.at[m, sibrows], ref.at[:, mycols], SIB, 123 + m).wait_send()
        remote(fin_ref.at[m, sibrows], ref.at[:, sibcols], SIB, 123 + m).wait_recv()
    for i in range(4):
        at = pl.ds(i * wide, wide)
        mo(i, at).wait_send()
        mo_out(i, at).wait()


def copy_kernel(*refs):
    srcs, dsts, held, sem_in, sem_out = refs[:4], refs[4:8], *refs[8:]
    into = [pltpu.make_async_copy(src, held.at[i], sem_in.at[i]) for i, src in enumerate(srcs)]
    out = [pltpu.make_async_copy(held.at[i], dst, sem_out.at[i]) for i, dst in enumerate(dsts)]
    for copy in into:
        copy.start()
    for i in range(4):
        into[i].wait()
        out[i].start()
    for copy in out:
        copy.wait()


def paired(query_proj, key_proj, value_proj, short_filter, long_filter, out_weight, grad_out):
    count, width = query_proj.shape
    length = long_filter.shape[1]
    columns = out_weight.shape[1]
    half = width // 2
    span = 2 * count
    bw = half // 8
    groups = bw // GROUP
    lags = length // count

    vmem = pl.BlockSpec(memory_space=pltpu.VMEM)
    hbm = pl.BlockSpec(memory_space=pl.ANY)
    flat = jax.ShapeDtypeStruct((count, width), BF16)
    block = (span, bw)
    results = pl.pallas_call(
        pair_kernel,
        in_specs=[hbm] * 3 + [vmem] + [hbm] * 3,
        out_specs=[hbm] * 4,
        out_shape=[flat] * 4,
        scratch_shapes=[
            pltpu.VMEM((2, 8, 2 * bw, columns), BF16),
            pltpu.VMEM((span, columns), BF16),
            pltpu.VMEM((3, 16 + span, half), BF16),
            pltpu.VMEM((8, 16, bw), F32),
            pltpu.VMEM((2, 4 * groups, length), BF16),
            pltpu.VMEM((4 * groups, length, count), BF16),
            pltpu.VMEM((4 * groups, length // 2, count), BF16),
            pltpu.VMEM((2, 4 * groups, length), F32),
            pltpu.VMEM((3, 8) + block, F32),
            pltpu.VMEM((8,) + block, BF16),
            pltpu.VMEM((8,) + block, BF16),
            pltpu.VMEM((4, 4) + block, BF16),
            pltpu.VMEM((4, 4) + block, BF16),
            pltpu.VMEM((2, 4) + block, BF16),
            pltpu.VMEM((2, 4) + block, BF16),
            pltpu.VMEM((groups, 3 + lags, GROUP, count), BF16),
            pltpu.VMEM((lags // 2, groups, GROUP, count), F32),
            pltpu.VMEM((2, 4, 2) + block, BF16),
            pltpu.VMEM((8,) + block, BF16),
            pltpu.VMEM((8,) + block, BF16),
            pltpu.VMEM((8,) + block, F32),
            pltpu.VMEM((2, span, 4 * bw), F32),
            pltpu.VMEM((4, 3) + block, BF16),
            pltpu.VMEM((4, 3) + block, BF16),
            pltpu.VMEM((4, 3) + block, BF16),
            pltpu.VMEM((4, 3) + block, BF16),
            pltpu.VMEM((2, 8, span, 2 * bw), BF16),
            pltpu.VMEM((span, columns), F32),
            pltpu.VMEM((3, 8) + block, BF16),
            pltpu.VMEM((3, 8, 16, bw), BF16),
            pltpu.VMEM((3, span, half), BF16),
            pltpu.VMEM((count, columns), BF16),
            pltpu.VMEM((count, columns), BF16),
            pltpu.VMEM((count, columns), BF16),
            pltpu.SemaphoreType.DMA((2, 8)),
            pltpu.SemaphoreType.DMA((6,)),
            pltpu.SemaphoreType.DMA((196,)),
            pltpu.SemaphoreType.DMA((196,)),
            pltpu.SemaphoreType.DMA((7,)),
        ],
        compiler_params=pltpu.CompilerParams(
            collective_id=0, has_side_effects=True, vmem_limit_bytes=62 * 1024 * 1024
        ),
        name="step",
    )(
        query_proj, key_proj, value_proj, short_filter.transpose(0, 2, 1),
        long_filter, out_weight, grad_out,
    )
    return pl.pallas_call(
        copy_kernel,
        in_specs=[hbm] * 4,
        out_specs=[hbm] * 4,
        out_shape=[flat] * 4,
        scratch_shapes=[
            pltpu.VMEM((4, count, width), BF16),
            pltpu.SemaphoreType.DMA((4,)),
            pltpu.SemaphoreType.DMA((4,)),
        ],
        compiler_params=pltpu.CompilerParams(vmem_limit_bytes=62 * 1024 * 1024),
        name="last",
    )(*results)


def either(query_proj, key_proj, value_proj, short_filter, long_filter, out_weight, grad_out):
    args = (query_proj, key_proj, value_proj, short_filter, long_filter, out_weight, grad_out)
    count, width = query_proj.shape
    fits = (
        lax.axis_size("seq") == 8
        and lax.axis_size("chan") == 4
        and count % 128 == 0
        and width % 2048 == 0
        and long_filter.shape[1] == 8 * count
    )
    return paired(*args) if fits else local(*args)


def solution(mesh):
    return jax.shard_map(
        either,
        mesh=mesh,
        in_specs=(
            P("seq", "chan"),
            P("seq", "chan"),
            P("seq", "chan"),
            P(None, "chan", None),
            P("chan", None),
            P(None, "chan"),
            P("seq", "chan"),
        ),
        out_specs=(P("seq", "chan"), P("seq", "chan"), P("seq", "chan"), P("seq", "chan")),
        check_vma=False,
    )
```
